32 devices in a mesh: mp: 4 (over y, core), tile: 8 (over z, x).
Axes of the slice: x: 2, y: 2, z: 4, core: 2. Of those that a mesh axis runs over, the one named last changes fastest.
Arguments:
- state: float32 [4, 128, 16384], P('mp', None, 'tile'), may hold values from -6 to 6
- diffusivity: float32 [4, 6, 16384], P('mp', None, 'tile'), may hold values from 0.02 to 0.16
- neighbours: int32 [4, 6, 16384], P('mp', None, 'tile'), may hold values from 0 to 2111, as said below
- vertical_mix: float32 [4, 128, 128], P('mp'), may hold values from -0.5 to 0.5
- transfer_rates: float32 [4, 8, 16384], P('mp', None, 'tile'), may hold values from 0.5 to 2
- bulk_map: float32 [8, 128], replicated, may hold values from -0.5 to 0.5
- absorb_map: float32 [128, 8], replicated, may hold values from -2 to 2
- block_dest: int32 [8, 3, 32], P('tile'), may hold values from 0 to 127, as said below
- block_rows: int32 [8, 3, 32], P('tile'), may hold values from 32 to 128
- block_weights: bfloat16 [8, 3, 32, 128, 128], P('tile'), may hold values from -0.5 to 0.5
Outputs:
- new_state: float32 [4, 128, 16384], P('mp', None, 'tile')
- ocean_flux: float32 [8, 16384], P(None, 'tile')
The draws below stay inside these ranges and needn't reach their ends.
Inputs may be any that keep to these rules, and one draw needn't show every extreme that they name: `neighbours`: each neighbour index lies within 32 of the column's own index plus 32, never equal to it. `block_dest`: ocean row block numbers; the ocean tile of block number r is floor(r / 16). The blocks of one atmosphere tile and strip name at most 4 blocks of any one ocean tile, and exactly 4 of one ocean tile that is the same for all tiles of the strip.
All inputs are finite; a program needn't handle non-finite values.
Results may differ from the reference program's by a relative error of at most 0.0033.
Values may be sent and summed in bfloat16 or wider, within the bound.
No kernel may reach another device: no remote copies, remote signals or barrier semaphores. Data moves between devices by JAX's collectives and lax.ppermute only.
A program may use at most 64 MiB of HBM per device.

```python
import math
import jax
import jax.numpy as jnp
from jax import lax

LEVELS = 128
CHIP_CELL_COUNT = 2048
NEIGH_COUNT = 6
HALO_WIDTH = 32
SUBSTEPS = 4
FIELDS = 8
WEIGHT_TILE_EDGE = 128
GRID_PATCH_MEETS = 2
CHIP_GROUP_COUNT = 16
REMAP_BLOCKS = 32
SLOT_CAP = 4
ZONAL_RIBBONS = 3
BAND_COLUMNS = 16384
N_MP = 4
N_TILE = 8


def draw_neighbours(key, part):
    key_reach, key_side = jax.random.split(jax.random.fold_in(key, 3))
    shape = (N_MP, NEIGH_COUNT, BAND_COLUMNS)
    reach = jax.random.randint(key_reach, shape, 1, HALO_WIDTH + 1)
    side = jax.random.randint(key_side, shape, 0, 2) * 2 - 1
    offset = reach * side
    position = (jnp.arange(BAND_COLUMNS, dtype=jnp.int32) % CHIP_CELL_COUNT)[None, None, :]
    leading = (jnp.arange(NEIGH_COUNT, dtype=jnp.int32) == 0)[None, :, None]
    offset = jnp.where(leading & (position == 0), -HALO_WIDTH, offset)
    offset = jnp.where(leading & (position == CHIP_CELL_COUNT - 1), HALO_WIDTH, offset)
    return (position + HALO_WIDTH + offset).astype(jnp.int32)


def draw_block_dest(key, part):
    key_crowd, key_order, key_local = jax.random.split(jax.random.fold_in(key, 5), 3)
    crowded = jax.random.randint(key_crowd, (ZONAL_RIBBONS,), 0, N_TILE)
    scores = jax.random.randint(key_order, (N_TILE, ZONAL_RIBBONS, N_TILE - 1), 0, 4096) * (N_TILE - 1)
    scores = scores + jnp.arange(N_TILE - 1, dtype=jnp.int32)[None, None, :]
    order = jnp.argsort(scores, axis=-1).astype(jnp.int32)
    block_index = jnp.arange(REMAP_BLOCKS, dtype=jnp.int32)
    other_rank = jnp.maximum(block_index - SLOT_CAP, 0) % (N_TILE - 1)
    picked = jnp.take_along_axis(order, jnp.broadcast_to(other_rank[None, None, :], (N_TILE, ZONAL_RIBBONS, REMAP_BLOCKS)), axis=2)
    other_tile = (crowded[None, :, None] + 1 + picked) % N_TILE
    tile_index = jnp.where(block_index[None, None, :] < SLOT_CAP, crowded[None, :, None], other_tile)
    local_block = jax.random.randint(key_local, (N_TILE, ZONAL_RIBBONS, REMAP_BLOCKS), 0, CHIP_GROUP_COUNT)
    return (tile_index * CHIP_GROUP_COUNT + local_block).astype(jnp.int32)


def plant(entries, stream_key, low, largest):
    longest = entries.shape.index(max(entries.shape))
    spots = []
    for shift in (0, 1):
        where = [jax.random.randint(jax.random.fold_in(stream_key, axis), (), 0, length) for axis, length in enumerate(entries.shape)]
        where[longest] = (where[longest] + shift) % entries.shape[longest]
        spots.append(tuple(where))
    return entries.at[spots[0]].set(low).at[spots[1]].set(largest)


def levels(stream_key, extent, cuts, least, largest):
    level, own = 1.0, jax.random.fold_in(stream_key, 6)
    for axis_at, blocks in cuts:
        draws = jnp.exp(jax.random.uniform(jax.random.fold_in(own, axis_at), (blocks,), jnp.float32, least / len(cuts), largest / len(cuts)))
        level = level * jnp.repeat(draws, extent[axis_at] // blocks).reshape([-1 if axis == axis_at else 1 for axis in range(len(extent))])
    return level


def bell_draw(key, extent, scale, bound, cuts=(), held_as=jnp.bfloat16):
    result = jax.random.normal(key, extent, jnp.float32) * scale
    if len(cuts) > 0:
        result = levels(key, extent, cuts, -0.22, 0.18) * result
    return jnp.clip(result, min=-bound, max=bound).astype(held_as)


def setup_inputs(seed: int = 0) -> dict:
    key_list = jax.random.split(jax.random.key(seed), 11)
    state = bell_draw(key_list[0], (N_MP, LEVELS, BAND_COLUMNS), 1.0, 6.0, ((0, 4), (2, 8)), jnp.float32)
    diffusivity = jnp.clip(0.02 + 0.14 * jax.random.uniform(key_list[1], (N_MP, NEIGH_COUNT, BAND_COLUMNS), jnp.float32) ** levels(key_list[1], (N_MP, NEIGH_COUNT, BAND_COLUMNS), ((0, 4), (2, 8)), -0.2, 0.2), 0.02, 0.16)
    neighbours = draw_neighbours(jax.random.fold_in(key_list[10], 71), 0)
    vertical_mix = bell_draw(key_list[3], (N_MP, LEVELS, LEVELS), LEVELS ** -0.5, 0.5, ((0, 4),), jnp.float32)
    transfer_rates = jnp.clip(jnp.exp(math.log(2.0) - 1.3862944 * jax.random.uniform(key_list[4], (N_MP, FIELDS, BAND_COLUMNS), jnp.float32) ** levels(key_list[4], (N_MP, FIELDS, BAND_COLUMNS), ((0, 4), (2, 8)), -0.2, 0.2)), 0.5, 2.0)
    bulk_map = bell_draw(key_list[5], (FIELDS, LEVELS), LEVELS ** -0.5, 0.5, (), jnp.float32)
    absorb_map = bell_draw(key_list[6], (LEVELS, FIELDS), FIELDS ** -0.5, 2.0, (), jnp.float32)
    block_dest = draw_block_dest(jax.random.fold_in(key_list[10], 71), 0)
    block_rows = plant(jax.random.randint(key_list[8], (N_TILE, ZONAL_RIBBONS, REMAP_BLOCKS), WEIGHT_TILE_EDGE // 4, WEIGHT_TILE_EDGE + 1), jax.random.fold_in(key_list[8], 1), WEIGHT_TILE_EDGE // 4, WEIGHT_TILE_EDGE).astype(jnp.int32)
    block_weights = bell_draw(key_list[9], (N_TILE, ZONAL_RIBBONS, REMAP_BLOCKS, WEIGHT_TILE_EDGE, WEIGHT_TILE_EDGE), WEIGHT_TILE_EDGE ** -0.5, 0.5, ((0, 8),))
    return dict(state=state, diffusivity=diffusivity, neighbours=neighbours, vertical_mix=vertical_mix, transfer_rates=transfer_rates, bulk_map=bulk_map, absorb_map=absorb_map, block_dest=block_dest, block_rows=block_rows, block_weights=block_weights)


def reference(state, diffusivity, neighbours, vertical_mix, transfer_rates, bulk_map, absorb_map, block_dest, block_rows, block_weights):
    peak_magnitude = lax.Precision.HIGHEST
    boundary_entries = state[N_MP - 1, 0].astype(jnp.bfloat16).reshape(N_TILE * CHIP_GROUP_COUNT, WEIGHT_TILE_EDGE)
    atmos = state[:ZONAL_RIBBONS].reshape(ZONAL_RIBBONS, LEVELS, N_TILE, CHIP_CELL_COUNT).transpose(2, 0, 1, 3)
    coefs = transfer_rates[:ZONAL_RIBBONS].reshape(ZONAL_RIBBONS, FIELDS, N_TILE, CHIP_CELL_COUNT).transpose(2, 0, 1, 3)
    ocean_index = jnp.arange(WEIGHT_TILE_EDGE, dtype=jnp.int32)

    def per_tile(pieces):
        weights, destination_cells, live_rows, field, transfer_scaling = pieces
        filtered_entries = jnp.where(ocean_index[None, None, None, :] < live_rows[:, :, None, None], weights, jnp.zeros_like(weights))
        filtered_widened_entries = filtered_entries.astype(jnp.float32)
        ocean_warmth_pieces = boundary_entries[destination_cells].astype(jnp.float32)
        ocean_warmth_products = jnp.einsum('deqt,det->deq', filtered_widened_entries, ocean_warmth_pieces, precision=peak_magnitude)
        ocean_warmth_on_air_grid = ocean_warmth_products.reshape(ZONAL_RIBBONS, CHIP_GROUP_COUNT, GRID_PATCH_MEETS, WEIGHT_TILE_EDGE).sum(axis=2).reshape(ZONAL_RIBBONS, CHIP_CELL_COUNT)
        mapped_transport = jnp.einsum('fl,slc->sfc', bulk_map, field, precision=peak_magnitude)
        boundary_transport = (mapped_transport - transfer_scaling * ocean_warmth_on_air_grid[:, None, :]).astype(jnp.bfloat16)
        flux_blocks = boundary_transport.reshape(ZONAL_RIBBONS, FIELDS, CHIP_GROUP_COUNT, WEIGHT_TILE_EDGE).transpose(0, 2, 1, 3)
        flux_blocks = jnp.repeat(flux_blocks, GRID_PATCH_MEETS, axis=1).astype(jnp.float32)
        contrib = jnp.einsum('snfa,snao->snfo', flux_blocks, filtered_widened_entries, precision=peak_magnitude)
        return boundary_transport, contrib

    fluxes, contribs = lax.map(per_tile, (block_weights, block_dest, block_rows, atmos, coefs))
    summed = jax.ops.segment_sum(contribs.reshape(-1, FIELDS, WEIGHT_TILE_EDGE), block_dest.reshape(-1), num_segments=N_TILE * CHIP_GROUP_COUNT)
    ocean_flux = summed.transpose(1, 0, 2).reshape(FIELDS, BAND_COLUMNS)

    flux_all = fluxes.transpose(1, 2, 0, 3).reshape(ZONAL_RIBBONS, FIELDS, BAND_COLUMNS)
    forcing = jnp.einsum('lf,sfc->slc', absorb_map, flux_all.astype(jnp.float32), precision=peak_magnitude)
    field = jnp.concatenate([state[:ZONAL_RIBBONS] - forcing, state[ZONAL_RIBBONS:]], axis=0)

    base = (jnp.arange(BAND_COLUMNS, dtype=jnp.int32) // CHIP_CELL_COUNT) * CHIP_CELL_COUNT
    lookup = (base[None, None, :] + neighbours - HALO_WIDTH) % BAND_COLUMNS
    take_rows = jax.vmap(lambda rows, index: rows[:, index])
    for substep in range(SUBSTEPS):
        spread = jnp.zeros_like(field)
        for neighbour in range(NEIGH_COUNT):
            beside = take_rows(field, lookup[:, neighbour])
            spread = spread + diffusivity[:, neighbour][:, None, :] * (beside - field)
        field = field + spread
        field = field + 0.25 * jnp.einsum('mij,mjc->mic', vertical_mix, field, precision=peak_magnitude)
    ocean_part = field[N_MP - 1] + jnp.dot(absorb_map, transfer_rates[N_MP - 1] * ocean_flux, precision=peak_magnitude)
    field = jnp.concatenate([field[:ZONAL_RIBBONS], ocean_part[None]], axis=0)
    return field, ocean_flux
```

```python
import jax
import jax.numpy as jnp
from jax import lax
from jax.experimental import pallas as pl
from jax.experimental.pallas import tpu as pltpu
from jax.sharding import PartitionSpec as P

HALO_WIDTH = 32
SUBSTEPS = 4
FIELDS = 8
EDGE = 128
LEVELS = 128
NEIGH = 6
SLOTS = 4
PAYLOAD = 48
F32 = jnp.float32
BF16 = jnp.bfloat16
HIGHEST = lax.Precision.HIGHEST


def lanes(shape):
    return lax.broadcasted_iota(jnp.int32, shape, len(shape) - 1)


def prep_kernel(top, first, last, nbr, dif, sst, to_left, to_right):
    columns = nbr.shape[2]
    blocks = columns // EDGE
    for b in range(blocks):
        row = top[0, 0:1, b * EDGE : (b + 1) * EDGE]
        sst[b : b + 1, :] = row.astype(BF16).astype(F32)
    for out, edge, b in ((to_left, first, 0), (to_right, last, blocks - 1)):
        at = slice(b * EDGE, (b + 1) * EDGE)
        out[0:LEVELS, :] = edge[0]
        out[LEVELS : LEVELS + NEIGH, :] = (nbr[0, :, at] - (HALO_WIDTH + b * EDGE)).astype(F32)
        out[LEVELS + 8 : LEVELS + 8 + NEIGH, :] = dif[0, :, at]
        out[LEVELS + 6 : LEVELS + 8, :] = jnp.zeros((2, EDGE), F32)
        out[LEVELS + 14 : LEVELS + 16, :] = jnp.zeros((2, EDGE), F32)


def prep(state, neighbours, diffusivity):
    columns = state.shape[2]
    blocks = columns // EDGE
    whole = pl.BlockSpec((1, NEIGH, columns), lambda i: (0, 0, 0))
    halo = jax.ShapeDtypeStruct((LEVELS + 16, EDGE), F32)
    halo_spec = pl.BlockSpec((LEVELS + 16, EDGE), lambda i: (0, 0))
    return pl.pallas_call(
        prep_kernel,
        grid=(1,),
        in_specs=[
            pl.BlockSpec((1, 8, columns), lambda i: (0, 0, 0)),
            pl.BlockSpec((1, LEVELS, EDGE), lambda i: (0, 0, 0)),
            pl.BlockSpec((1, LEVELS, EDGE), lambda i: (0, 0, blocks - 1)),
            whole,
            whole,
        ],
        out_specs=[pl.BlockSpec((blocks, EDGE), lambda i: (0, 0)), halo_spec, halo_spec],
        out_shape=[jax.ShapeDtypeStruct((blocks, EDGE), F32), halo, halo],
        name="prep",
    )(state, state, state, neighbours, diffusivity)


def take(x, index):
    return jnp.take_along_axis(x, index, axis=1, mode="promise_in_bounds")


def stencil(xp, xc, xn, low, place, inside, weight, keep):
    beyond = jnp.where(low, xn, xp)
    total = keep * xc
    for k in range(NEIGH):
        value = jnp.where(inside[k], take(xc, place[k]), take(beyond, place[k]))
        total = total + weight[k] * value
    return total


def block_terms(index, weight, c):
    shape = (8, EDGE)
    place, inside, rate = [], [], []
    for k in range(NEIGH):
        j = jnp.broadcast_to(index[c, k : k + 1, :], shape)
        inside.append((j >= 0) & (j < EDGE))
        place.append(j & (EDGE - 1))
        rate.append(jnp.broadcast_to(weight[c, k : k + 1, :], shape))
    keep = jnp.broadcast_to(weight[c, NEIGH : NEIGH + 1, :], shape)
    return place, inside, rate, keep


def build_band(index, weight, band, c):
    group = 8
    targets = []
    for k in range(NEIGH):
        j = index[c, k : k + 1, :]
        j = jnp.where((j >= 0) & (j < EDGE), j, EDGE + (j & (EDGE - 1)))
        targets.append((jnp.broadcast_to(j, (group, EDGE)), jnp.broadcast_to(weight[c, k : k + 1, :], (group, EDGE))))
    row = lax.broadcasted_iota(jnp.int32, (group, EDGE), 0)
    for start in range(0, 2 * EDGE, 16):
        if EDGE + HALO_WIDTH <= start < 2 * EDGE - HALO_WIDTH:
            high = jnp.zeros((16, EDGE), BF16)
            low = high
        else:
            parts = []
            for at in (start, start + group):
                total = jnp.zeros((group, EDGE), F32)
                for j, d in targets:
                    total = total + jnp.where(row == j - at, d, 0.0)
                parts.append(total)
            exact = jnp.concatenate(parts, axis=0)
            high = exact.astype(BF16)
            low = (exact - high.astype(F32)).astype(BF16)
        band[c, start : start + 16, 0:EDGE] = high
        band[c, start : start + 16, EDGE : 2 * EDGE] = low


def split(x):
    high = x.astype(BF16)
    return high, (x - high.astype(F32)).astype(BF16)


def state_kernel(meta, state, left, right, nbr, dif, vmix, bulk, absorb, mixed, mapped, spread, index, weight, e, f0, f1, band):
    blocks = nbr.shape[2] // EDGE
    outer = blocks + 2
    zeros = jnp.zeros((2, EDGE), jnp.int32)
    for c in range(outer):
        if c == 0 or c == outer - 1:
            halo = left if c == 0 else right
            x = halo[0:LEVELS, :]
            j = halo[LEVELS : LEVELS + NEIGH, :].astype(jnp.int32)
            d = halo[LEVELS + 8 : LEVELS + 8 + NEIGH, :]
        else:
            at = slice((c - 1) * EDGE, c * EDGE)
            x = state[0, :, at]
            j = nbr[0, :, at] - (HALO_WIDTH + (c - 1) * EDGE)
            d = dif[0, :, at]
            mapped[:, at] = jnp.dot(bulk[...], x, precision=HIGHEST, preferred_element_type=F32)
        index[c, 0:NEIGH, :] = j
        index[c, NEIGH:8, :] = zeros
        weight[c, 0:NEIGH, :] = d
        weight[c, NEIGH:8, :] = jnp.broadcast_to(1.0 - jnp.sum(d, axis=0, keepdims=True), (2, EDGE))
        e[c] = x
        f0[c, 0:LEVELS, :], f0[c, LEVELS : 2 * LEVELS, :] = split(x)

    @pl.loop(0, outer)
    def _(c):
        build_band(index, weight, band, c)

    low = lanes((2 * LEVELS, EDGE)) < EDGE // 2
    for step in range(SUBSTEPS):
        src, dst = (f0, f1) if step % 2 == 0 else (f1, f0)
        first, last = (0, outer) if step < SUBSTEPS - 1 else (1, outer - 1)

        @pl.loop(first, last)
        def _(c):
            before = jnp.maximum(c - 1, 0)
            after = jnp.minimum(c + 1, outer - 1)
            near = jnp.concatenate([src[c], jnp.where(low, src[after], src[before])], axis=1)
            product = jnp.dot(near, band[c], preferred_element_type=F32)
            x = weight[c, NEIGH : NEIGH + 1, :] * e[c] + (
                product[0:LEVELS, 0:EDGE] + (product[0:LEVELS, EDGE:] + product[LEVELS:, 0:EDGE])
            )
            e[c] = x
            if step < SUBSTEPS - 1:
                dst[c, 0:LEVELS, :], dst[c, LEVELS : 2 * LEVELS, :] = split(x)

    eye = (lax.broadcasted_iota(jnp.int32, (LEVELS, LEVELS), 0) == lanes((LEVELS, LEVELS))).astype(F32)
    a = eye + 0.25 * vmix[0]
    power = a
    for _ in range(SUBSTEPS - 1):
        power = jnp.dot(power, a, precision=HIGHEST, preferred_element_type=F32)
    for c in range(blocks):
        mixed[:, c * EDGE : (c + 1) * EDGE] = jnp.dot(
            power, e[c + 1], precision=HIGHEST, preferred_element_type=F32
        )
    mapped_absorb = jnp.dot(power, absorb[...], precision=HIGHEST, preferred_element_type=F32)
    spread[...] = jnp.where(meta[0] == meta[2], absorb[...], -mapped_absorb)


def vmem():
    return pl.BlockSpec(memory_space=pltpu.VMEM)


def smem():
    return pl.BlockSpec(memory_space=pltpu.SMEM)


def mix_state(meta, state, left, right, neighbours, diffusivity, vertical_mix, bulk_map, absorb_map):
    columns = state.shape[2]
    outer = columns // EDGE + 2
    return pl.pallas_call(
        state_kernel,
        in_specs=[smem()] + [vmem()] * 8,
        out_specs=[vmem()] * 5,
        out_shape=[
            jax.ShapeDtypeStruct((LEVELS, columns), F32),
            jax.ShapeDtypeStruct((FIELDS, columns), F32),
            jax.ShapeDtypeStruct((LEVELS, FIELDS), F32),
            jax.ShapeDtypeStruct((outer, 8, EDGE), jnp.int32),
            jax.ShapeDtypeStruct((outer, 8, EDGE), F32),
        ],
        scratch_shapes=[
            pltpu.VMEM((outer, LEVELS, EDGE), F32),
            pltpu.VMEM((outer, 2 * LEVELS, EDGE), BF16),
            pltpu.VMEM((outer, 2 * LEVELS, EDGE), BF16),
            pltpu.VMEM((outer, 2 * EDGE, 2 * EDGE), BF16),
        ],
        compiler_params=pltpu.CompilerParams(vmem_limit_bytes=32 * 2**20),
        name="mix_state",
    )(meta, state, left, right, neighbours, diffusivity, vertical_mix, bulk_map, absorb_map)


def flux_kernel(meta, dest, live, sst, weights, mapped, rates, message, flux, terms, codes, count):
    blocks = mapped.shape[1] // EDGE
    tiles = terms.shape[0] // SLOTS
    groups = message.shape[0] // tiles
    my_tile, strip = meta[1], meta[3]
    shape = (FIELDS, EDGE)
    lane = lanes(shape)
    for t in range(tiles):
        count[t] = 0
    codes[...] = jnp.zeros_like(codes)
    terms[...] = jnp.zeros_like(terms)
    first_lane = (my_tile % 4) * (SLOTS * FIELDS)
    edges = []
    for g in range(blocks):
        at = slice(g * EDGE, (g + 1) * EDGE)
        warmth = jnp.zeros(shape, F32)
        held = []
        for h in range(2):
            b = 2 * g + h
            where = dest[0, strip, b]
            owner, local = where // blocks, where % blocks
            slot = count[owner]
            count[owner] = slot + 1
            start = first_lane + slot * FIELDS
            mine = (lane >= start) & (lane < start + FIELDS)
            codes[owner] = codes[owner] + jnp.where(mine, local * FIELDS + 1 + lane - start, 0)
            alive = lane < live[0, strip, b]
            row = sst[pl.ds((owner ^ my_tile) * blocks + local, 1), :]
            row = jnp.where(alive, jnp.broadcast_to(row, shape), 0.0).astype(BF16)
            warmth = warmth + lax.dot_general(
                row, weights[0, 0, b], (((1,), (1,)), ((), ())), preferred_element_type=F32
            )
            held.append((b, owner * SLOTS + slot, alive))
        here = (mapped[:, at] - rates[0, :, at] * warmth).astype(BF16)
        flux[:, at] = here.astype(F32)
        if g in (0, blocks - 1):
            edges.append(here.astype(F32))
        for b, spot, alive in held:
            part = jnp.dot(here, weights[0, 0, b], preferred_element_type=F32)
            terms[spot] = jnp.where(alive, part, 0.0)
    for t in range(tiles):
        to_right = lax.rem(my_tile + 1, tiles) == t
        edge = jnp.where(to_right, edges[1], edges[0])
        body = terms[t * SLOTS : (t + 1) * SLOTS].reshape(SLOTS * FIELDS, EDGE).astype(BF16)
        rest = jnp.concatenate([edge, codes[t].astype(F32)], axis=0).astype(BF16)
        for m in range(groups):
            message[m * tiles + t, 0 : SLOTS * FIELDS, :] = body
            message[m * tiles + t, SLOTS * FIELDS : PAYLOAD, :] = rest


def make_flux(meta, groups, tiles, dest, live, sst, weights, mapped, rates):
    columns = mapped.shape[1]
    blocks = weights.shape[2]
    whole = lambda *shape: pl.BlockSpec(shape, lambda i, m: (0,) * len(shape))
    return pl.pallas_call(
        flux_kernel,
        grid_spec=pltpu.PrefetchScalarGridSpec(
            num_scalar_prefetch=1,
            grid=(1,),
            in_specs=[
                smem(),
                smem(),
                whole(*sst.shape),
                pl.BlockSpec((1, 1, blocks, EDGE, EDGE), lambda i, m: (0, m[3], 0, 0, 0)),
                whole(FIELDS, columns),
                whole(1, FIELDS, columns),
            ],
            out_specs=[whole(groups * tiles, PAYLOAD, EDGE), whole(FIELDS, columns)],
            scratch_shapes=[
                pltpu.VMEM((tiles * SLOTS, FIELDS, EDGE), F32),
                pltpu.VMEM((tiles, 8, EDGE), jnp.int32),
                pltpu.SMEM((tiles,), jnp.int32),
            ],
        ),
        out_shape=[
            jax.ShapeDtypeStruct((groups * tiles, PAYLOAD, EDGE), BF16),
            jax.ShapeDtypeStruct((FIELDS, columns), F32),
        ],
        compiler_params=pltpu.CompilerParams(vmem_limit_bytes=32 * 2**20),
        name="make_flux",
    )(meta, dest, live, sst, weights, mapped, rates)


def final_kernel(meta, got, flux, mixed, spread, rates, index, weight, out, ocean, x0, x1, drive):
    columns = flux.shape[1]
    blocks = columns // EDGE
    outer = blocks + 2
    peers = got.shape[0]
    groups = 4
    tiles = peers // groups
    my_group, my_tile = meta[0], meta[1]
    is_ocean = my_group == meta[2]
    body = SLOTS * FIELDS
    row = lax.broadcasted_iota(jnp.int32, (EDGE, EDGE), 0)
    total = jnp.zeros((EDGE, EDGE), F32)
    for q in range(0, (groups - 1) * tiles, 4):
        codes = got[q, body:PAYLOAD, :].astype(F32)
        data = [got[q, 0:body, :]]
        for p in range(q + 1, q + 4):
            codes = codes + got[p, body:PAYLOAD, :].astype(F32)
            data.append(got[p, 0:body, :])
        place = jnp.broadcast_to(codes[8:9, :], (EDGE, EDGE))
        chosen = ((row + 1).astype(F32) == place).astype(BF16)
        total = total + jnp.dot(chosen, jnp.concatenate(data, axis=0), preferred_element_type=F32)
    for b in range(blocks):
        ocean[:, b * EDGE : (b + 1) * EDGE] = total[b * FIELDS : (b + 1) * FIELDS, :]

    @pl.when(is_ocean)
    def _():
        for b in range(blocks):
            at = slice(b * EDGE, (b + 1) * EDGE)
            drive[:, at] = rates[0, :, at] * total[b * FIELDS : (b + 1) * FIELDS, :]

    @pl.when(jnp.logical_not(is_ocean))
    def _():
        before = my_group * tiles + lax.rem(my_tile + tiles - 1, tiles)
        after = my_group * tiles + lax.rem(my_tile + 1, tiles)
        x0[0] = got[before, body:PAYLOAD, :].astype(F32)[0:FIELDS, :]
        x0[outer - 1] = got[after, body:PAYLOAD, :].astype(F32)[0:FIELDS, :]
        for b in range(blocks):
            x0[b + 1] = flux[:, b * EDGE : (b + 1) * EDGE]
        low = lanes((8, EDGE)) < EDGE // 2
        for step in range(SUBSTEPS):
            src, dst = (x0, x1) if step % 2 == 0 else (x1, x0)
            first, last = (0, outer) if step < SUBSTEPS - 1 else (1, outer - 1)
            for c in range(first, last):
                place, inside, rate, keep = block_terms(index, weight, c)
                dst[c] = stencil(
                    src[max(c - 1, 0)], src[c], src[min(c + 1, outer - 1)], low, place, inside, rate, keep
                )
        final = x0 if SUBSTEPS % 2 == 0 else x1
        for b in range(blocks):
            drive[:, b * EDGE : (b + 1) * EDGE] = final[b + 1]

    out[0] = mixed[...] + jnp.dot(spread[...], drive[...], precision=HIGHEST, preferred_element_type=F32)


def finish(meta, got, flux, mixed, spread, rates, index, weight):
    columns = flux.shape[1]
    outer = columns // EDGE + 2
    return pl.pallas_call(
        final_kernel,
        in_specs=[smem()] + [vmem()] * 7,
        out_specs=[vmem()] * 2,
        out_shape=[
            jax.ShapeDtypeStruct((1, LEVELS, columns), F32),
            jax.ShapeDtypeStruct((FIELDS, columns), F32),
        ],
        scratch_shapes=[
            pltpu.VMEM((outer, FIELDS, EDGE), F32),
            pltpu.VMEM((outer, FIELDS, EDGE), F32),
            pltpu.VMEM((FIELDS, columns), F32),
        ],
        compiler_params=pltpu.CompilerParams(vmem_limit_bytes=32 * 2**20),
        name="finish",
    )(meta, got, flux, mixed, spread, rates, index, weight)


def swap(x, axis, bit):
    return lax.ppermute(x, axis, [(i, i ^ bit) for i in range(lax.axis_size(axis))])


def shards(
    state,
    diffusivity,
    neighbours,
    vertical_mix,
    transfer_rates,
    bulk_map,
    absorb_map,
    block_dest,
    block_rows,
    block_weights,
):
    tiles, groups = lax.axis_size("tile"), lax.axis_size("mp")
    my_tile, my_group = lax.axis_index("tile"), lax.axis_index("mp")
    strip = jnp.minimum(my_group, block_dest.shape[1] - 1)
    meta = jnp.stack([my_group, my_tile, jnp.int32(groups - 1), strip]).astype(jnp.int32)
    sst, to_left, to_right = prep(state, neighbours, diffusivity)
    bit = groups // 2
    while bit:
        other = swap(sst, "mp", bit)
        sst = jnp.where((my_group & bit) != 0, sst, other)
        bit //= 2
    left = lax.ppermute(to_right, "tile", [(i, (i + 1) % tiles) for i in range(tiles)])
    right = lax.ppermute(to_left, "tile", [((i + 1) % tiles, i) for i in range(tiles)])
    bit = 1
    while bit < tiles:
        sst = jnp.concatenate([sst, swap(sst, "tile", bit)], axis=0)
        bit *= 2
    mixed, mapped, spread, index, weight = mix_state(
        meta, state, left, right, neighbours, diffusivity, vertical_mix, bulk_map, absorb_map
    )
    message, flux = make_flux(
        meta, groups, tiles, block_dest, block_rows, sst, block_weights, mapped, transfer_rates
    )
    got = lax.all_to_all(message, ("mp", "tile"), 0, 0, tiled=True)
    return tuple(finish(meta, got, flux, mixed, spread, transfer_rates, index, weight))


def solution(mesh):
    placed = (
        P("mp", None, "tile"),
        P("mp", None, "tile"),
        P("mp", None, "tile"),
        P("mp", None, None),
        P("mp", None, "tile"),
        P(),
        P(),
        P("tile", None, None),
        P("tile", None, None),
        P("tile", None, None, None, None),
    )
    return jax.shard_map(
        shards,
        mesh=mesh,
        in_specs=placed,
        out_specs=(P("mp", None, "tile"), P(None, "tile")),
        check_vma=False,
    )
```

```python
import jax
import jax.numpy as jnp
from jax import lax
from jax.experimental import pallas as pl
from jax.experimental.pallas import tpu as pltpu
from jax.sharding import PartitionSpec as P

HALO_WIDTH = 32
SUBSTEPS = 4
FIELDS = 8
EDGE = 128
LEVELS = 128
NEIGH = 6
SLOTS = 4
PAYLOAD = 48
F32 = jnp.float32
BF16 = jnp.bfloat16
HIGHEST = lax.Precision.HIGHEST


def lanes(shape):
    return lax.broadcasted_iota(jnp.int32, shape, len(shape) - 1)


def prep_kernel(top, first, last, nbr, dif, sst, to_left, to_right):
    columns = nbr.shape[2]
    blocks = columns // EDGE
    for b in range(blocks):
        row = top[0, 0:1, b * EDGE : (b + 1) * EDGE]
        sst[b : b + 1, :] = row.astype(BF16).astype(F32)
    for out, edge, b in ((to_left, first, 0), (to_right, last, blocks - 1)):
        at = slice(b * EDGE, (b + 1) * EDGE)
        out[0:LEVELS, :] = edge[0]
        for k in range(NEIGH):
            out[LEVELS + k : LEVELS + k + 1, :] = (nbr[k, :, at] - (HALO_WIDTH + b * EDGE)).astype(F32)
            out[LEVELS + 8 + k : LEVELS + 9 + k, :] = dif[k, :, at]
        out[LEVELS + 6 : LEVELS + 8, :] = jnp.zeros((2, EDGE), F32)
        out[LEVELS + 14 : LEVELS + 16, :] = jnp.zeros((2, EDGE), F32)


def prep(state, neighbours, diffusivity):
    columns = state.shape[2]
    blocks = columns // EDGE
    whole = pl.BlockSpec((NEIGH, 1, columns), lambda i: (0, 0, 0))
    halo = jax.ShapeDtypeStruct((LEVELS + 16, EDGE), F32)
    halo_spec = pl.BlockSpec((LEVELS + 16, EDGE), lambda i: (0, 0))
    return pl.pallas_call(
        prep_kernel,
        grid=(1,),
        in_specs=[
            pl.BlockSpec((1, 8, columns), lambda i: (0, 0, 0)),
            pl.BlockSpec((1, LEVELS, EDGE), lambda i: (0, 0, 0)),
            pl.BlockSpec((1, LEVELS, EDGE), lambda i: (0, 0, blocks - 1)),
            whole,
            whole,
        ],
        out_specs=[pl.BlockSpec((blocks, EDGE), lambda i: (0, 0)), halo_spec, halo_spec],
        out_shape=[jax.ShapeDtypeStruct((blocks, EDGE), F32), halo, halo],
        name="prep",
    )(state, state, state, neighbours, diffusivity)


def take(x, index):
    return jnp.take_along_axis(x, index, axis=1, mode="promise_in_bounds")


def stencil(xp, xc, xn, low, place, inside, weight, keep):
    beyond = jnp.where(low, xn, xp)
    total = keep * xc
    for k in range(NEIGH):
        value = jnp.where(inside[k], take(xc, place[k]), take(beyond, place[k]))
        total = total + weight[k] * value
    return total


def block_terms(index, weight, c):
    shape = (8, EDGE)
    place, inside, rate = [], [], []
    for k in range(NEIGH):
        j = jnp.broadcast_to(index[c, k : k + 1, :], shape)
        inside.append((j >= 0) & (j < EDGE))
        place.append(j & (EDGE - 1))
        rate.append(jnp.broadcast_to(weight[c, k : k + 1, :], shape))
    keep = jnp.broadcast_to(weight[c, NEIGH : NEIGH + 1, :], shape)
    return place, inside, rate, keep


def split(x):
    high = x.astype(BF16)
    return high, (x - high.astype(F32)).astype(BF16)


def vmem():
    return pl.BlockSpec(memory_space=pltpu.VMEM)


def smem():
    return pl.BlockSpec(memory_space=pltpu.SMEM)


def params():
    return pltpu.CompilerParams(vmem_limit_bytes=24 * 2**20)


def shape_of(*shape, dtype=F32):
    return jax.ShapeDtypeStruct(shape, dtype)


def cost(flops, size):
    return pl.CostEstimate(flops=flops, bytes_accessed=size, transcendentals=0)


def map_kernel(meta, state, bulk, weights, mapped, held, done):
    copy = pltpu.make_async_copy(weights.at[0, meta[3]], held, done)
    copy.start()
    mapped[...] = jnp.dot(bulk[...], state[0], precision=HIGHEST, preferred_element_type=F32)
    copy.wait()


def map_state(meta, state, bulk_map, block_weights):
    columns, blocks = state.shape[2], block_weights.shape[2]
    return pl.pallas_call(
        map_kernel,
        in_specs=[smem(), vmem(), vmem(), pl.BlockSpec(memory_space=pl.ANY)],
        out_specs=[vmem(), vmem()],
        out_shape=[shape_of(FIELDS, columns), shape_of(blocks, EDGE, EDGE, dtype=BF16)],
        scratch_shapes=[pltpu.SemaphoreType.DMA],
        compiler_params=params(),
        cost_estimate=cost(2**30, 2**21),
        name="map_state",
    )(meta, state, bulk_map, block_weights)


def build_band(index, weight, band, c):
    group = 8
    targets = []
    for k in range(NEIGH):
        j = index[c, k : k + 1, :]
        j = jnp.where((j >= 0) & (j < EDGE), j, EDGE + (j & (EDGE - 1)))
        targets.append((jnp.broadcast_to(j, (group, EDGE)), jnp.broadcast_to(weight[c, k : k + 1, :], (group, EDGE))))
    row = lax.broadcasted_iota(jnp.int32, (group, EDGE), 0)
    for start in range(0, 2 * EDGE, 16):
        if EDGE + HALO_WIDTH <= start < 2 * EDGE - HALO_WIDTH:
            high = jnp.zeros((16, EDGE), BF16)
            low = high
        else:
            parts = []
            for at in (start, start + group):
                total = jnp.zeros((group, EDGE), F32)
                for j, d in targets:
                    total = total + jnp.where(row == j - at, d, 0.0)
                parts.append(total)
            exact = jnp.concatenate(parts, axis=0)
            high = exact.astype(BF16)
            low = (exact - high.astype(F32)).astype(BF16)
        band[c, start : start + 16, 0:EDGE] = high
        band[c, start : start + 16, EDGE : 2 * EDGE] = low


def fill_terms(index, weight, c, j, d):
    index[c, 0:NEIGH, :] = j
    index[c, NEIGH:8, :] = jnp.zeros((2, EDGE), jnp.int32)
    weight[c, 0:NEIGH, :] = d
    weight[c, NEIGH:8, :] = jnp.broadcast_to(1.0 - jnp.sum(d, axis=0, keepdims=True), (2, EDGE))


def band_kernel(meta, nbr, dif, vmix, absorb, index, weight, band, power, spread):
    blocks = nbr.shape[2] // EDGE
    for c in range(blocks):
        at = slice(c * EDGE, (c + 1) * EDGE)
        j = jnp.concatenate([nbr[k, :, at] for k in range(NEIGH)], axis=0) - (HALO_WIDTH + c * EDGE)
        d = jnp.concatenate([dif[k, :, at] for k in range(NEIGH)], axis=0)
        fill_terms(index, weight, c, j, d)

    @pl.loop(0, blocks, unroll=2)
    def _(c):
        build_band(index, weight, band, c)

    eye = (lax.broadcasted_iota(jnp.int32, (LEVELS, LEVELS), 0) == lanes((LEVELS, LEVELS))).astype(F32)
    a = eye + 0.25 * vmix[0]
    total = a
    for _ in range(SUBSTEPS - 1):
        total = jnp.dot(total, a, precision=HIGHEST, preferred_element_type=F32)
    power[...] = total
    mapped_absorb = jnp.dot(total, absorb[...], precision=HIGHEST, preferred_element_type=F32)
    spread[...] = jnp.where(meta[0] == meta[2], absorb[...], -mapped_absorb)


def make_band(meta, neighbours, diffusivity, vertical_mix, absorb_map):
    blocks = neighbours.shape[2] // EDGE
    return pl.pallas_call(
        band_kernel,
        in_specs=[smem()] + [vmem()] * 4,
        out_specs=[vmem()] * 5,
        out_shape=[
            shape_of(blocks, 8, EDGE, dtype=jnp.int32),
            shape_of(blocks, 8, EDGE),
            shape_of(blocks, 2 * EDGE, 2 * EDGE, dtype=BF16),
            shape_of(LEVELS, LEVELS),
            shape_of(LEVELS, FIELDS),
        ],
        compiler_params=params(),
        cost_estimate=cost(2**31, 2**22),
        name="make_band",
    )(meta, neighbours, diffusivity, vertical_mix, absorb_map)


def one_step(e, f, f_next, weight, weight_halo, band, band_halo, e_next, outer, final):
    low = lanes((2 * LEVELS, EDGE)) < EDGE // 2
    for c in range(1, outer - 1) if final else range(outer):
        edge = 0 if c == 0 else 1 if c == outer - 1 else None
        matrix = band[c - 1] if edge is None else band_halo[edge]
        keep = weight[c - 1, NEIGH : NEIGH + 1, :] if edge is None else weight_halo[edge, NEIGH : NEIGH + 1, :]
        near = jnp.concatenate([f[c], jnp.where(low, f[min(c + 1, outer - 1)], f[max(c - 1, 0)])], axis=1)
        product = jnp.dot(near, matrix, preferred_element_type=F32)
        x = keep * e[c] + (product[0:LEVELS, 0:EDGE] + (product[0:LEVELS, EDGE:] + product[LEVELS:, 0:EDGE]))
        e_next[c] = x
        if not final:
            f_next[c, 0:LEVELS, :], f_next[c, LEVELS : 2 * LEVELS, :] = split(x)


def first_kernel(state, left, right, weight, band, e_next, f_next, index_halo, weight_halo, band_halo, e, f):
    outer = weight.shape[0] + 2
    for edge, halo in ((0, left), (1, right)):
        j = halo[LEVELS : LEVELS + NEIGH, :].astype(jnp.int32)
        fill_terms(index_halo, weight_halo, edge, j, halo[LEVELS + 8 : LEVELS + 8 + NEIGH, :])
        build_band(index_halo, weight_halo, band_halo, edge)
    for c in range(outer):
        x = left[0:LEVELS, :] if c == 0 else right[0:LEVELS, :] if c == outer - 1 else state[0, :, (c - 1) * EDGE : c * EDGE]
        e[c] = x
        f[c, 0:LEVELS, :], f[c, LEVELS : 2 * LEVELS, :] = split(x)
    one_step(e, f, f_next, weight, weight_halo, band, band_halo, e_next, outer, False)


def first_step(state, left, right, weight, band):
    outer = weight.shape[0] + 2
    fields = [shape_of(outer, LEVELS, EDGE), shape_of(outer, 2 * LEVELS, EDGE, dtype=BF16)]
    return pl.pallas_call(
        first_kernel,
        in_specs=[vmem()] * 5,
        out_specs=[vmem()] * 5,
        out_shape=fields
        + [
            shape_of(2, 8, EDGE, dtype=jnp.int32),
            shape_of(2, 8, EDGE),
            shape_of(2, 2 * EDGE, 2 * EDGE, dtype=BF16),
        ],
        scratch_shapes=[pltpu.VMEM(x.shape, x.dtype) for x in fields],
        compiler_params=params(),
        cost_estimate=cost(2**30, 2**22),
        name="first_step",
    )(state, left, right, weight, band)


def middle_kernel(e, f, weight, weight_halo, band, band_halo, e_next, f_next):
    one_step(e, f, f_next, weight, weight_halo, band, band_halo, e_next, e.shape[0], False)


def last_kernel(e, f, weight, weight_halo, band, band_halo, power, mixed, e_next):
    outer = e.shape[0]
    one_step(e, f, None, weight, weight_halo, band, band_halo, e_next, outer, True)
    for c in range(outer - 2):
        mixed[:, c * EDGE : (c + 1) * EDGE] = jnp.dot(
            power[...], e_next[c + 1], precision=HIGHEST, preferred_element_type=F32
        )


def middle_step(e, f, weight, weight_halo, band, band_halo):
    return pl.pallas_call(
        middle_kernel,
        in_specs=[vmem()] * 6,
        out_specs=[vmem()] * 2,
        out_shape=[shape_of(*e.shape), shape_of(*f.shape, dtype=BF16)],
        compiler_params=params(),
        cost_estimate=cost(2**30, 2**22),
        name="middle_step",
    )(e, f, weight, weight_halo, band, band_halo)


def last_step(e, f, weight, weight_halo, band, band_halo, power):
    return pl.pallas_call(
        last_kernel,
        in_specs=[vmem()] * 7,
        out_specs=vmem(),
        out_shape=shape_of(LEVELS, (e.shape[0] - 2) * EDGE),
        scratch_shapes=[pltpu.VMEM(e.shape, F32)],
        compiler_params=params(),
        cost_estimate=cost(2**30, 2**22),
        name="last_step",
    )(e, f, weight, weight_halo, band, band_halo, power)


def reverse_bits(value, count):
    return sum(((value >> k) & 1) << (count - 1 - k) for k in range(count))


def flux_kernel(meta, dest, live, sst, weights, mapped, rates, keep, send, flux, first, last, terms, codes, count):
    blocks = mapped.shape[1] // EDGE
    tiles = terms.shape[0] // SLOTS
    bits = tiles.bit_length() - 1
    my_tile, strip = meta[1], meta[3]
    shape = (FIELDS, EDGE)
    lane = lanes(shape)
    for t in range(tiles):
        count[t] = 0
    codes[...] = jnp.zeros_like(codes)
    terms[...] = jnp.zeros_like(terms)
    active = meta[0] != meta[2]
    for g in range(blocks):
        at = slice(g * EDGE, (g + 1) * EDGE)
        warmth = jnp.zeros(shape, F32)
        held = []
        for h in range(2):
            b = 2 * g + h
            where = dest[strip, 0, b]
            owner, local = (where // blocks) ^ my_tile, where % blocks
            slot = count[owner]
            count[owner] = slot + 1
            start = (owner % 4) * (SLOTS * FIELDS) + slot * FIELDS
            mine = (lane >= start) & (lane < start + FIELDS) & active
            codes[owner] = codes[owner] + jnp.where(mine, local * FIELDS + 1 + lane - start, 0)
            alive = lane < live[strip, 0, b]
            row = sst[pl.ds(owner * blocks + local, 1), :]
            row = jnp.where(alive, jnp.broadcast_to(row, shape), 0.0).astype(BF16)
            warmth = warmth + lax.dot_general(
                row, weights[b], (((1,), (1,)), ((), ())), preferred_element_type=F32
            )
            held.append((b, owner * SLOTS + slot, alive))
        here = (mapped[:, at] - rates[0, :, at] * warmth).astype(BF16)
        flux[:, at] = here.astype(F32)
        if g == 0:
            first[...] = here.astype(F32)
        if g == blocks - 1:
            last[...] = here.astype(F32)
        for b, spot, alive in held:
            part = jnp.dot(here, weights[b], preferred_element_type=F32)
            terms[spot] = jnp.where(alive, part, 0.0)
    for t in range(tiles):
        body = terms[t * SLOTS : (t + 1) * SLOTS].reshape(SLOTS * FIELDS, EDGE).astype(BF16)
        place = codes[t].astype(F32)
        i = reverse_bits(t, bits)
        out, i = (keep, i) if i < tiles // 2 else (send, i - tiles // 2)
        out[i, 0 : SLOTS * FIELDS, :] = body
        out[i, SLOTS * FIELDS : PAYLOAD, :] = jnp.concatenate([place, place], axis=0).astype(BF16)


def make_flux(meta, tiles, dest, live, sst, weights, mapped, rates):
    columns = mapped.shape[1]
    piece = shape_of(tiles // 2, PAYLOAD, EDGE, dtype=BF16)
    return pl.pallas_call(
        flux_kernel,
        in_specs=[smem()] * 3 + [vmem()] * 4,
        out_specs=[vmem()] * 5,
        out_shape=[piece, piece, shape_of(FIELDS, columns), shape_of(FIELDS, EDGE), shape_of(FIELDS, EDGE)],
        scratch_shapes=[
            pltpu.VMEM((tiles * SLOTS, FIELDS, EDGE), F32),
            pltpu.VMEM((tiles, 8, EDGE), jnp.int32),
            pltpu.SMEM((tiles,), jnp.int32),
        ],
        compiler_params=params(),
        cost_estimate=cost(2**30, 2**22),
        name="make_flux",
    )(meta, dest, live, sst, weights, mapped, rates)


def collect_kernel(near, far, out):
    body = SLOTS * FIELDS
    row = (lax.broadcasted_iota(jnp.int32, (EDGE, EDGE), 0) + 1).astype(F32)
    total = jnp.zeros((EDGE, EDGE), F32)
    for got in (near, far):
        for q in range(0, got.shape[0], 4):
            codes = got[q, body:PAYLOAD, :].astype(F32)
            for p in range(q + 1, q + 4):
                codes = codes + got[p, body:PAYLOAD, :].astype(F32)
            chosen = (row == jnp.broadcast_to(codes[0:1, :], (EDGE, EDGE))).astype(BF16)
            data = jnp.concatenate([got[p, 0:body, :] for p in range(q, q + 4)], axis=0)
            total = total + jnp.dot(chosen, data, preferred_element_type=F32)
    out[...] = total


def collect(near, far):
    return pl.pallas_call(
        collect_kernel,
        in_specs=[vmem()] * 2,
        out_specs=vmem(),
        out_shape=shape_of(EDGE, EDGE),
        compiler_params=params(),
        cost_estimate=cost(2**27, 2**18),
        name="collect",
    )(near, far)


def spread_kernel(flux, before, after, index, weight, index_halo, weight_halo, out, x0, x1):
    blocks = index.shape[0]
    outer = blocks + 2
    x0[0] = before[...]
    x0[outer - 1] = after[...]
    for b in range(blocks):
        x0[b + 1] = flux[:, b * EDGE : (b + 1) * EDGE]
    low = lanes((8, EDGE)) < EDGE // 2
    for step in range(SUBSTEPS):
        src, dst = (x0, x1) if step % 2 == 0 else (x1, x0)
        for c in range(outer) if step < SUBSTEPS - 1 else range(1, outer - 1):
            edge = 0 if c == 0 else 1 if c == outer - 1 else None
            found = block_terms(index, weight, c - 1) if edge is None else block_terms(index_halo, weight_halo, edge)
            value = stencil(src[max(c - 1, 0)], src[c], src[min(c + 1, outer - 1)], low, *found)
            if step < SUBSTEPS - 1:
                dst[c] = value
            else:
                out[:, (c - 1) * EDGE : c * EDGE] = value


def spread_flux(flux, before, after, index, weight, index_halo, weight_halo):
    outer = index.shape[0] + 2
    return pl.pallas_call(
        spread_kernel,
        in_specs=[vmem()] * 7,
        out_specs=vmem(),
        out_shape=shape_of(*flux.shape),
        scratch_shapes=[pltpu.VMEM((outer, FIELDS, EDGE), F32)] * 2,
        compiler_params=params(),
        cost_estimate=cost(2**30, 2**22),
        name="spread_flux",
    )(flux, before, after, index, weight, index_halo, weight_halo)


def final_kernel(meta, part0, part1, mixed, spread, rates, strips, out, ocean, drive):
    blocks = mixed.shape[1] // EDGE
    is_ocean = meta[0] == meta[2]
    for b in range(blocks):
        at = slice(b * EDGE, (b + 1) * EDGE)
        rows = slice(b * FIELDS, (b + 1) * FIELDS)
        total = part0[rows, :] + part1[rows, :]
        ocean[:, at] = total
        drive[:, at] = jnp.where(is_ocean, rates[0, :, at] * total, strips[:, at])
    out[0] = mixed[...] + jnp.dot(spread[...], drive[...], precision=HIGHEST, preferred_element_type=F32)


def finish(meta, part0, part1, mixed, spread, rates, strips):
    columns = mixed.shape[1]
    return pl.pallas_call(
        final_kernel,
        in_specs=[smem()] + [vmem()] * 6,
        out_specs=[vmem()] * 2,
        out_shape=[shape_of(1, LEVELS, columns), shape_of(FIELDS, columns)],
        scratch_shapes=[pltpu.VMEM((FIELDS, columns), F32)],
        compiler_params=params(),
        cost_estimate=cost(2**28, 2**21),
        name="finish",
    )(meta, part0, part1, mixed, spread, rates, strips)


def swap(x, axis, bit):
    return lax.ppermute(x, axis, [(i, i ^ bit) for i in range(lax.axis_size(axis))])


def shift(x, axis, by):
    size = lax.axis_size(axis)
    return lax.ppermute(x, axis, [(i, (i + by) % size) for i in range(size)])


def shards(
    state,
    diffusivity,
    neighbours,
    vertical_mix,
    transfer_rates,
    bulk_map,
    absorb_map,
    block_dest,
    block_rows,
    block_weights,
):
    tiles, groups = lax.axis_size("tile"), lax.axis_size("mp")
    my_tile, my_group = lax.axis_index("tile"), lax.axis_index("mp")
    strip = jnp.minimum(my_group, block_dest.shape[1] - 1)
    meta = jnp.stack([my_group, my_tile, jnp.int32(groups - 1), strip]).astype(jnp.int32)
    neighbours = jnp.transpose(neighbours, (1, 0, 2))
    diffusivity = jnp.transpose(diffusivity, (1, 0, 2))
    dest = jnp.transpose(block_dest, (1, 0, 2))
    live = jnp.transpose(block_rows, (1, 0, 2))
    sst, to_left, to_right = prep(state, neighbours, diffusivity)
    mapped, weights = map_state(meta, state, bulk_map, block_weights)
    index, weight, band, power, spread = make_band(meta, neighbours, diffusivity, vertical_mix, absorb_map)
    bit = groups // 2
    while bit:
        other = swap(sst, "mp", bit)
        sst = jnp.where((my_group & bit) != 0, sst, other)
        bit //= 2
    left = shift(to_right, "tile", 1)
    right = shift(to_left, "tile", -1)
    bit = 1
    while bit < tiles:
        sst = jnp.concatenate([sst, swap(sst, "tile", bit)], axis=0)
        bit *= 2
    keep, send, flux, first, last = make_flux(meta, tiles, dest, live, sst, weights, mapped, transfer_rates)
    e, f, index_halo, weight_halo, band_halo = first_step(state, left, right, weight, band)
    for _ in range(SUBSTEPS - 2):
        e, f = middle_step(e, f, weight, weight_halo, band, band_halo)
    mixed = last_step(e, f, weight, weight_halo, band, band_halo, power)
    keep, send = keep[None], send[None]
    bit = 1
    while True:
        got = swap(send, "tile", bit)
        bit *= 2
        if bit == tiles:
            break
        half = keep.shape[1] // 2
        send = jnp.concatenate([keep[:, half:], got[:, half:]], axis=0)
        keep = jnp.concatenate([keep[:, :half], got[:, :half]], axis=0)
    before = shift(last, "tile", 1)
    after = shift(first, "tile", -1)
    strips = spread_flux(flux, before, after, index, weight, index_halo, weight_halo)
    total = collect(keep[:, 0], got[:, 0])
    bit = groups // 2
    while bit > 1:
        total = total + swap(total, "mp", bit)
        bit //= 2
    return tuple(finish(meta, total, swap(total, "mp", 1), mixed, spread, transfer_rates, strips))


def solution(mesh):
    placed = (
        P("mp", None, "tile"),
        P("mp", None, "tile"),
        P("mp", None, "tile"),
        P("mp", None, None),
        P("mp", None, "tile"),
        P(),
        P(),
        P("tile", None, None),
        P("tile", None, None),
        P("tile", None, None, None, None),
    )
    return jax.shard_map(
        shards,
        mesh=mesh,
        in_specs=placed,
        out_specs=(P("mp", None, "tile"), P(None, "tile")),
        check_vma=False,
    )
```

```python
import jax
import jax.numpy as jnp
from jax import lax
from jax.experimental import pallas as pl
from jax.experimental.pallas import tpu as pltpu
from jax.sharding import PartitionSpec as P

HALO_WIDTH = 32
SUBSTEPS = 4
FIELDS = 8
EDGE = 128
LEVELS = 128
NEIGH = 6
SLOTS = 4
PAYLOAD = 48
HALO_ROWS = 2 * LEVELS + 2 * EDGE + 48
F32 = jnp.float32
BF16 = jnp.bfloat16
HIGHEST = lax.Precision.HIGHEST


def lanes(shape):
    return lax.broadcasted_iota(jnp.int32, shape, len(shape) - 1)


def split(x):
    high = x.astype(BF16)
    return high, (x - high.astype(F32)).astype(BF16)


def vmem():
    return pl.BlockSpec(memory_space=pltpu.VMEM)


def smem():
    return pl.BlockSpec(memory_space=pltpu.SMEM)


def params():
    return pltpu.CompilerParams(vmem_limit_bytes=10 * 2**20)


def shape_of(*shape, dtype=F32):
    return jax.ShapeDtypeStruct(shape, dtype)


def cost(flops, size):
    return pl.CostEstimate(flops=1024, bytes_accessed=1024, transcendentals=0)


def in_hbm(x):
    return pltpu.with_memory_space_constraint(x, pltpu.HBM)


def anywhere():
    return pl.BlockSpec(memory_space=pltpu.HBM)


def surface_kernel(state, sst, top, done):
    copy = pltpu.make_async_copy(state.at[0, 0:8, :], top, done)
    copy.start()
    copy.wait()
    for b in range(sst.shape[0]):
        row = top[0:1, b * EDGE : (b + 1) * EDGE]
        sst[b : b + 1, :] = row.astype(BF16).astype(F32)


def surface(state):
    columns = state.shape[2]
    return pl.pallas_call(
        surface_kernel,
        in_specs=[anywhere()],
        out_specs=vmem(),
        out_shape=shape_of(columns // EDGE, EDGE),
        scratch_shapes=[pltpu.VMEM((8, columns), F32), pltpu.SemaphoreType.DMA],
        compiler_params=params(),
        cost_estimate=cost(2**20, 2**16),
        name="surface",
    )(in_hbm(state))


def load_kernel(meta, dest_h, live_h, state, nbr, dif, bulk, dest, live, spots, places, state_v, nbr_v, dif_v, bulk_v, codes, count, done):
    tiles = places.shape[0]
    blocks = state_v.shape[1] // EDGE
    pairs = [(dest_h, dest), (live_h, live), (state.at[0], state_v), (nbr, nbr_v), (dif, dif_v), (bulk, bulk_v)]
    copies = [pltpu.make_async_copy(a, b, done.at[k]) for k, (a, b) in enumerate(pairs)]
    for copy in copies:
        copy.start()
    lane = lanes((8, EDGE))
    for t in range(tiles):
        count[t] = 0
    codes[...] = jnp.zeros_like(codes)
    active = meta[0] != meta[2]
    copies[0].wait()
    for b in range(spots.shape[0]):
        where = dest[meta[3], 0, b]
        owner, local = (where // blocks) ^ meta[1], where % blocks
        slot = count[owner]
        count[owner] = slot + 1
        spots[b] = owner * SLOTS + slot
        start = (owner % 4) * (SLOTS * FIELDS) + slot * FIELDS
        mine = (lane >= start) & (lane < start + FIELDS) & active
        codes[owner] = codes[owner] + jnp.where(mine, local * FIELDS + 1 + lane - start, 0)
    for t in range(tiles):
        place = codes[t].astype(F32)
        places[t] = jnp.concatenate([place, place], axis=0).astype(BF16)
    for copy in copies[1:]:
        copy.wait()


def load(meta, tiles, dest, live, state, neighbours, diffusivity, bulk_map):
    columns = state.shape[2]
    arrays = (dest, live, state, neighbours, diffusivity, bulk_map)
    return pl.pallas_call(
        load_kernel,
        in_specs=[smem()] + [anywhere()] * 6,
        out_specs=[smem()] * 3 + [vmem()] * 5,
        out_shape=[
            shape_of(*dest.shape, dtype=jnp.int32),
            shape_of(*live.shape, dtype=jnp.int32),
            shape_of(dest.shape[2], dtype=jnp.int32),
            shape_of(tiles, 16, EDGE, dtype=BF16),
            shape_of(LEVELS, columns),
            shape_of(NEIGH, 1, columns, dtype=jnp.int32),
            shape_of(NEIGH, 1, columns),
            shape_of(FIELDS, LEVELS),
        ],
        scratch_shapes=[
            pltpu.VMEM((tiles, 8, EDGE), jnp.int32),
            pltpu.SMEM((tiles,), jnp.int32),
            pltpu.SemaphoreType.DMA((6,)),
        ],
        compiler_params=params(),
        cost_estimate=cost(2**20, 2**21),
        name="load",
    )(meta, *(in_hbm(x) for x in arrays))


def weights_kernel(meta, weights, rates, vmix, absorb, weights_v, turned, rates_v, vmix_v, absorb_v, done):
    count = weights_v.shape[0]
    part = count // 8
    pairs = [(weights.at[0, meta[3], pl.ds(k * part, part)], weights_v.at[pl.ds(k * part, part)]) for k in range(8)]
    pairs += [(rates.at[0], rates_v), (vmix.at[0], vmix_v), (absorb, absorb_v)]
    copies = [pltpu.make_async_copy(a, b, done.at[k]) for k, (a, b) in enumerate(pairs)]
    for copy in copies:
        copy.start()
    for k in range(8):
        copies[k].wait()
        for b in range(k * part, (k + 1) * part):
            turned[b] = jnp.transpose(weights_v[b])
    for copy in copies[8:]:
        copy.wait()


def load_weights(meta, weights, rates, vertical_mix, absorb_map):
    columns, blocks = rates.shape[2], weights.shape[2]
    arrays = (weights, rates, vertical_mix, absorb_map)
    square = shape_of(blocks, EDGE, EDGE, dtype=BF16)
    return pl.pallas_call(
        weights_kernel,
        in_specs=[smem()] + [anywhere()] * 4,
        out_specs=[vmem()] * 5,
        out_shape=[square, square, shape_of(FIELDS, columns), shape_of(LEVELS, LEVELS), shape_of(FIELDS, LEVELS)],
        scratch_shapes=[pltpu.SemaphoreType.DMA((11,))],
        compiler_params=params(),
        cost_estimate=cost(2**20, 2**21),
        name="load_weights",
    )(meta, *(in_hbm(x) for x in arrays))


def halo_kernel(meta, dest, live, state, weights, nbr, dif, rates, absorb_t, out_a, out_b, absorb):
    blocks = state.shape[1] // EDGE
    strip = meta[3]

    def fill(out, e):
        b = 0 if e == 0 else blocks - 1
        at = slice(b * EDGE, (b + 1) * EDGE)
        out[0:LEVELS, :], out[LEVELS : 2 * LEVELS, :] = split(state[:, at])
        base = 2 * LEVELS
        out[base : base + EDGE, :] = weights[2 * b]
        out[base + EDGE : base + 2 * EDGE, :] = weights[2 * b + 1]
        base += 2 * EDGE
        row = lax.broadcasted_iota(jnp.int32, (8, EDGE), 0)
        place = jnp.zeros((8, EDGE), jnp.int32)
        rate = jnp.zeros((8, EDGE), F32)
        for k in range(NEIGH):
            place = jnp.where(row == k, nbr[k, :, at] - (HALO_WIDTH + b * EDGE), place)
            rate = jnp.where(row == k, dif[k, :, at], rate)
        target = jnp.zeros((8, EDGE), jnp.int32)
        for h in range(2):
            block = dest[strip, 0, 2 * b + h]
            for k, value in enumerate((block // blocks, block % blocks, live[strip, 0, 2 * b + h])):
                target = jnp.where(row == 3 * h + k, value, target)
        high, low = split(rate)
        out[base : base + 16, :] = jnp.concatenate([place, target], axis=0).astype(F32).astype(BF16)
        out[base + 16 : base + 32, :] = jnp.concatenate([high.astype(F32), low.astype(F32)], axis=0).astype(BF16)
        high, low = split(rates[:, at])
        out[base + 32 : base + 48, :] = jnp.concatenate([high.astype(F32), low.astype(F32)], axis=0).astype(BF16)

    odd = meta[1] & 1

    @pl.when(odd == 0)
    def _():
        fill(out_a, 1)
        fill(out_b, 0)

    @pl.when(odd == 1)
    def _():
        fill(out_a, 0)
        fill(out_b, 1)

    tall = jnp.concatenate([absorb_t[...], jnp.zeros((LEVELS - FIELDS, LEVELS), F32)], axis=0)
    absorb[...] = jnp.transpose(tall)[:, 0:FIELDS]


def make_halo(meta, dest, live, state, weights, neighbours, diffusivity, rates, absorb_t):
    halo = shape_of(HALO_ROWS, EDGE, dtype=BF16)
    return pl.pallas_call(
        halo_kernel,
        in_specs=[smem()] * 3 + [vmem()] * 6,
        out_specs=[vmem()] * 3,
        out_shape=[halo, halo, shape_of(LEVELS, FIELDS)],
        compiler_params=params(),
        cost_estimate=cost(2**20, 2**18),
        name="make_halo",
    )(meta, dest, live, state, weights, neighbours, diffusivity, rates, absorb_t)


def map_kernel(state, bulk, mapped):
    b0, b1 = split(bulk[...])
    both = jnp.concatenate([b0.astype(F32), b1.astype(F32)], axis=0).astype(BF16)
    for c in range(state.shape[1] // EDGE):
        at = slice(c * EDGE, (c + 1) * EDGE)
        x0, x1 = split(state[:, at])
        high = jnp.dot(both, x0, preferred_element_type=F32)
        low = jnp.dot(both, x1, preferred_element_type=F32)
        mapped[:, at] = high[0:FIELDS] + (high[FIELDS:] + low[0:FIELDS])


def map_state(state, bulk_map):
    return pl.pallas_call(
        map_kernel,
        in_specs=[vmem()] * 2,
        out_specs=vmem(),
        out_shape=shape_of(FIELDS, state.shape[1]),
        compiler_params=params(),
        cost_estimate=cost(2**28, 2**20),
        name="map_state",
    )(state, bulk_map)


def build_band(index, weight, band, c):
    group = 8
    targets = []
    for k in range(NEIGH):
        j = index[c, k : k + 1, :]
        j = jnp.where((j >= 0) & (j < EDGE), j, EDGE + (j & (EDGE - 1)))
        targets.append((jnp.broadcast_to(j, (group, EDGE)), jnp.broadcast_to(weight[c, k : k + 1, :], (group, EDGE))))
    row = lax.broadcasted_iota(jnp.int32, (group, EDGE), 0)
    for start in range(0, 2 * EDGE, 16):
        if EDGE + HALO_WIDTH <= start < 2 * EDGE - HALO_WIDTH:
            high = jnp.zeros((16, EDGE), BF16)
            low = high
        else:
            parts = []
            for at in (start, start + group):
                total = jnp.zeros((group, EDGE), F32)
                for j, d in targets:
                    total = total + jnp.where(row == j - at, d, 0.0)
                parts.append(total)
            exact = jnp.concatenate(parts, axis=0)
            high = exact.astype(BF16)
            low = (exact - high.astype(F32)).astype(BF16)
        band[c, start : start + 16, 0:EDGE] = high
        band[c, start : start + 16, EDGE : 2 * EDGE] = low


def fill_terms(index, weight, c, j, d):
    index[c, 0:NEIGH, :] = j
    index[c, NEIGH:8, :] = jnp.zeros((2, EDGE), jnp.int32)
    weight[c, 0:NEIGH, :] = d
    weight[c, NEIGH:8, :] = jnp.broadcast_to(1.0 - jnp.sum(d, axis=0, keepdims=True), (2, EDGE))


def fill_terms(index, weight, c, j, d):
    index[c, 0:NEIGH, :] = j
    index[c, NEIGH:8, :] = jnp.zeros((2, EDGE), jnp.int32)
    weight[c, 0:NEIGH, :] = d
    weight[c, NEIGH:8, :] = jnp.broadcast_to(1.0 - jnp.sum(d, axis=0, keepdims=True), (2, EDGE))


def band_kernel(nbr, dif, weight, band, index):
    blocks = nbr.shape[2] // EDGE
    for c in range(blocks):
        at = slice(c * EDGE, (c + 1) * EDGE)
        j = jnp.concatenate([nbr[k, :, at] for k in range(NEIGH)], axis=0) - (HALO_WIDTH + c * EDGE)
        d = jnp.concatenate([dif[k, :, at] for k in range(NEIGH)], axis=0)
        fill_terms(index, weight, c, j, d)

    @pl.loop(0, blocks, unroll=2)
    def _(c):
        build_band(index, weight, band, c)


def make_band(neighbours, diffusivity):
    blocks = neighbours.shape[2] // EDGE
    return pl.pallas_call(
        band_kernel,
        in_specs=[vmem()] * 2,
        out_specs=[vmem()] * 2,
        out_shape=[shape_of(blocks, 8, EDGE), shape_of(blocks, 2 * EDGE, 2 * EDGE, dtype=BF16)],
        scratch_shapes=[pltpu.VMEM((blocks, 8, EDGE), jnp.int32)],
        compiler_params=params(),
        cost_estimate=cost(2**30, 2**22),
        name="make_band",
    )(neighbours, diffusivity)


def power_kernel(vmix, power):
    eye = (lax.broadcasted_iota(jnp.int32, (LEVELS, LEVELS), 0) == lanes((LEVELS, LEVELS))).astype(F32)
    total = eye + 0.25 * vmix[...]
    a = total
    for _ in range(SUBSTEPS - 1):
        total = jnp.dot(total, a, precision=HIGHEST, preferred_element_type=F32)
    power[...] = total


def make_power(vertical_mix):
    return pl.pallas_call(
        power_kernel,
        in_specs=[vmem()],
        out_specs=vmem(),
        out_shape=shape_of(LEVELS, LEVELS),
        compiler_params=params(),
        cost_estimate=cost(2**27, 2**18),
        name="make_power",
    )(vertical_mix)


def one_step(e, f, f_next, weight, weight_halo, band, band_halo, e_next, outer, final):
    low = lanes((2 * LEVELS, EDGE)) < EDGE // 2
    for c in range(1, outer - 1) if final else range(outer):
        edge = 0 if c == 0 else 1 if c == outer - 1 else None
        matrix = band[c - 1] if edge is None else band_halo[edge]
        keep = weight[c - 1, NEIGH : NEIGH + 1, :] if edge is None else weight_halo[edge, NEIGH : NEIGH + 1, :]
        near = jnp.concatenate([f(c), jnp.where(low, f(min(c + 1, outer - 1)), f(max(c - 1, 0)))], axis=1)
        product = jnp.dot(near, matrix, preferred_element_type=F32)
        x = keep * e(c) + (product[0:LEVELS, 0:EDGE] + (product[0:LEVELS, EDGE:] + product[LEVELS:, 0:EDGE]))
        e_next[c] = x
        if not final:
            f_next[c, 0:LEVELS, :], f_next[c, LEVELS : 2 * LEVELS, :] = split(x)


def three_parts(x):
    high = x.astype(BF16).astype(F32)
    middle = (x - high).astype(BF16).astype(F32)
    return high, middle, x - high - middle


def absorbing(meta, absorb):
    active = (meta[0] != meta[2]).astype(F32)
    return jnp.concatenate(three_parts(absorb[...] * active), axis=1).astype(BF16)


def absorbed(x, absorb, flux):
    return x - jnp.dot(absorb, jnp.concatenate([flux, flux, flux], axis=0).astype(BF16), preferred_element_type=F32)


def forced_kernel(meta, state, flux, absorb, e, f):
    matrix = absorbing(meta, absorb)
    for c in range(e.shape[0]):
        at = slice(c * EDGE, (c + 1) * EDGE)
        x = absorbed(state[:, at], matrix, flux[:, at])
        e[c] = x
        f[c, 0:LEVELS, :], f[c, LEVELS : 2 * LEVELS, :] = split(x)


def force_state(meta, state, flux, absorb_map):
    blocks = state.shape[1] // EDGE
    return pl.pallas_call(
        forced_kernel,
        in_specs=[smem()] + [vmem()] * 3,
        out_specs=[vmem()] * 2,
        out_shape=[shape_of(blocks, LEVELS, EDGE), shape_of(blocks, 2 * LEVELS, EDGE, dtype=BF16)],
        compiler_params=params(),
        cost_estimate=cost(2**28, 2**21),
        name="force_state",
    )(meta, state, flux, absorb_map)


def first_kernel(meta, e, f, sst, got_a, got_b, bulk, absorb, weight, band, e_next, f_next, weight_halo, band_halo, e_halo, f_halo, halo, index_halo):
    outer = weight.shape[0] + 2
    odd = meta[1] & 1

    @pl.when(odd == 0)
    def _():
        halo[0] = got_b[...]
        halo[1] = got_a[...]

    @pl.when(odd == 1)
    def _():
        halo[0] = got_a[...]
        halo[1] = got_b[...]

    matrix = absorbing(meta, absorb)
    surface_rows = sst[...].astype(BF16)
    lane = lanes((FIELDS, EDGE))
    for edge in range(2):
        base = 2 * LEVELS
        x = halo[edge, 0:LEVELS, :].astype(F32) + halo[edge, LEVELS : 2 * LEVELS, :].astype(F32)
        blocks_held = [halo[edge, base + h * EDGE : base + (h + 1) * EDGE, :] for h in range(2)]
        base += 2 * EDGE
        small = halo[edge, base : base + 16, :].astype(F32)
        rate = halo[edge, base + 16 : base + 32, :].astype(F32)
        scale = halo[edge, base + 32 : base + 48, :].astype(F32)
        fill_terms(index_halo, weight_halo, edge, small[0:NEIGH].astype(jnp.int32), (rate[0:8] + rate[8:16])[0:NEIGH])
        build_band(index_halo, weight_halo, band_halo, edge)
        target = small[8:16].astype(jnp.int32)
        warmth = jnp.zeros((FIELDS, EDGE), F32)
        for h in range(2):
            owner, local, alive = target[3 * h : 3 * h + 1], target[3 * h + 1 : 3 * h + 2], target[3 * h + 2 : 3 * h + 3]
            spot = jnp.broadcast_to((owner ^ meta[1]) * (outer - 2) + local, lane.shape)
            row = jnp.zeros((FIELDS, EDGE), F32)
            for q in range(0, sst.shape[0], EDGE):
                chosen = (lane + q == spot).astype(BF16)
                row = row + jnp.dot(chosen, surface_rows[q : q + EDGE], preferred_element_type=F32)
            row = jnp.where(lane < jnp.broadcast_to(alive, lane.shape), row, 0.0).astype(BF16)
            warmth = warmth + lax.dot_general(
                row, blocks_held[h], (((1,), (1,)), ((), ())), preferred_element_type=F32
            )
        linear = jnp.dot(bulk[...], x, precision=HIGHEST, preferred_element_type=F32)
        here = (linear - (scale[0:8] + scale[8:16]) * warmth).astype(BF16).astype(F32)
        x = absorbed(x, matrix, here)
        e_halo[edge] = x
        f_halo[edge, 0:LEVELS, :], f_halo[edge, LEVELS : 2 * LEVELS, :] = split(x)

    def block(own, edges):
        return lambda c: edges[0] if c == 0 else edges[1] if c == outer - 1 else own[c - 1]

    one_step(block(e, e_halo), block(f, f_halo), f_next, weight, weight_halo, band, band_halo, e_next, outer, False)


def first_step(meta, e, f, sst, got_a, got_b, bulk_map, absorb_map, weight, band):
    outer = weight.shape[0] + 2
    return pl.pallas_call(
        first_kernel,
        in_specs=[smem()] + [vmem()] * 9,
        out_specs=[vmem()] * 4,
        out_shape=[
            shape_of(outer, LEVELS, EDGE),
            shape_of(outer, 2 * LEVELS, EDGE, dtype=BF16),
            shape_of(2, 8, EDGE),
            shape_of(2, 2 * EDGE, 2 * EDGE, dtype=BF16),
        ],
        scratch_shapes=[
            pltpu.VMEM((2, LEVELS, EDGE), F32),
            pltpu.VMEM((2, 2 * LEVELS, EDGE), BF16),
            pltpu.VMEM((2, HALO_ROWS, EDGE), BF16),
            pltpu.VMEM((2, 8, EDGE), jnp.int32),
        ],
        compiler_params=params(),
        cost_estimate=cost(2**30, 2**22),
        name="first_step",
    )(meta, e, f, sst, got_a, got_b, bulk_map, absorb_map, weight, band)


def middle_kernel(e, f, weight, weight_halo, band, band_halo, e_next, f_next):
    one_step(e.__getitem__, f.__getitem__, f_next, weight, weight_halo, band, band_halo, e_next, e.shape[0], False)


def last_kernel(e, f, weight, weight_halo, band, band_halo, power, mixed, e_next):
    outer = e.shape[0]
    one_step(e.__getitem__, f.__getitem__, None, weight, weight_halo, band, band_halo, e_next, outer, True)
    for c in range(outer - 2):
        mixed[:, c * EDGE : (c + 1) * EDGE] = jnp.dot(
            power[...], e_next[c + 1], precision=HIGHEST, preferred_element_type=F32
        )


def middle_step(e, f, weight, weight_halo, band, band_halo):
    return pl.pallas_call(
        middle_kernel,
        in_specs=[vmem()] * 6,
        out_specs=[vmem()] * 2,
        out_shape=[shape_of(*e.shape), shape_of(*f.shape, dtype=BF16)],
        compiler_params=params(),
        cost_estimate=cost(2**30, 2**22),
        name="middle_step",
    )(e, f, weight, weight_halo, band, band_halo)


def last_step(e, f, weight, weight_halo, band, band_halo, power):
    return pl.pallas_call(
        last_kernel,
        in_specs=[vmem()] * 7,
        out_specs=vmem(),
        out_shape=shape_of(LEVELS, (e.shape[0] - 2) * EDGE),
        scratch_shapes=[pltpu.VMEM(e.shape, F32)],
        compiler_params=params(),
        cost_estimate=cost(2**30, 2**22),
        name="last_step",
    )(e, f, weight, weight_halo, band, band_halo, power)


def reverse_bits(value, count):
    return sum(((value >> k) & 1) << (count - 1 - k) for k in range(count))


def flux_kernel(meta, dest, live, spots, sst, weights, turned, mapped, rates, places, keep, send, flux, terms):
    blocks = mapped.shape[1] // EDGE
    tiles = terms.shape[0] // SLOTS
    bits = tiles.bit_length() - 1
    strip = meta[3]
    shape = (FIELDS, EDGE)
    lane = lanes(shape)
    terms[...] = jnp.zeros_like(terms)
    for g in range(blocks):
        at = slice(g * EDGE, (g + 1) * EDGE)
        warmth = jnp.zeros(shape, F32)
        held = []
        for b in (2 * g, 2 * g + 1):
            alive = lane < live[strip, 0, b]
            row = sst[pl.ds(dest[strip, 0, b] ^ (meta[1] * blocks), 1), :]
            row = jnp.where(alive, jnp.broadcast_to(row, shape), 0.0).astype(BF16)
            warmth = warmth + jnp.dot(row, turned[b], preferred_element_type=F32)
            held.append((b, alive))
        here = (mapped[:, at] - rates[:, at] * warmth).astype(BF16)
        flux[:, at] = here.astype(F32)
        for b, alive in held:
            part = jnp.dot(here, weights[b], preferred_element_type=F32)
            terms[spots[b]] = jnp.where(alive, part, 0.0)
    for t in range(tiles):
        i = reverse_bits(t, bits)
        out, i = (keep, i) if i < tiles // 2 else (send, i - tiles // 2)
        body = terms[t * SLOTS : (t + 1) * SLOTS].reshape(SLOTS * FIELDS, EDGE)
        out[i, 0 : SLOTS * FIELDS, :] = body.astype(BF16)
        out[i, SLOTS * FIELDS : PAYLOAD, :] = places[t]


def make_flux(meta, tiles, dest, live, spots, sst, weights, turned, mapped, rates, places):
    columns = mapped.shape[1]
    piece = shape_of(tiles // 2, PAYLOAD, EDGE, dtype=BF16)
    return pl.pallas_call(
        flux_kernel,
        in_specs=[smem()] * 4 + [vmem()] * 6,
        out_specs=[vmem()] * 3,
        out_shape=[piece, piece, shape_of(FIELDS, columns)],
        scratch_shapes=[pltpu.VMEM((tiles * SLOTS, FIELDS, EDGE), F32)],
        compiler_params=params(),
        cost_estimate=cost(2**30, 2**22),
        name="make_flux",
    )(meta, dest, live, spots, sst, weights, turned, mapped, rates, places)


def collect_kernel(near, far, out):
    body = SLOTS * FIELDS
    row = (lax.broadcasted_iota(jnp.int32, (EDGE, EDGE), 0) + 1).astype(F32)
    total = jnp.zeros((EDGE, EDGE), F32)
    for got in (near, far):
        for q in range(0, got.shape[0], 4):
            codes = got[q, body:PAYLOAD, :].astype(F32)
            for p in range(q + 1, q + 4):
                codes = codes + got[p, body:PAYLOAD, :].astype(F32)
            chosen = (row == jnp.broadcast_to(codes[0:1, :], (EDGE, EDGE))).astype(BF16)
            data = jnp.concatenate([got[p, 0:body, :] for p in range(q, q + 4)], axis=0)
            total = total + jnp.dot(chosen, data, preferred_element_type=F32)
    out[...] = total


def collect(near, far):
    return pl.pallas_call(
        collect_kernel,
        in_specs=[vmem()] * 2,
        out_specs=vmem(),
        out_shape=shape_of(EDGE, EDGE),
        compiler_params=params(),
        cost_estimate=cost(2**27, 2**18),
        name="collect",
    )(near, far)


def final_kernel(meta, part0, part1, mixed, absorb, rates, out, ocean, result, flux, done):
    blocks = mixed.shape[1] // EDGE
    active = (meta[0] == meta[2]).astype(F32)
    a0, a1, _ = three_parts(absorb[...] * active)
    absorbing = jnp.concatenate([a0, a0, a1, a1], axis=1).astype(BF16)
    for b in range(blocks):
        rows = slice(b * FIELDS, (b + 1) * FIELDS)
        flux[:, b * EDGE : (b + 1) * EDGE] = part0[rows, :] + part1[rows, :]
    copies = [pltpu.make_async_copy(flux, ocean, done.at[0])]
    copies[0].start()
    chunk = 2 * EDGE
    for k in range(blocks // 2):
        at = slice(k * chunk, (k + 1) * chunk)
        x0, x1, _ = three_parts(rates[:, at] * flux[:, at])
        drive = jnp.concatenate([x0, x1, x0, x1], axis=0).astype(BF16)
        result[:, at] = mixed[:, at] + jnp.dot(absorbing, drive, preferred_element_type=F32)
        copy = pltpu.make_async_copy(result.at[:, at], out.at[0, :, at], done.at[k + 1])
        copy.start()
        copies.append(copy)
    for copy in copies:
        copy.wait()


def finish(meta, part0, part1, mixed, absorb_map, rates):
    columns = mixed.shape[1]
    return pl.pallas_call(
        final_kernel,
        in_specs=[smem()] + [vmem()] * 5,
        out_specs=[anywhere()] * 2,
        out_shape=[shape_of(1, LEVELS, columns), shape_of(FIELDS, columns)],
        scratch_shapes=[
            pltpu.VMEM((LEVELS, columns), F32),
            pltpu.VMEM((FIELDS, columns), F32),
            pltpu.SemaphoreType.DMA((1 + columns // (2 * EDGE),)),
        ],
        compiler_params=params(),
        cost_estimate=cost(2**28, 2**21),
        name="finish",
    )(meta, part0, part1, mixed, absorb_map, rates)


def swap(x, axis, bit):
    return lax.ppermute(x, axis, [(i, i ^ bit) for i in range(lax.axis_size(axis))])


def shards(
    state,
    diffusivity,
    neighbours,
    vertical_mix,
    transfer_rates,
    bulk_map,
    absorb_map,
    block_dest,
    block_rows,
    block_weights,
):
    tiles, groups = lax.axis_size("tile"), lax.axis_size("mp")
    my_tile, my_group = lax.axis_index("tile"), lax.axis_index("mp")
    strip = jnp.minimum(my_group, block_dest.shape[1] - 1)
    meta = jnp.stack([my_group, my_tile, jnp.int32(groups - 1), strip]).astype(jnp.int32)
    neighbours = jnp.transpose(neighbours, (1, 0, 2))
    diffusivity = jnp.transpose(diffusivity, (1, 0, 2))
    dest = jnp.transpose(block_dest, (1, 0, 2))
    live = jnp.transpose(block_rows, (1, 0, 2))
    sst = surface(state)
    dest, live, spots, places, state, neighbours, diffusivity, bulk_map = load(
        meta, tiles, dest, live, state, neighbours, diffusivity, bulk_map
    )
    beside = lax.optimization_barrier
    bit = groups // 2
    while bit:
        other = swap(sst, "mp", bit)
        if bit > 1:
            other, state = beside((other, state))
        sst = jnp.where((my_group & bit) != 0, sst, other)
        bit //= 2
    weights, turned, rates, vertical_mix, absorb_map = load_weights(
        meta, block_weights, transfer_rates, vertical_mix, absorb_map.T
    )
    weight, band = make_band(neighbours, diffusivity)
    mapped = map_state(state, bulk_map)
    to_a, to_b, absorb_map = make_halo(meta, dest, live, state, weights, neighbours, diffusivity, rates, absorb_map)
    power = make_power(vertical_mix)
    to_a, power = beside((to_a, power))
    got_a = swap(to_a, "tile", 1)
    bit = 1
    while bit < tiles:
        other = swap(sst, "tile", bit)
        if bit == 1:
            other, weights = beside((other, weights))
        if bit == 2:
            other, band, to_b = beside((other, band, to_b))
        if bit == 4:
            other, mapped, power = beside((other, mapped, power))
        sst = jnp.concatenate([sst, other], axis=0)
        bit *= 2
    keep, send, flux = make_flux(meta, tiles, dest, live, spots, sst, weights, turned, mapped, rates, places)
    keep, send = keep[None], send[None]
    bit = 1
    while True:
        got = swap(send, "tile", bit)
        if bit == 1:
            e, f = force_state(meta, state, flux, absorb_map)
            to_b, e = beside((to_b, e))
            pairs = [(i, (i + (1 if i % 2 else -1)) % tiles) for i in range(tiles)]
            got_b = lax.ppermute(to_b, "tile", pairs)
            e, f, weight_halo, band_halo = first_step(
                meta, e, f, sst, got_a, got_b, bulk_map, absorb_map, weight, band
            )
        if bit == 2:
            got, e = beside((got, e))
            for _ in range(SUBSTEPS - 2):
                e, f = middle_step(e, f, weight, weight_halo, band, band_halo)
        if bit == 4:
            got, e = beside((got, e))
            mixed = last_step(e, f, weight, weight_halo, band, band_halo, power)
        bit *= 2
        if bit == tiles:
            break
        half = keep.shape[1] // 2
        send = jnp.concatenate([keep[:, half:], got[:, half:]], axis=0)
        keep = jnp.concatenate([keep[:, :half], got[:, :half]], axis=0)
    total = collect(keep[:, 0], got[:, 0])
    bit = groups // 2
    while bit > 1:
        other = swap(total, "mp", bit)
        if bit == groups // 2:
            other, mixed = beside((other, mixed))
        total = total + other
        bit //= 2
    return tuple(finish(meta, total, swap(total, "mp", 1), mixed, absorb_map, rates))


def solution(mesh):
    placed = (
        P("mp", None, "tile"),
        P("mp", None, "tile"),
        P("mp", None, "tile"),
        P("mp", None, None),
        P("mp", None, "tile"),
        P(),
        P(),
        P("tile", None, None),
        P("tile", None, None),
        P("tile", None, None, None, None),
    )
    return jax.shard_map(
        shards,
        mesh=mesh,
        in_specs=placed,
        out_specs=(P("mp", None, "tile"), P(None, "tile")),
        check_vma=False,
    )
```

```python
import jax
import jax.numpy as jnp
from jax import lax
from jax.experimental import pallas as pl
from jax.experimental.pallas import tpu as pltpu
from jax.sharding import PartitionSpec as P

HALO_WIDTH = 32
SUBSTEPS = 4
FIELDS = 8
EDGE = 128
LEVELS = 128
NEIGH = 6
SLOTS = 4
PAYLOAD = 48
HALO_ROWS = LEVELS + 2 * EDGE + 48
F32 = jnp.float32
BF16 = jnp.bfloat16
HIGHEST = lax.Precision.HIGHEST


def lanes(shape):
    return lax.broadcasted_iota(jnp.int32, shape, len(shape) - 1)


def split(x):
    high = x.astype(BF16)
    return high, (x - high.astype(F32)).astype(BF16)


def vmem():
    return pl.BlockSpec(memory_space=pltpu.VMEM)


def smem():
    return pl.BlockSpec(memory_space=pltpu.SMEM)


def params():
    return pltpu.CompilerParams(vmem_limit_bytes=10 * 2**20)


def shape_of(*shape, dtype=F32):
    return jax.ShapeDtypeStruct(shape, dtype)


def cost(flops, size):
    return pl.CostEstimate(flops=1024, bytes_accessed=1024, transcendentals=0)


def in_hbm(x):
    return pltpu.with_memory_space_constraint(x, pltpu.HBM)


def anywhere():
    return pl.BlockSpec(memory_space=pltpu.HBM)


def surface_kernel(state, sst, top, done):
    copy = pltpu.make_async_copy(state.at[0, 0:1, :], top, done)
    copy.start()
    copy.wait()
    for b in range(sst.shape[0]):
        row = top[0:1, b * EDGE : (b + 1) * EDGE]
        sst[b : b + 1, :] = row.astype(BF16).astype(F32)


def surface(state):
    columns = state.shape[2]
    return pl.pallas_call(
        surface_kernel,
        in_specs=[anywhere()],
        out_specs=vmem(),
        out_shape=shape_of(columns // EDGE, EDGE),
        scratch_shapes=[pltpu.VMEM((1, columns), F32), pltpu.SemaphoreType.DMA],
        compiler_params=params(),
        cost_estimate=cost(2**20, 2**16),
        name="surface",
    )(in_hbm(state))


def load_kernel(meta, dest_h, live_h, state, nbr, dif, bulk, dest, live, spots, places, state_v, nbr_v, dif_v, bulk_v, codes, count, done):
    tiles = places.shape[0]
    blocks = state_v.shape[1] // EDGE
    pairs = [(dest_h, dest), (live_h, live), (state.at[0], state_v), (nbr, nbr_v), (dif, dif_v), (bulk, bulk_v)]
    copies = [pltpu.make_async_copy(a, b, done.at[k]) for k, (a, b) in enumerate(pairs)]
    for copy in copies:
        copy.start()
    lane = lanes((8, EDGE))
    for t in range(tiles):
        count[t] = 0
    codes[...] = jnp.zeros_like(codes)
    active = meta[0] != meta[2]
    copies[0].wait()
    for b in range(spots.shape[0]):
        where = dest[meta[3], 0, b]
        owner, local = (where // blocks) ^ meta[1], where % blocks
        slot = count[owner]
        count[owner] = slot + 1
        spots[b] = owner * SLOTS + slot
        start = (owner % 4) * (SLOTS * FIELDS) + slot * FIELDS
        mine = (lane >= start) & (lane < start + FIELDS) & active
        codes[owner] = codes[owner] + jnp.where(mine, local * FIELDS + 1 + lane - start, 0)
    for t in range(tiles):
        place = codes[t].astype(F32)
        places[t] = jnp.concatenate([place, place], axis=0).astype(BF16)
    for copy in copies[1:]:
        copy.wait()


def load(meta, tiles, dest, live, state, neighbours, diffusivity, bulk_map):
    columns = state.shape[2]
    arrays = (dest, live, state, neighbours, diffusivity, bulk_map)
    return pl.pallas_call(
        load_kernel,
        in_specs=[smem()] + [anywhere()] * 6,
        out_specs=[smem()] * 3 + [vmem()] * 5,
        out_shape=[
            shape_of(*dest.shape, dtype=jnp.int32),
            shape_of(*live.shape, dtype=jnp.int32),
            shape_of(dest.shape[2], dtype=jnp.int32),
            shape_of(tiles, 16, EDGE, dtype=BF16),
            shape_of(LEVELS, columns),
            shape_of(NEIGH, 1, columns, dtype=jnp.int32),
            shape_of(NEIGH, 1, columns),
            shape_of(FIELDS, LEVELS),
        ],
        scratch_shapes=[
            pltpu.VMEM((tiles, 8, EDGE), jnp.int32),
            pltpu.SMEM((tiles,), jnp.int32),
            pltpu.SemaphoreType.DMA((6,)),
        ],
        compiler_params=params(),
        cost_estimate=cost(2**20, 2**21),
        name="load",
    )(meta, *(in_hbm(x) for x in arrays))


def weights_kernel(meta, weights, rates, vmix, absorb, weights_v, turned, rates_v, vmix_v, absorb_v, done):
    count = weights_v.shape[0]
    part = count // 8
    pairs = [(weights.at[0, meta[3], pl.ds(k * part, part)], weights_v.at[pl.ds(k * part, part)]) for k in range(8)]
    pairs += [(rates.at[0], rates_v), (vmix.at[0], vmix_v), (absorb, absorb_v)]
    copies = [pltpu.make_async_copy(a, b, done.at[k]) for k, (a, b) in enumerate(pairs)]
    for copy in copies:
        copy.start()
    for k in range(8):
        copies[k].wait()
        for b in range(k * part, (k + 1) * part):
            turned[b] = jnp.transpose(weights_v[b])
    for copy in copies[8:]:
        copy.wait()


def load_weights(meta, weights, rates, vertical_mix, absorb_map):
    columns, blocks = rates.shape[2], weights.shape[2]
    arrays = (weights, rates, vertical_mix, absorb_map)
    square = shape_of(blocks, EDGE, EDGE, dtype=BF16)
    return pl.pallas_call(
        weights_kernel,
        in_specs=[smem()] + [anywhere()] * 4,
        out_specs=[vmem()] * 5,
        out_shape=[square, square, shape_of(FIELDS, columns), shape_of(LEVELS, LEVELS), shape_of(FIELDS, LEVELS)],
        scratch_shapes=[pltpu.SemaphoreType.DMA((11,))],
        compiler_params=params(),
        cost_estimate=cost(2**20, 2**21),
        name="load_weights",
    )(meta, *(in_hbm(x) for x in arrays))


def halo_kernel(meta, dest, live, state, weights, nbr, dif, rates, absorb_t, out_a, out_b, absorb):
    blocks = state.shape[1] // EDGE
    strip = meta[3]

    def fill(out, e):
        b = 0 if e == 0 else blocks - 1
        at = slice(b * EDGE, (b + 1) * EDGE)
        out[0:LEVELS, :] = state[:, at].astype(BF16)
        base = LEVELS
        out[base : base + EDGE, :] = weights[2 * b]
        out[base + EDGE : base + 2 * EDGE, :] = weights[2 * b + 1]
        base += 2 * EDGE
        row = lax.broadcasted_iota(jnp.int32, (8, EDGE), 0)
        place = jnp.zeros((8, EDGE), jnp.int32)
        rate = jnp.zeros((8, EDGE), F32)
        for k in range(NEIGH):
            place = jnp.where(row == k, nbr[k, :, at] - (HALO_WIDTH + b * EDGE), place)
            rate = jnp.where(row == k, dif[k, :, at], rate)
        target = jnp.zeros((8, EDGE), jnp.int32)
        for h in range(2):
            block = dest[strip, 0, 2 * b + h]
            for k, value in enumerate((block // blocks, block % blocks, live[strip, 0, 2 * b + h])):
                target = jnp.where(row == 3 * h + k, value, target)
        high, low = split(rate)
        out[base : base + 16, :] = jnp.concatenate([place, target], axis=0).astype(F32).astype(BF16)
        out[base + 16 : base + 32, :] = jnp.concatenate([high.astype(F32), low.astype(F32)], axis=0).astype(BF16)
        high, low = split(rates[:, at])
        out[base + 32 : base + 48, :] = jnp.concatenate([high.astype(F32), low.astype(F32)], axis=0).astype(BF16)

    odd = meta[1] & 1

    @pl.when(odd == 0)
    def _():
        fill(out_a, 1)
        fill(out_b, 0)

    @pl.when(odd == 1)
    def _():
        fill(out_a, 0)
        fill(out_b, 1)

    tall = jnp.concatenate([absorb_t[...], jnp.zeros((LEVELS - FIELDS, LEVELS), F32)], axis=0)
    absorb[...] = jnp.transpose(tall)[:, 0:FIELDS]


def make_halo(meta, dest, live, state, weights, neighbours, diffusivity, rates, absorb_t):
    halo = shape_of(HALO_ROWS, EDGE, dtype=BF16)
    return pl.pallas_call(
        halo_kernel,
        in_specs=[smem()] * 3 + [vmem()] * 6,
        out_specs=[vmem()] * 3,
        out_shape=[halo, halo, shape_of(LEVELS, FIELDS)],
        compiler_params=params(),
        cost_estimate=cost(2**20, 2**18),
        name="make_halo",
    )(meta, dest, live, state, weights, neighbours, diffusivity, rates, absorb_t)


def map_kernel(state, bulk, mapped):
    b0, b1 = split(bulk[...])
    both = jnp.concatenate([b0.astype(F32), b1.astype(F32)], axis=0).astype(BF16)
    for c in range(state.shape[1] // EDGE):
        at = slice(c * EDGE, (c + 1) * EDGE)
        x0, x1 = split(state[:, at])
        high = jnp.dot(both, x0, preferred_element_type=F32)
        low = jnp.dot(both, x1, preferred_element_type=F32)
        mapped[:, at] = high[0:FIELDS] + (high[FIELDS:] + low[0:FIELDS])


def map_state(state, bulk_map):
    return pl.pallas_call(
        map_kernel,
        in_specs=[vmem()] * 2,
        out_specs=vmem(),
        out_shape=shape_of(FIELDS, state.shape[1]),
        compiler_params=params(),
        cost_estimate=cost(2**28, 2**20),
        name="map_state",
    )(state, bulk_map)


def build_band(index, weight, band, c):
    group = 8
    targets = []
    for k in range(NEIGH):
        j = index[c, k : k + 1, :]
        j = jnp.where((j >= 0) & (j < EDGE), j, EDGE + (j & (EDGE - 1)))
        targets.append((jnp.broadcast_to(j, (group, EDGE)), jnp.broadcast_to(weight[c, k : k + 1, :], (group, EDGE))))
    row = lax.broadcasted_iota(jnp.int32, (group, EDGE), 0)
    for start in range(0, 2 * EDGE, 16):
        if EDGE + HALO_WIDTH <= start < 2 * EDGE - HALO_WIDTH:
            high = jnp.zeros((16, EDGE), BF16)
            low = high
        else:
            parts = []
            for at in (start, start + group):
                total = jnp.zeros((group, EDGE), F32)
                for j, d in targets:
                    total = total + jnp.where(row == j - at, d, 0.0)
                parts.append(total)
            exact = jnp.concatenate(parts, axis=0)
            high = exact.astype(BF16)
            low = (exact - high.astype(F32)).astype(BF16)
        band[c, start : start + 16, 0:EDGE] = high
        band[c, start : start + 16, EDGE : 2 * EDGE] = low


def fill_terms(index, weight, c, j, d):
    index[c, 0:NEIGH, :] = j
    index[c, NEIGH:8, :] = jnp.zeros((2, EDGE), jnp.int32)
    weight[c, 0:NEIGH, :] = d
    weight[c, NEIGH:8, :] = jnp.broadcast_to(1.0 - jnp.sum(d, axis=0, keepdims=True), (2, EDGE))


def fill_terms(index, weight, c, j, d):
    index[c, 0:NEIGH, :] = j
    index[c, NEIGH:8, :] = jnp.zeros((2, EDGE), jnp.int32)
    weight[c, 0:NEIGH, :] = d
    weight[c, NEIGH:8, :] = jnp.broadcast_to(1.0 - jnp.sum(d, axis=0, keepdims=True), (2, EDGE))


def band_kernel(nbr, dif, weight, band, index):
    blocks = nbr.shape[2] // EDGE
    for c in range(blocks):
        at = slice(c * EDGE, (c + 1) * EDGE)
        j = jnp.concatenate([nbr[k, :, at] for k in range(NEIGH)], axis=0) - (HALO_WIDTH + c * EDGE)
        d = jnp.concatenate([dif[k, :, at] for k in range(NEIGH)], axis=0)
        fill_terms(index, weight, c, j, d)

    @pl.loop(0, blocks, unroll=2)
    def _(c):
        build_band(index, weight, band, c)


def make_band(neighbours, diffusivity):
    blocks = neighbours.shape[2] // EDGE
    return pl.pallas_call(
        band_kernel,
        in_specs=[vmem()] * 2,
        out_specs=[vmem()] * 2,
        out_shape=[shape_of(blocks, 8, EDGE), shape_of(blocks, 2 * EDGE, 2 * EDGE, dtype=BF16)],
        scratch_shapes=[pltpu.VMEM((blocks, 8, EDGE), jnp.int32)],
        compiler_params=params(),
        cost_estimate=cost(2**30, 2**22),
        name="make_band",
    )(neighbours, diffusivity)


def power_kernel(vmix, power):
    eye = (lax.broadcasted_iota(jnp.int32, (LEVELS, LEVELS), 0) == lanes((LEVELS, LEVELS))).astype(F32)
    total = eye + 0.25 * vmix[...]
    a = total
    for _ in range(SUBSTEPS - 1):
        total = jnp.dot(total, a, precision=HIGHEST, preferred_element_type=F32)
    power[...] = total


def make_power(vertical_mix):
    return pl.pallas_call(
        power_kernel,
        in_specs=[vmem()],
        out_specs=vmem(),
        out_shape=shape_of(LEVELS, LEVELS),
        compiler_params=params(),
        cost_estimate=cost(2**27, 2**18),
        name="make_power",
    )(vertical_mix)


def one_step(e, f, f_next, weight, weight_halo, band, band_halo, e_next, outer, final):
    low = lanes((2 * LEVELS, EDGE)) < EDGE // 2
    for c in range(1, outer - 1) if final else range(outer):
        edge = 0 if c == 0 else 1 if c == outer - 1 else None
        matrix = band[c - 1] if edge is None else band_halo[edge]
        keep = weight[c - 1, NEIGH : NEIGH + 1, :] if edge is None else weight_halo[edge, NEIGH : NEIGH + 1, :]
        near = jnp.concatenate([f(c), jnp.where(low, f(min(c + 1, outer - 1)), f(max(c - 1, 0)))], axis=1)
        product = jnp.dot(near, matrix, preferred_element_type=F32)
        x = keep * e(c) + (product[0:LEVELS, 0:EDGE] + (product[0:LEVELS, EDGE:] + product[LEVELS:, 0:EDGE]))
        e_next[c] = x
        if not final:
            f_next[c, 0:LEVELS, :], f_next[c, LEVELS : 2 * LEVELS, :] = split(x)


def three_parts(x):
    high = x.astype(BF16).astype(F32)
    middle = (x - high).astype(BF16).astype(F32)
    return high, middle, x - high - middle


def absorbing(meta, absorb):
    active = (meta[0] != meta[2]).astype(F32)
    return jnp.concatenate(three_parts(absorb[...] * active), axis=1).astype(BF16)


def absorbed(x, absorb, flux):
    return x - jnp.dot(absorb, jnp.concatenate([flux, flux, flux], axis=0).astype(BF16), preferred_element_type=F32)


def forced_kernel(meta, state, flux, absorb, e, f):
    matrix = absorbing(meta, absorb)
    for c in range(e.shape[0]):
        at = slice(c * EDGE, (c + 1) * EDGE)
        x = absorbed(state[:, at], matrix, flux[:, at])
        e[c] = x
        f[c, 0:LEVELS, :], f[c, LEVELS : 2 * LEVELS, :] = split(x)


def force_state(meta, state, flux, absorb_map):
    blocks = state.shape[1] // EDGE
    return pl.pallas_call(
        forced_kernel,
        in_specs=[smem()] + [vmem()] * 3,
        out_specs=[vmem()] * 2,
        out_shape=[shape_of(blocks, LEVELS, EDGE), shape_of(blocks, 2 * LEVELS, EDGE, dtype=BF16)],
        compiler_params=params(),
        cost_estimate=cost(2**28, 2**21),
        name="force_state",
    )(meta, state, flux, absorb_map)


def first_kernel(meta, e, f, sst, got_a, got_b, bulk, absorb, weight, band, e_next, f_next, weight_halo, band_halo, e_halo, f_halo, halo, index_halo):
    outer = weight.shape[0] + 2
    odd = meta[1] & 1

    @pl.when(odd == 0)
    def _():
        halo[0] = got_b[...]
        halo[1] = got_a[...]

    @pl.when(odd == 1)
    def _():
        halo[0] = got_a[...]
        halo[1] = got_b[...]

    matrix = absorbing(meta, absorb)
    surface_rows = sst[...].astype(BF16)
    lane = lanes((FIELDS, EDGE))
    for edge in range(2):
        base = LEVELS
        x = halo[edge, 0:LEVELS, :].astype(F32)
        blocks_held = [halo[edge, base + h * EDGE : base + (h + 1) * EDGE, :] for h in range(2)]
        base += 2 * EDGE
        small = halo[edge, base : base + 16, :].astype(F32)
        rate = halo[edge, base + 16 : base + 32, :].astype(F32)
        scale = halo[edge, base + 32 : base + 48, :].astype(F32)
        fill_terms(index_halo, weight_halo, edge, small[0:NEIGH].astype(jnp.int32), (rate[0:8] + rate[8:16])[0:NEIGH])
        build_band(index_halo, weight_halo, band_halo, edge)
        target = small[8:16].astype(jnp.int32)
        warmth = jnp.zeros((FIELDS, EDGE), F32)
        for h in range(2):
            owner, local, alive = target[3 * h : 3 * h + 1], target[3 * h + 1 : 3 * h + 2], target[3 * h + 2 : 3 * h + 3]
            spot = jnp.broadcast_to((owner ^ meta[1]) * (outer - 2) + local, lane.shape)
            row = jnp.zeros((FIELDS, EDGE), F32)
            for q in range(0, sst.shape[0], EDGE):
                chosen = (lane + q == spot).astype(BF16)
                row = row + jnp.dot(chosen, surface_rows[q : q + EDGE], preferred_element_type=F32)
            row = jnp.where(lane < jnp.broadcast_to(alive, lane.shape), row, 0.0).astype(BF16)
            warmth = warmth + lax.dot_general(
                row, blocks_held[h], (((1,), (1,)), ((), ())), preferred_element_type=F32
            )
        linear = jnp.dot(bulk[...], x, precision=HIGHEST, preferred_element_type=F32)
        here = (linear - (scale[0:8] + scale[8:16]) * warmth).astype(BF16).astype(F32)
        x = absorbed(x, matrix, here)
        e_halo[edge] = x
        f_halo[edge, 0:LEVELS, :], f_halo[edge, LEVELS : 2 * LEVELS, :] = split(x)

    def block(own, edges):
        return lambda c: edges[0] if c == 0 else edges[1] if c == outer - 1 else own[c - 1]

    one_step(block(e, e_halo), block(f, f_halo), f_next, weight, weight_halo, band, band_halo, e_next, outer, False)


def first_step(meta, e, f, sst, got_a, got_b, bulk_map, absorb_map, weight, band):
    outer = weight.shape[0] + 2
    return pl.pallas_call(
        first_kernel,
        in_specs=[smem()] + [vmem()] * 9,
        out_specs=[vmem()] * 4,
        out_shape=[
            shape_of(outer, LEVELS, EDGE),
            shape_of(outer, 2 * LEVELS, EDGE, dtype=BF16),
            shape_of(2, 8, EDGE),
            shape_of(2, 2 * EDGE, 2 * EDGE, dtype=BF16),
        ],
        scratch_shapes=[
            pltpu.VMEM((2, LEVELS, EDGE), F32),
            pltpu.VMEM((2, 2 * LEVELS, EDGE), BF16),
            pltpu.VMEM((2, HALO_ROWS, EDGE), BF16),
            pltpu.VMEM((2, 8, EDGE), jnp.int32),
        ],
        compiler_params=params(),
        cost_estimate=cost(2**30, 2**22),
        name="first_step",
    )(meta, e, f, sst, got_a, got_b, bulk_map, absorb_map, weight, band)


def middle_kernel(e, f, weight, weight_halo, band, band_halo, e_next, f_next):
    one_step(e.__getitem__, f.__getitem__, f_next, weight, weight_halo, band, band_halo, e_next, e.shape[0], False)


def last_kernel(e, f, weight, weight_halo, band, band_halo, power, mixed, e_next):
    outer = e.shape[0]
    one_step(e.__getitem__, f.__getitem__, None, weight, weight_halo, band, band_halo, e_next, outer, True)
    for c in range(outer - 2):
        mixed[:, c * EDGE : (c + 1) * EDGE] = jnp.dot(
            power[...], e_next[c + 1], precision=HIGHEST, preferred_element_type=F32
        )


def middle_step(e, f, weight, weight_halo, band, band_halo):
    return pl.pallas_call(
        middle_kernel,
        in_specs=[vmem()] * 6,
        out_specs=[vmem()] * 2,
        out_shape=[shape_of(*e.shape), shape_of(*f.shape, dtype=BF16)],
        compiler_params=params(),
        cost_estimate=cost(2**30, 2**22),
        name="middle_step",
    )(e, f, weight, weight_halo, band, band_halo)


def last_step(e, f, weight, weight_halo, band, band_halo, power):
    return pl.pallas_call(
        last_kernel,
        in_specs=[vmem()] * 7,
        out_specs=vmem(),
        out_shape=shape_of(LEVELS, (e.shape[0] - 2) * EDGE),
        scratch_shapes=[pltpu.VMEM(e.shape, F32)],
        compiler_params=params(),
        cost_estimate=cost(2**30, 2**22),
        name="last_step",
    )(e, f, weight, weight_halo, band, band_halo, power)


def reverse_bits(value, count):
    return sum(((value >> k) & 1) << (count - 1 - k) for k in range(count))


def flux_kernel(meta, dest, live, spots, sst, weights, turned, mapped, rates, places, keep, send, flux, terms):
    blocks = mapped.shape[1] // EDGE
    tiles = terms.shape[0] // SLOTS
    bits = tiles.bit_length() - 1
    strip = meta[3]
    shape = (FIELDS, EDGE)
    lane = lanes(shape)
    terms[...] = jnp.zeros_like(terms)
    for g in range(blocks):
        at = slice(g * EDGE, (g + 1) * EDGE)
        warmth = jnp.zeros(shape, F32)
        held = []
        for b in (2 * g, 2 * g + 1):
            alive = lane < live[strip, 0, b]
            row = sst[pl.ds(dest[strip, 0, b] ^ (meta[1] * blocks), 1), :]
            row = jnp.where(alive, jnp.broadcast_to(row, shape), 0.0).astype(BF16)
            warmth = warmth + jnp.dot(row, turned[b], preferred_element_type=F32)
            held.append((b, alive))
        here = (mapped[:, at] - rates[:, at] * warmth).astype(BF16)
        flux[:, at] = here.astype(F32)
        for b, alive in held:
            part = jnp.dot(here, weights[b], preferred_element_type=F32)
            terms[spots[b]] = jnp.where(alive, part, 0.0)
    for t in range(tiles):
        i = reverse_bits(t, bits)
        out, i = (keep, i) if i < tiles // 2 else (send, i - tiles // 2)
        body = terms[t * SLOTS : (t + 1) * SLOTS].reshape(SLOTS * FIELDS, EDGE)
        out[i, 0 : SLOTS * FIELDS, :] = body.astype(BF16)
        out[i, SLOTS * FIELDS : PAYLOAD, :] = places[t]


def make_flux(meta, tiles, dest, live, spots, sst, weights, turned, mapped, rates, places):
    columns = mapped.shape[1]
    piece = shape_of(tiles // 2, PAYLOAD, EDGE, dtype=BF16)
    return pl.pallas_call(
        flux_kernel,
        in_specs=[smem()] * 4 + [vmem()] * 6,
        out_specs=[vmem()] * 3,
        out_shape=[piece, piece, shape_of(FIELDS, columns)],
        scratch_shapes=[pltpu.VMEM((tiles * SLOTS, FIELDS, EDGE), F32)],
        compiler_params=params(),
        cost_estimate=cost(2**30, 2**22),
        name="make_flux",
    )(meta, dest, live, spots, sst, weights, turned, mapped, rates, places)


def collect_kernel(near, far, out):
    body = SLOTS * FIELDS
    row = (lax.broadcasted_iota(jnp.int32, (EDGE, EDGE), 0) + 1).astype(F32)
    total = jnp.zeros((EDGE, EDGE), F32)
    for got in (near, far):
        for q in range(0, got.shape[0], 4):
            codes = got[q, body:PAYLOAD, :].astype(F32)
            for p in range(q + 1, q + 4):
                codes = codes + got[p, body:PAYLOAD, :].astype(F32)
            chosen = (row == jnp.broadcast_to(codes[0:1, :], (EDGE, EDGE))).astype(BF16)
            data = jnp.concatenate([got[p, 0:body, :] for p in range(q, q + 4)], axis=0)
            total = total + jnp.dot(chosen, data, preferred_element_type=F32)
    out[...] = total


def collect(near, far):
    return pl.pallas_call(
        collect_kernel,
        in_specs=[vmem()] * 2,
        out_specs=vmem(),
        out_shape=shape_of(EDGE, EDGE),
        compiler_params=params(),
        cost_estimate=cost(2**27, 2**18),
        name="collect",
    )(near, far)


def final_kernel(meta, part0, part1, mixed, absorb, rates, out, ocean, result, flux, done):
    blocks = mixed.shape[1] // EDGE
    active = (meta[0] == meta[2]).astype(F32)
    a0, a1, _ = three_parts(absorb[...] * active)
    absorbing = jnp.concatenate([a0, a0, a1, a1], axis=1).astype(BF16)
    for b in range(blocks):
        rows = slice(b * FIELDS, (b + 1) * FIELDS)
        flux[:, b * EDGE : (b + 1) * EDGE] = part0[rows, :] + part1[rows, :]
    copies = [pltpu.make_async_copy(flux, ocean, done.at[0])]
    copies[0].start()
    chunk = 2 * EDGE
    for k in range(blocks // 2):
        at = slice(k * chunk, (k + 1) * chunk)
        x0, x1, _ = three_parts(rates[:, at] * flux[:, at])
        drive = jnp.concatenate([x0, x1, x0, x1], axis=0).astype(BF16)
        result[:, at] = mixed[:, at] + jnp.dot(absorbing, drive, preferred_element_type=F32)
        copy = pltpu.make_async_copy(result.at[:, at], out.at[0, :, at], done.at[k + 1])
        copy.start()
        copies.append(copy)
    for copy in copies:
        copy.wait()


def finish(meta, part0, part1, mixed, absorb_map, rates):
    columns = mixed.shape[1]
    return pl.pallas_call(
        final_kernel,
        in_specs=[smem()] + [vmem()] * 5,
        out_specs=[anywhere()] * 2,
        out_shape=[shape_of(1, LEVELS, columns), shape_of(FIELDS, columns)],
        scratch_shapes=[
            pltpu.VMEM((LEVELS, columns), F32),
            pltpu.VMEM((FIELDS, columns), F32),
            pltpu.SemaphoreType.DMA((1 + columns // (2 * EDGE),)),
        ],
        compiler_params=params(),
        cost_estimate=cost(2**28, 2**21),
        name="finish",
    )(meta, part0, part1, mixed, absorb_map, rates)


def swap(x, axis, bit):
    return lax.ppermute(x, axis, [(i, i ^ bit) for i in range(lax.axis_size(axis))])


def shards(
    state,
    diffusivity,
    neighbours,
    vertical_mix,
    transfer_rates,
    bulk_map,
    absorb_map,
    block_dest,
    block_rows,
    block_weights,
):
    tiles, groups = lax.axis_size("tile"), lax.axis_size("mp")
    my_tile, my_group = lax.axis_index("tile"), lax.axis_index("mp")
    strip = jnp.minimum(my_group, block_dest.shape[1] - 1)
    meta = jnp.stack([my_group, my_tile, jnp.int32(groups - 1), strip]).astype(jnp.int32)
    neighbours = jnp.transpose(neighbours, (1, 0, 2))
    diffusivity = jnp.transpose(diffusivity, (1, 0, 2))
    dest = jnp.transpose(block_dest, (1, 0, 2))
    live = jnp.transpose(block_rows, (1, 0, 2))
    sst = surface(state)
    dest, live, spots, places, state, neighbours, diffusivity, bulk_map = load(
        meta, tiles, dest, live, state, neighbours, diffusivity, bulk_map
    )
    beside = lax.optimization_barrier
    bit = groups // 2
    while bit:
        other = swap(sst, "mp", bit)
        if bit > 1:
            other, state = beside((other, state))
        sst = jnp.where((my_group & bit) != 0, sst, other)
        bit //= 2
    weights, turned, rates, vertical_mix, absorb_map = load_weights(
        meta, block_weights, transfer_rates, vertical_mix, absorb_map.T
    )
    weight, band = make_band(neighbours, diffusivity)
    to_a, to_b, absorb_map = make_halo(meta, dest, live, state, weights, neighbours, diffusivity, rates, absorb_map)
    bit = 1
    while bit < tiles:
        other = swap(sst, "tile", bit)
        if bit == 1:
            other, weights = beside((other, weights))
        if bit == 2:
            other, band, to_a, to_b, bulk_map = beside((other, band, to_a, to_b, bulk_map))
            mapped = map_state(state, bulk_map)
            to_a, mapped = beside((to_a, mapped))
            got_a = swap(to_a, "tile", 1)
            got_b = lax.ppermute(to_b, "tile", [(i, (i + (1 if i % 2 else -1)) % tiles) for i in range(tiles)])
        if bit == 4:
            other, mapped = beside((other, mapped))
        sst = jnp.concatenate([sst, other], axis=0)
        bit *= 2
    keep, send, flux = make_flux(meta, tiles, dest, live, spots, sst, weights, turned, mapped, rates, places)
    keep, send = keep[None], send[None]
    bit = 1
    while True:
        got = swap(send, "tile", bit)
        if bit == 1:
            e, f = force_state(meta, state, flux, absorb_map)
            got, e, got_a, got_b = beside((got, e, got_a, got_b))
            e, f, weight_halo, band_halo = first_step(
                meta, e, f, sst, got_a, got_b, bulk_map, absorb_map, weight, band
            )
        if bit == 2:
            got, e = beside((got, e))
            for _ in range(SUBSTEPS - 2):
                e, f = middle_step(e, f, weight, weight_halo, band, band_halo)
        if bit == 4:
            got, e = beside((got, e))
            vertical_mix, e = beside((vertical_mix, e))
            power = make_power(vertical_mix)
            mixed = last_step(e, f, weight, weight_halo, band, band_halo, power)
        bit *= 2
        if bit == tiles:
            break
        half = keep.shape[1] // 2
        send = jnp.concatenate([keep[:, half:], got[:, half:]], axis=0)
        keep = jnp.concatenate([keep[:, :half], got[:, :half]], axis=0)
    total = collect(keep[:, 0], got[:, 0])
    bit = groups // 2
    while bit > 1:
        other = swap(total, "mp", bit)
        if bit == groups // 2:
            other, mixed = beside((other, mixed))
        total = total + other
        bit //= 2
    return tuple(finish(meta, total, swap(total, "mp", 1), mixed, absorb_map, rates))


def solution(mesh):
    placed = (
        P("mp", None, "tile"),
        P("mp", None, "tile"),
        P("mp", None, "tile"),
        P("mp", None, None),
        P("mp", None, "tile"),
        P(),
        P(),
        P("tile", None, None),
        P("tile", None, None),
        P("tile", None, None, None, None),
    )
    return jax.shard_map(
        shards,
        mesh=mesh,
        in_specs=placed,
        out_specs=(P("mp", None, "tile"), P(None, "tile")),
        check_vma=False,
    )
```

```python
import jax
import jax.numpy as jnp
from jax import lax
from jax.experimental import pallas as pl
from jax.experimental.pallas import tpu as pltpu
from jax.sharding import PartitionSpec as P

HALO_WIDTH = 32
SUBSTEPS = 4
FIELDS = 8
EDGE = 128
LEVELS = 128
NEIGH = 6
SLOTS = 4
PAYLOAD = 48
HALO_ROWS = LEVELS + 2 * EDGE + 48
F32 = jnp.float32
BF16 = jnp.bfloat16
HIGHEST = lax.Precision.HIGHEST


def lanes(shape):
    return lax.broadcasted_iota(jnp.int32, shape, len(shape) - 1)


def split(x):
    high = x.astype(BF16)
    return high, (x - high.astype(F32)).astype(BF16)


def vmem():
    return pl.BlockSpec(memory_space=pltpu.VMEM)


def smem():
    return pl.BlockSpec(memory_space=pltpu.SMEM)


def params():
    return pltpu.CompilerParams(vmem_limit_bytes=10 * 2**20)


def shape_of(*shape, dtype=F32):
    return jax.ShapeDtypeStruct(shape, dtype)


def cost(flops, size):
    return pl.CostEstimate(flops=1024, bytes_accessed=1024, transcendentals=0)


def in_hbm(x):
    return pltpu.with_memory_space_constraint(x, pltpu.HBM)


def anywhere():
    return pl.BlockSpec(memory_space=pltpu.HBM)


def surface_kernel(state, sst, top, done):
    copy = pltpu.make_async_copy(state.at[0, 0:1, :], top, done)
    copy.start()
    copy.wait()
    for b in range(sst.shape[0]):
        row = top[0:1, b * EDGE : (b + 1) * EDGE]
        sst[b : b + 1, :] = row.astype(BF16).astype(F32)


def surface(state):
    columns = state.shape[2]
    return pl.pallas_call(
        surface_kernel,
        in_specs=[anywhere()],
        out_specs=vmem(),
        out_shape=shape_of(columns // EDGE, EDGE),
        scratch_shapes=[pltpu.VMEM((1, columns), F32), pltpu.SemaphoreType.DMA],
        compiler_params=params(),
        cost_estimate=cost(2**20, 2**16),
        name="surface",
    )(in_hbm(state))


def load_kernel(meta, dest_h, live_h, state, nbr, dif, bulk, dest, live, spots, places, state_v, nbr_v, dif_v, bulk_v, codes, count, done):
    tiles = places.shape[0]
    blocks = state_v.shape[1] // EDGE
    pairs = [(dest_h, dest), (live_h, live), (state.at[0], state_v), (nbr, nbr_v), (dif, dif_v), (bulk, bulk_v)]
    copies = [pltpu.make_async_copy(a, b, done.at[k]) for k, (a, b) in enumerate(pairs)]
    for copy in copies:
        copy.start()
    lane = lanes((8, EDGE))
    for t in range(tiles):
        count[t] = 0
    codes[...] = jnp.zeros_like(codes)
    active = meta[0] != meta[2]
    copies[0].wait()
    for b in range(spots.shape[0]):
        where = dest[meta[3], 0, b]
        owner, local = (where // blocks) ^ meta[1], where % blocks
        slot = count[owner]
        count[owner] = slot + 1
        spots[b] = owner * SLOTS + slot
        start = (owner % 4) * (SLOTS * FIELDS) + slot * FIELDS
        mine = (lane >= start) & (lane < start + FIELDS) & active
        codes[owner] = codes[owner] + jnp.where(mine, local * FIELDS + 1 + lane - start, 0)
    for t in range(tiles):
        place = codes[t].astype(F32)
        places[t] = jnp.concatenate([place, place], axis=0).astype(BF16)
    for copy in copies[1:]:
        copy.wait()


def load(meta, tiles, dest, live, state, neighbours, diffusivity, bulk_map):
    columns = state.shape[2]
    arrays = (dest, live, state, neighbours, diffusivity, bulk_map)
    return pl.pallas_call(
        load_kernel,
        in_specs=[smem()] + [anywhere()] * 6,
        out_specs=[smem()] * 3 + [vmem()] * 5,
        out_shape=[
            shape_of(*dest.shape, dtype=jnp.int32),
            shape_of(*live.shape, dtype=jnp.int32),
            shape_of(dest.shape[2], dtype=jnp.int32),
            shape_of(tiles, 16, EDGE, dtype=BF16),
            shape_of(LEVELS, columns),
            shape_of(NEIGH, 1, columns, dtype=jnp.int32),
            shape_of(NEIGH, 1, columns),
            shape_of(FIELDS, LEVELS),
        ],
        scratch_shapes=[
            pltpu.VMEM((tiles, 8, EDGE), jnp.int32),
            pltpu.SMEM((tiles,), jnp.int32),
            pltpu.SemaphoreType.DMA((6,)),
        ],
        compiler_params=params(),
        cost_estimate=cost(2**20, 2**21),
        name="load",
    )(meta, *(in_hbm(x) for x in arrays))


def weights_kernel(meta, weights, rates, vmix, absorb, weights_v, turned, rates_v, vmix_v, absorb_v, done):
    count = weights_v.shape[0]
    part = count // 8
    pairs = [(weights.at[0, meta[3], pl.ds(k * part, part)], weights_v.at[pl.ds(k * part, part)]) for k in range(8)]
    pairs += [(rates.at[0], rates_v), (vmix.at[0], vmix_v), (absorb, absorb_v)]
    copies = [pltpu.make_async_copy(a, b, done.at[k]) for k, (a, b) in enumerate(pairs)]
    for copy in copies:
        copy.start()
    for k in range(8):
        copies[k].wait()
        for b in range(k * part, (k + 1) * part):
            turned[b] = jnp.transpose(weights_v[b])
    for copy in copies[8:]:
        copy.wait()


def load_weights(meta, weights, rates, vertical_mix, absorb_map):
    columns, blocks = rates.shape[2], weights.shape[2]
    arrays = (weights, rates, vertical_mix, absorb_map)
    square = shape_of(blocks, EDGE, EDGE, dtype=BF16)
    return pl.pallas_call(
        weights_kernel,
        in_specs=[smem()] + [anywhere()] * 4,
        out_specs=[vmem()] * 5,
        out_shape=[square, square, shape_of(FIELDS, columns), shape_of(LEVELS, LEVELS), shape_of(FIELDS, LEVELS)],
        scratch_shapes=[pltpu.SemaphoreType.DMA((11,))],
        compiler_params=params(),
        cost_estimate=cost(2**20, 2**21),
        name="load_weights",
    )(meta, *(in_hbm(x) for x in arrays))


def halo_kernel(meta, dest, live, state, weights, nbr, dif, rates, absorb_t, out_a, out_b, absorb):
    blocks = state.shape[1] // EDGE
    strip = meta[3]

    def fill(out, e):
        b = 0 if e == 0 else blocks - 1
        at = slice(b * EDGE, (b + 1) * EDGE)
        out[0:LEVELS, :] = state[:, at].astype(BF16)
        base = LEVELS
        out[base : base + EDGE, :] = weights[2 * b]
        out[base + EDGE : base + 2 * EDGE, :] = weights[2 * b + 1]
        base += 2 * EDGE
        row = lax.broadcasted_iota(jnp.int32, (8, EDGE), 0)
        place = jnp.zeros((8, EDGE), jnp.int32)
        rate = jnp.zeros((8, EDGE), F32)
        for k in range(NEIGH):
            place = jnp.where(row == k, nbr[k, :, at] - (HALO_WIDTH + b * EDGE), place)
            rate = jnp.where(row == k, dif[k, :, at], rate)
        target = jnp.zeros((8, EDGE), jnp.int32)
        for h in range(2):
            block = dest[strip, 0, 2 * b + h]
            for k, value in enumerate((block // blocks, block % blocks, live[strip, 0, 2 * b + h])):
                target = jnp.where(row == 3 * h + k, value, target)
        high, low = split(rate)
        out[base : base + 16, :] = jnp.concatenate([place, target], axis=0).astype(F32).astype(BF16)
        out[base + 16 : base + 32, :] = jnp.concatenate([high.astype(F32), low.astype(F32)], axis=0).astype(BF16)
        high, low = split(rates[:, at])
        out[base + 32 : base + 48, :] = jnp.concatenate([high.astype(F32), low.astype(F32)], axis=0).astype(BF16)

    odd = meta[1] & 1

    @pl.when(odd == 0)
    def _():
        fill(out_a, 1)
        fill(out_b, 0)

    @pl.when(odd == 1)
    def _():
        fill(out_a, 0)
        fill(out_b, 1)

    tall = jnp.concatenate([absorb_t[...], jnp.zeros((LEVELS - FIELDS, LEVELS), F32)], axis=0)
    absorb[...] = jnp.transpose(tall)[:, 0:FIELDS]


def make_halo(meta, dest, live, state, weights, neighbours, diffusivity, rates, absorb_t):
    halo = shape_of(HALO_ROWS, EDGE, dtype=BF16)
    return pl.pallas_call(
        halo_kernel,
        in_specs=[smem()] * 3 + [vmem()] * 6,
        out_specs=[vmem()] * 3,
        out_shape=[halo, halo, shape_of(LEVELS, FIELDS)],
        compiler_params=params(),
        cost_estimate=cost(2**20, 2**18),
        name="make_halo",
    )(meta, dest, live, state, weights, neighbours, diffusivity, rates, absorb_t)


def map_kernel(state, bulk, mapped):
    b0, b1 = split(bulk[...])
    both = jnp.concatenate([b0.astype(F32), b1.astype(F32)], axis=0).astype(BF16)
    for c in range(state.shape[1] // EDGE):
        at = slice(c * EDGE, (c + 1) * EDGE)
        x0, x1 = split(state[:, at])
        high = jnp.dot(both, x0, preferred_element_type=F32)
        low = jnp.dot(both, x1, preferred_element_type=F32)
        mapped[:, at] = high[0:FIELDS] + (high[FIELDS:] + low[0:FIELDS])


def map_state(state, bulk_map):
    return pl.pallas_call(
        map_kernel,
        in_specs=[vmem()] * 2,
        out_specs=vmem(),
        out_shape=shape_of(FIELDS, state.shape[1]),
        compiler_params=params(),
        cost_estimate=cost(2**28, 2**20),
        name="map_state",
    )(state, bulk_map)


def build_band(index, weight, band, c):
    group = 8
    targets = []
    for k in range(NEIGH):
        j = index[c, k : k + 1, :]
        j = jnp.where((j >= 0) & (j < EDGE), j, EDGE + (j & (EDGE - 1)))
        targets.append((jnp.broadcast_to(j, (group, EDGE)), jnp.broadcast_to(weight[c, k : k + 1, :], (group, EDGE))))
    row = lax.broadcasted_iota(jnp.int32, (group, EDGE), 0)
    for start in range(0, 2 * EDGE, 16):
        if EDGE + HALO_WIDTH <= start < 2 * EDGE - HALO_WIDTH:
            high = jnp.zeros((16, EDGE), BF16)
            low = high
        else:
            parts = []
            for at in (start, start + group):
                total = jnp.zeros((group, EDGE), F32)
                for j, d in targets:
                    total = total + jnp.where(row == j - at, d, 0.0)
                parts.append(total)
            exact = jnp.concatenate(parts, axis=0)
            high = exact.astype(BF16)
            low = (exact - high.astype(F32)).astype(BF16)
        band[c, start : start + 16, 0:EDGE] = high
        band[c, start : start + 16, EDGE : 2 * EDGE] = low


def fill_terms(index, weight, c, j, d):
    index[c, 0:NEIGH, :] = j
    index[c, NEIGH:8, :] = jnp.zeros((2, EDGE), jnp.int32)
    weight[c, 0:NEIGH, :] = d
    weight[c, NEIGH:8, :] = jnp.broadcast_to(1.0 - jnp.sum(d, axis=0, keepdims=True), (2, EDGE))


def fill_terms(index, weight, c, j, d):
    index[c, 0:NEIGH, :] = j
    index[c, NEIGH:8, :] = jnp.zeros((2, EDGE), jnp.int32)
    weight[c, 0:NEIGH, :] = d
    weight[c, NEIGH:8, :] = jnp.broadcast_to(1.0 - jnp.sum(d, axis=0, keepdims=True), (2, EDGE))


def mixing_power(vmix):
    eye = (lax.broadcasted_iota(jnp.int32, (LEVELS, LEVELS), 0) == lanes((LEVELS, LEVELS))).astype(F32)
    total = eye + 0.25 * vmix
    a = total
    for _ in range(SUBSTEPS - 1):
        total = jnp.dot(total, a, precision=HIGHEST, preferred_element_type=F32)
    return total


def one_step(e, f, f_next, weight, weight_halo, band, band_halo, e_next, outer, final):
    low = lanes((2 * LEVELS, EDGE)) < EDGE // 2
    for c in range(1, outer - 1) if final else range(outer):
        edge = 0 if c == 0 else 1 if c == outer - 1 else None
        matrix = band[c - 1] if edge is None else band_halo[edge]
        keep = weight[c - 1, NEIGH : NEIGH + 1, :] if edge is None else weight_halo[edge, NEIGH : NEIGH + 1, :]
        near = jnp.concatenate([f(c), jnp.where(low, f(min(c + 1, outer - 1)), f(max(c - 1, 0)))], axis=1)
        product = jnp.dot(near, matrix, preferred_element_type=F32)
        x = keep * e(c) + (product[0:LEVELS, 0:EDGE] + (product[0:LEVELS, EDGE:] + product[LEVELS:, 0:EDGE]))
        e_next[c] = x
        if not final:
            f_next[c, 0:LEVELS, :], f_next[c, LEVELS : 2 * LEVELS, :] = split(x)


def three_parts(x):
    high = x.astype(BF16).astype(F32)
    middle = (x - high).astype(BF16).astype(F32)
    return high, middle, x - high - middle


def absorbing(meta, absorb):
    active = (meta[0] != meta[2]).astype(F32)
    return jnp.concatenate(three_parts(absorb[...] * active), axis=1).astype(BF16)


def absorbed(x, absorb, flux):
    return x - jnp.dot(absorb, jnp.concatenate([flux, flux, flux], axis=0).astype(BF16), preferred_element_type=F32)


def forced_kernel(meta, state, flux, absorb, nbr, dif, e, f, weight, band, index):
    matrix = absorbing(meta, absorb)
    for c in range(e.shape[0]):
        at = slice(c * EDGE, (c + 1) * EDGE)
        x = absorbed(state[:, at], matrix, flux[:, at])
        e[c] = x
        f[c, 0:LEVELS, :], f[c, LEVELS : 2 * LEVELS, :] = split(x)
        j = jnp.concatenate([nbr[k, :, at] for k in range(NEIGH)], axis=0) - (HALO_WIDTH + c * EDGE)
        d = jnp.concatenate([dif[k, :, at] for k in range(NEIGH)], axis=0)
        fill_terms(index, weight, c, j, d)

    @pl.loop(0, e.shape[0], unroll=2)
    def _(c):
        build_band(index, weight, band, c)


def force_state(meta, state, flux, absorb_map, neighbours, diffusivity):
    blocks = state.shape[1] // EDGE
    return pl.pallas_call(
        forced_kernel,
        in_specs=[smem()] + [vmem()] * 5,
        out_specs=[vmem()] * 4,
        out_shape=[
            shape_of(blocks, LEVELS, EDGE),
            shape_of(blocks, 2 * LEVELS, EDGE, dtype=BF16),
            shape_of(blocks, 8, EDGE),
            shape_of(blocks, 2 * EDGE, 2 * EDGE, dtype=BF16),
        ],
        scratch_shapes=[pltpu.VMEM((blocks, 8, EDGE), jnp.int32)],
        compiler_params=params(),
        cost_estimate=cost(2**28, 2**21),
        name="force_state",
    )(meta, state, flux, absorb_map, neighbours, diffusivity)


def first_kernel(meta, e, f, sst, got_a, got_b, bulk, absorb, weight, band, vmix, power, e_next, f_next, weight_halo, band_halo, e_halo, f_halo, halo, index_halo):
    outer = weight.shape[0] + 2
    odd = meta[1] & 1

    @pl.when(odd == 0)
    def _():
        halo[0] = got_b[...]
        halo[1] = got_a[...]

    @pl.when(odd == 1)
    def _():
        halo[0] = got_a[...]
        halo[1] = got_b[...]

    power[...] = mixing_power(vmix[...])
    matrix = absorbing(meta, absorb)
    surface_rows = sst[...].astype(BF16)
    lane = lanes((FIELDS, EDGE))
    for edge in range(2):
        base = LEVELS
        x = halo[edge, 0:LEVELS, :].astype(F32)
        blocks_held = [halo[edge, base + h * EDGE : base + (h + 1) * EDGE, :] for h in range(2)]
        base += 2 * EDGE
        small = halo[edge, base : base + 16, :].astype(F32)
        rate = halo[edge, base + 16 : base + 32, :].astype(F32)
        scale = halo[edge, base + 32 : base + 48, :].astype(F32)
        fill_terms(index_halo, weight_halo, edge, small[0:NEIGH].astype(jnp.int32), (rate[0:8] + rate[8:16])[0:NEIGH])
        build_band(index_halo, weight_halo, band_halo, edge)
        target = small[8:16].astype(jnp.int32)
        warmth = jnp.zeros((FIELDS, EDGE), F32)
        for h in range(2):
            owner, local, alive = target[3 * h : 3 * h + 1], target[3 * h + 1 : 3 * h + 2], target[3 * h + 2 : 3 * h + 3]
            spot = jnp.broadcast_to((owner ^ meta[1]) * (outer - 2) + local, lane.shape)
            row = jnp.zeros((FIELDS, EDGE), F32)
            for q in range(0, sst.shape[0], EDGE):
                chosen = (lane + q == spot).astype(BF16)
                row = row + jnp.dot(chosen, surface_rows[q : q + EDGE], preferred_element_type=F32)
            row = jnp.where(lane < jnp.broadcast_to(alive, lane.shape), row, 0.0).astype(BF16)
            warmth = warmth + lax.dot_general(
                row, blocks_held[h], (((1,), (1,)), ((), ())), preferred_element_type=F32
            )
        linear = jnp.dot(bulk[...], x, precision=HIGHEST, preferred_element_type=F32)
        here = (linear - (scale[0:8] + scale[8:16]) * warmth).astype(BF16).astype(F32)
        x = absorbed(x, matrix, here)
        e_halo[edge] = x
        f_halo[edge, 0:LEVELS, :], f_halo[edge, LEVELS : 2 * LEVELS, :] = split(x)

    def block(own, edges):
        return lambda c: edges[0] if c == 0 else edges[1] if c == outer - 1 else own[c - 1]

    one_step(block(e, e_halo), block(f, f_halo), f_next, weight, weight_halo, band, band_halo, e_next, outer, False)


def first_step(meta, e, f, sst, got_a, got_b, bulk_map, absorb_map, weight, band, vertical_mix):
    outer = weight.shape[0] + 2
    return pl.pallas_call(
        first_kernel,
        in_specs=[smem()] + [vmem()] * 10,
        out_specs=[vmem()] * 5,
        out_shape=[
            shape_of(LEVELS, LEVELS),
            shape_of(outer, LEVELS, EDGE),
            shape_of(outer, 2 * LEVELS, EDGE, dtype=BF16),
            shape_of(2, 8, EDGE),
            shape_of(2, 2 * EDGE, 2 * EDGE, dtype=BF16),
        ],
        scratch_shapes=[
            pltpu.VMEM((2, LEVELS, EDGE), F32),
            pltpu.VMEM((2, 2 * LEVELS, EDGE), BF16),
            pltpu.VMEM((2, HALO_ROWS, EDGE), BF16),
            pltpu.VMEM((2, 8, EDGE), jnp.int32),
        ],
        compiler_params=params(),
        cost_estimate=cost(2**30, 2**22),
        name="first_step",
    )(meta, e, f, sst, got_a, got_b, bulk_map, absorb_map, weight, band, vertical_mix)


def middle_kernel(e, f, weight, weight_halo, band, band_halo, e_next, f_next):
    one_step(e.__getitem__, f.__getitem__, f_next, weight, weight_halo, band, band_halo, e_next, e.shape[0], False)


def last_kernel(e, f, weight, weight_halo, band, band_halo, power, mixed, out, e_next, done):
    outer = e.shape[0]
    one_step(e.__getitem__, f.__getitem__, None, weight, weight_halo, band, band_halo, e_next, outer, True)
    copies = []
    for c in range(outer - 2):
        mixed[:, c * EDGE : (c + 1) * EDGE] = jnp.dot(
            power[...], e_next[c + 1], precision=HIGHEST, preferred_element_type=F32
        )
        if c % 2:
            at = slice((c - 1) * EDGE, (c + 1) * EDGE)
            copies.append(pltpu.make_async_copy(mixed.at[:, at], out.at[0, :, at], done.at[c // 2]))
            copies[-1].start()
    for copy in copies:
        copy.wait()


def middle_step(e, f, weight, weight_halo, band, band_halo):
    return pl.pallas_call(
        middle_kernel,
        in_specs=[vmem()] * 6,
        out_specs=[vmem()] * 2,
        out_shape=[shape_of(*e.shape), shape_of(*f.shape, dtype=BF16)],
        compiler_params=params(),
        cost_estimate=cost(2**30, 2**22),
        name="middle_step",
    )(e, f, weight, weight_halo, band, band_halo)


def last_step(e, f, weight, weight_halo, band, band_halo, power):
    columns = (e.shape[0] - 2) * EDGE
    return pl.pallas_call(
        last_kernel,
        in_specs=[vmem()] * 7,
        out_specs=[vmem(), anywhere()],
        out_shape=[shape_of(LEVELS, columns), shape_of(1, LEVELS, columns)],
        scratch_shapes=[pltpu.VMEM(e.shape, F32), pltpu.SemaphoreType.DMA((columns // (2 * EDGE),))],
        compiler_params=params(),
        cost_estimate=cost(2**30, 2**22),
        name="last_step",
    )(e, f, weight, weight_halo, band, band_halo, power)


def reverse_bits(value, count):
    return sum(((value >> k) & 1) << (count - 1 - k) for k in range(count))


def flux_kernel(meta, dest, live, spots, sst, weights, turned, mapped, rates, places, keep, send, flux, terms):
    blocks = mapped.shape[1] // EDGE
    tiles = terms.shape[0] // SLOTS
    bits = tiles.bit_length() - 1
    strip = meta[3]
    shape = (FIELDS, EDGE)
    lane = lanes(shape)
    terms[...] = jnp.zeros_like(terms)
    for g in range(blocks):
        at = slice(g * EDGE, (g + 1) * EDGE)
        warmth = jnp.zeros(shape, F32)
        held = []
        for b in (2 * g, 2 * g + 1):
            alive = lane < live[strip, 0, b]
            row = sst[pl.ds(dest[strip, 0, b] ^ (meta[1] * blocks), 1), :]
            row = jnp.where(alive, jnp.broadcast_to(row, shape), 0.0).astype(BF16)
            warmth = warmth + jnp.dot(row, turned[b], preferred_element_type=F32)
            held.append((b, alive))
        here = (mapped[:, at] - rates[:, at] * warmth).astype(BF16)
        flux[:, at] = here.astype(F32)
        for b, alive in held:
            part = jnp.dot(here, weights[b], preferred_element_type=F32)
            terms[spots[b]] = jnp.where(alive, part, 0.0)
    for t in range(tiles):
        i = reverse_bits(t, bits)
        out, i = (keep, i) if i < tiles // 2 else (send, i - tiles // 2)
        body = terms[t * SLOTS : (t + 1) * SLOTS].reshape(SLOTS * FIELDS, EDGE)
        out[i, 0 : SLOTS * FIELDS, :] = body.astype(BF16)
        out[i, SLOTS * FIELDS : PAYLOAD, :] = places[t]


def make_flux(meta, tiles, dest, live, spots, sst, weights, turned, mapped, rates, places):
    columns = mapped.shape[1]
    piece = shape_of(tiles // 2, PAYLOAD, EDGE, dtype=BF16)
    return pl.pallas_call(
        flux_kernel,
        in_specs=[smem()] * 4 + [vmem()] * 6,
        out_specs=[vmem()] * 3,
        out_shape=[piece, piece, shape_of(FIELDS, columns)],
        scratch_shapes=[pltpu.VMEM((tiles * SLOTS, FIELDS, EDGE), F32)],
        compiler_params=params(),
        cost_estimate=cost(2**30, 2**22),
        name="make_flux",
    )(meta, dest, live, spots, sst, weights, turned, mapped, rates, places)


def collect_kernel(near, far, out):
    body = SLOTS * FIELDS
    row = (lax.broadcasted_iota(jnp.int32, (EDGE, EDGE), 0) + 1).astype(F32)
    total = jnp.zeros((EDGE, EDGE), F32)
    for got in (near, far):
        for q in range(0, got.shape[0], 4):
            codes = got[q, body:PAYLOAD, :].astype(F32)
            for p in range(q + 1, q + 4):
                codes = codes + got[p, body:PAYLOAD, :].astype(F32)
            chosen = (row == jnp.broadcast_to(codes[0:1, :], (EDGE, EDGE))).astype(BF16)
            data = jnp.concatenate([got[p, 0:body, :] for p in range(q, q + 4)], axis=0)
            total = total + jnp.dot(chosen, data, preferred_element_type=F32)
    out[...] = total


def collect(near, far):
    return pl.pallas_call(
        collect_kernel,
        in_specs=[vmem()] * 2,
        out_specs=vmem(),
        out_shape=shape_of(EDGE, EDGE),
        compiler_params=params(),
        cost_estimate=cost(2**27, 2**18),
        name="collect",
    )(near, far)


def final_kernel(meta, part0, part1, mixed, absorb, rates, before, out, ocean, result, flux, done):
    blocks = mixed.shape[1] // EDGE
    for b in range(blocks):
        rows = slice(b * FIELDS, (b + 1) * FIELDS)
        flux[:, b * EDGE : (b + 1) * EDGE] = part0[rows, :] + part1[rows, :]
    whole = pltpu.make_async_copy(flux, ocean, done.at[0])
    whole.start()

    @pl.when(meta[0] == meta[2])
    def _():
        a0, a1, _ = three_parts(absorb[...])
        absorbing = jnp.concatenate([a0, a0, a1, a1], axis=1).astype(BF16)
        chunk = 2 * EDGE
        copies = []
        for k in range(blocks // 2):
            at = slice(k * chunk, (k + 1) * chunk)
            x0, x1, _ = three_parts(rates[:, at] * flux[:, at])
            drive = jnp.concatenate([x0, x1, x0, x1], axis=0).astype(BF16)
            result[:, at] = mixed[:, at] + jnp.dot(absorbing, drive, preferred_element_type=F32)
            copy = pltpu.make_async_copy(result.at[:, at], out.at[0, :, at], done.at[k + 1])
            copy.start()
            copies.append(copy)
        for copy in copies:
            copy.wait()

    whole.wait()


def finish(meta, part0, part1, mixed, absorb_map, rates, before):
    columns = mixed.shape[1]
    return pl.pallas_call(
        final_kernel,
        in_specs=[smem()] + [vmem()] * 5 + [anywhere()],
        out_specs=[anywhere()] * 2,
        out_shape=[shape_of(1, LEVELS, columns), shape_of(FIELDS, columns)],
        scratch_shapes=[
            pltpu.VMEM((LEVELS, columns), F32),
            pltpu.VMEM((FIELDS, columns), F32),
            pltpu.SemaphoreType.DMA((1 + columns // (2 * EDGE),)),
        ],
        input_output_aliases={6: 0},
        compiler_params=params(),
        cost_estimate=cost(2**28, 2**21),
        name="finish",
    )(meta, part0, part1, mixed, absorb_map, rates, before)


def swap(x, axis, bit):
    return lax.ppermute(x, axis, [(i, i ^ bit) for i in range(lax.axis_size(axis))])


def shards(
    state,
    diffusivity,
    neighbours,
    vertical_mix,
    transfer_rates,
    bulk_map,
    absorb_map,
    block_dest,
    block_rows,
    block_weights,
):
    tiles, groups = lax.axis_size("tile"), lax.axis_size("mp")
    my_tile, my_group = lax.axis_index("tile"), lax.axis_index("mp")
    strip = jnp.minimum(my_group, block_dest.shape[1] - 1)
    meta = jnp.stack([my_group, my_tile, jnp.int32(groups - 1), strip]).astype(jnp.int32)
    neighbours = jnp.transpose(neighbours, (1, 0, 2))
    diffusivity = jnp.transpose(diffusivity, (1, 0, 2))
    dest = jnp.transpose(block_dest, (1, 0, 2))
    live = jnp.transpose(block_rows, (1, 0, 2))
    sst = surface(state)
    dest, live, spots, places, state, neighbours, diffusivity, bulk_map = load(
        meta, tiles, dest, live, state, neighbours, diffusivity, bulk_map
    )
    beside = lax.optimization_barrier
    bit = groups // 2
    while bit:
        other = swap(sst, "mp", bit)
        if bit > 1:
            other, state = beside((other, state))
        sst = jnp.where((my_group & bit) != 0, sst, other)
        bit //= 2
    weights, turned, rates, vertical_mix, absorb_map = load_weights(
        meta, block_weights, transfer_rates, vertical_mix, absorb_map.T
    )
    mapped = map_state(state, bulk_map)
    to_a, to_b, absorb_map = make_halo(meta, dest, live, state, weights, neighbours, diffusivity, rates, absorb_map)
    bit = 1
    while bit < tiles:
        other = swap(sst, "tile", bit)
        if bit == 1:
            other, weights = beside((other, weights))
        if bit == 2:
            other, to_a, to_b, mapped = beside((other, to_a, to_b, mapped))
            got_a = swap(to_a, "tile", 1)
            got_b = lax.ppermute(to_b, "tile", [(i, (i + (1 if i % 2 else -1)) % tiles) for i in range(tiles)])
        if bit == 4:
            pass
        sst = jnp.concatenate([sst, other], axis=0)
        bit *= 2
    keep, send, flux = make_flux(meta, tiles, dest, live, spots, sst, weights, turned, mapped, rates, places)
    keep, send = keep[None], send[None]
    bit = 1
    while True:
        got = swap(send, "tile", bit)
        if bit == 1:
            e, f, weight, band = force_state(meta, state, flux, absorb_map, neighbours, diffusivity)
            got, e, got_a, got_b = beside((got, e, got_a, got_b))
            power, e, f, weight_halo, band_halo = first_step(
                meta, e, f, sst, got_a, got_b, bulk_map, absorb_map, weight, band, vertical_mix
            )
        if bit == 2:
            got, e = beside((got, e))
            for _ in range(SUBSTEPS - 2):
                e, f = middle_step(e, f, weight, weight_halo, band, band_halo)
        if bit == 4:
            got, e = beside((got, e))
            mixed, new_state = last_step(e, f, weight, weight_halo, band, band_halo, power)
        bit *= 2
        if bit == tiles:
            break
        half = keep.shape[1] // 2
        send = jnp.concatenate([keep[:, half:], got[:, half:]], axis=0)
        keep = jnp.concatenate([keep[:, :half], got[:, :half]], axis=0)
    total = collect(keep[:, 0], got[:, 0])
    total = total + swap(total, "mp", 1)
    bit = 2
    while True:
        other = swap(total, "mp", bit)
        if bit == 2:
            other, mixed = beside((other, mixed))
        bit *= 2
        if bit >= groups:
            break
        total = total + other
    return tuple(finish(meta, total, other, mixed, absorb_map, rates, new_state))


def solution(mesh):
    placed = (
        P("mp", None, "tile"),
        P("mp", None, "tile"),
        P("mp", None, "tile"),
        P("mp", None, None),
        P("mp", None, "tile"),
        P(),
        P(),
        P("tile", None, None),
        P("tile", None, None),
        P("tile", None, None, None, None),
    )
    return jax.shard_map(
        shards,
        mesh=mesh,
        in_specs=placed,
        out_specs=(P("mp", None, "tile"), P(None, "tile")),
        check_vma=False,
    )
```

```python
import jax
import jax.numpy as jnp
from jax import lax
from jax.experimental import pallas as pl
from jax.experimental.pallas import tpu as pltpu
from jax.sharding import PartitionSpec as P

HALO_WIDTH = 32
SUBSTEPS = 4
FIELDS = 8
EDGE = 128
LEVELS = 128
NEIGH = 6
SLOTS = 4
PAYLOAD = 48
HALO_ROWS = LEVELS + 2 * EDGE + 48
F32 = jnp.float32
BF16 = jnp.bfloat16
HIGHEST = lax.Precision.HIGHEST


def lanes(shape):
    return lax.broadcasted_iota(jnp.int32, shape, len(shape) - 1)


def split(x):
    high = x.astype(BF16)
    return high, (x - high.astype(F32)).astype(BF16)


def vmem():
    return pl.BlockSpec(memory_space=pltpu.VMEM)


def smem():
    return pl.BlockSpec(memory_space=pltpu.SMEM)


def params():
    return pltpu.CompilerParams(vmem_limit_bytes=10 * 2**20)


def shape_of(*shape, dtype=F32):
    return jax.ShapeDtypeStruct(shape, dtype)


def cost(flops, size):
    return pl.CostEstimate(flops=1024, bytes_accessed=1024, transcendentals=0)


def in_hbm(x):
    return pltpu.with_memory_space_constraint(x, pltpu.HBM)


def anywhere():
    return pl.BlockSpec(memory_space=pltpu.HBM)


def surface_kernel(state, sst, top, done):
    copy = pltpu.make_async_copy(state.at[0, 0:1, :], top, done)
    copy.start()
    copy.wait()
    for b in range(sst.shape[0]):
        row = top[0:1, b * EDGE : (b + 1) * EDGE]
        sst[b : b + 1, :] = row.astype(BF16).astype(F32)


def surface(state):
    columns = state.shape[2]
    return pl.pallas_call(
        surface_kernel,
        in_specs=[anywhere()],
        out_specs=vmem(),
        out_shape=shape_of(columns // EDGE, EDGE),
        scratch_shapes=[pltpu.VMEM((1, columns), F32), pltpu.SemaphoreType.DMA],
        compiler_params=params(),
        cost_estimate=cost(2**20, 2**16),
        name="surface",
    )(in_hbm(state))


def load_kernel(meta, dest_h, live_h, state, nbr, dif, bulk, dest, live, spots, places, state_v, nbr_v, dif_v, bulk_v, codes, count, done):
    tiles = places.shape[0]
    blocks = state_v.shape[1] // EDGE
    pairs = [(dest_h, dest), (live_h, live), (state.at[0], state_v), (nbr, nbr_v), (dif, dif_v), (bulk, bulk_v)]
    copies = [pltpu.make_async_copy(a, b, done.at[k]) for k, (a, b) in enumerate(pairs)]
    for copy in copies:
        copy.start()
    lane = lanes((8, EDGE))
    for t in range(tiles):
        count[t] = 0
    codes[...] = jnp.zeros_like(codes)
    active = meta[0] != meta[2]
    copies[0].wait()
    for b in range(spots.shape[0]):
        where = dest[meta[3], 0, b]
        owner, local = (where // blocks) ^ meta[1], where % blocks
        slot = count[owner]
        count[owner] = slot + 1
        spots[b] = owner * SLOTS + slot
        start = (owner % 4) * (SLOTS * FIELDS) + slot * FIELDS
        mine = (lane >= start) & (lane < start + FIELDS) & active
        codes[owner] = codes[owner] + jnp.where(mine, local * FIELDS + 1 + lane - start, 0)
    for t in range(tiles):
        place = codes[t].astype(F32)
        places[t] = jnp.concatenate([place, place], axis=0).astype(BF16)
    for copy in copies[1:]:
        copy.wait()


def load(meta, tiles, dest, live, state, neighbours, diffusivity, bulk_map):
    columns = state.shape[2]
    arrays = (dest, live, state, neighbours, diffusivity, bulk_map)
    return pl.pallas_call(
        load_kernel,
        in_specs=[smem()] + [anywhere()] * 6,
        out_specs=[smem()] * 3 + [vmem()] * 5,
        out_shape=[
            shape_of(*dest.shape, dtype=jnp.int32),
            shape_of(*live.shape, dtype=jnp.int32),
            shape_of(dest.shape[2], dtype=jnp.int32),
            shape_of(tiles, 16, EDGE, dtype=BF16),
            shape_of(LEVELS, columns),
            shape_of(NEIGH, 1, columns, dtype=jnp.int32),
            shape_of(NEIGH, 1, columns),
            shape_of(FIELDS, LEVELS),
        ],
        scratch_shapes=[
            pltpu.VMEM((tiles, 8, EDGE), jnp.int32),
            pltpu.SMEM((tiles,), jnp.int32),
            pltpu.SemaphoreType.DMA((6,)),
        ],
        compiler_params=params(),
        cost_estimate=cost(2**20, 2**21),
        name="load",
    )(meta, *(in_hbm(x) for x in arrays))


def weights_kernel(meta, weights, rates, vmix, absorb, weights_v, turned, rates_v, vmix_v, absorb_v, done):
    count = weights_v.shape[0]
    part = count // 8
    pairs = [(weights.at[0, meta[3], pl.ds(k * part, part)], weights_v.at[pl.ds(k * part, part)]) for k in range(8)]
    pairs += [(rates.at[0], rates_v), (vmix.at[0], vmix_v), (absorb, absorb_v)]
    copies = [pltpu.make_async_copy(a, b, done.at[k]) for k, (a, b) in enumerate(pairs)]
    for copy in copies:
        copy.start()
    for k in range(8):
        copies[k].wait()
        for b in range(k * part, (k + 1) * part):
            turned[b] = jnp.transpose(weights_v[b])
    for copy in copies[8:]:
        copy.wait()


def load_weights(meta, weights, rates, vertical_mix, absorb_map):
    columns, blocks = rates.shape[2], weights.shape[2]
    arrays = (weights, rates, vertical_mix, absorb_map)
    square = shape_of(blocks, EDGE, EDGE, dtype=BF16)
    return pl.pallas_call(
        weights_kernel,
        in_specs=[smem()] + [anywhere()] * 4,
        out_specs=[vmem()] * 5,
        out_shape=[square, square, shape_of(FIELDS, columns), shape_of(LEVELS, LEVELS), shape_of(FIELDS, LEVELS)],
        scratch_shapes=[pltpu.SemaphoreType.DMA((11,))],
        compiler_params=params(),
        cost_estimate=cost(2**20, 2**21),
        name="load_weights",
    )(meta, *(in_hbm(x) for x in arrays))


def halo_kernel(meta, dest, live, state, weights, nbr, dif, rates, absorb_t, out_a, out_b, absorb):
    blocks = state.shape[1] // EDGE
    strip = meta[3]

    def fill(out, e):
        b = 0 if e == 0 else blocks - 1
        at = slice(b * EDGE, (b + 1) * EDGE)
        out[0:LEVELS, :] = state[:, at].astype(BF16)
        base = LEVELS
        out[base : base + EDGE, :] = weights[2 * b]
        out[base + EDGE : base + 2 * EDGE, :] = weights[2 * b + 1]
        base += 2 * EDGE
        row = lax.broadcasted_iota(jnp.int32, (8, EDGE), 0)
        place = jnp.zeros((8, EDGE), jnp.int32)
        rate = jnp.zeros((8, EDGE), F32)
        for k in range(NEIGH):
            place = jnp.where(row == k, nbr[k, :, at] - (HALO_WIDTH + b * EDGE), place)
            rate = jnp.where(row == k, dif[k, :, at], rate)
        target = jnp.zeros((8, EDGE), jnp.int32)
        for h in range(2):
            block = dest[strip, 0, 2 * b + h]
            for k, value in enumerate((block // blocks, block % blocks, live[strip, 0, 2 * b + h])):
                target = jnp.where(row == 3 * h + k, value, target)
        high, low = split(rate)
        out[base : base + 16, :] = jnp.concatenate([place, target], axis=0).astype(F32).astype(BF16)
        out[base + 16 : base + 32, :] = jnp.concatenate([high.astype(F32), low.astype(F32)], axis=0).astype(BF16)
        high, low = split(rates[:, at])
        out[base + 32 : base + 48, :] = jnp.concatenate([high.astype(F32), low.astype(F32)], axis=0).astype(BF16)

    odd = meta[1] & 1

    @pl.when(odd == 0)
    def _():
        fill(out_a, 1)
        fill(out_b, 0)

    @pl.when(odd == 1)
    def _():
        fill(out_a, 0)
        fill(out_b, 1)

    tall = jnp.concatenate([absorb_t[...], jnp.zeros((LEVELS - FIELDS, LEVELS), F32)], axis=0)
    absorb[...] = jnp.transpose(tall)[:, 0:FIELDS]


def make_halo(meta, dest, live, state, weights, neighbours, diffusivity, rates, absorb_t):
    halo = shape_of(HALO_ROWS, EDGE, dtype=BF16)
    return pl.pallas_call(
        halo_kernel,
        in_specs=[smem()] * 3 + [vmem()] * 6,
        out_specs=[vmem()] * 3,
        out_shape=[halo, halo, shape_of(LEVELS, FIELDS)],
        compiler_params=params(),
        cost_estimate=cost(2**20, 2**18),
        name="make_halo",
    )(meta, dest, live, state, weights, neighbours, diffusivity, rates, absorb_t)


def map_kernel(state, bulk, mapped):
    b0, b1 = split(bulk[...])
    both = jnp.concatenate([b0.astype(F32), b1.astype(F32)], axis=0).astype(BF16)
    for c in range(state.shape[1] // EDGE):
        at = slice(c * EDGE, (c + 1) * EDGE)
        x0, x1 = split(state[:, at])
        high = jnp.dot(both, x0, preferred_element_type=F32)
        low = jnp.dot(both, x1, preferred_element_type=F32)
        mapped[:, at] = high[0:FIELDS] + (high[FIELDS:] + low[0:FIELDS])


def map_state(state, bulk_map):
    return pl.pallas_call(
        map_kernel,
        in_specs=[vmem()] * 2,
        out_specs=vmem(),
        out_shape=shape_of(FIELDS, state.shape[1]),
        compiler_params=params(),
        cost_estimate=cost(2**28, 2**20),
        name="map_state",
    )(state, bulk_map)


def build_band(index, weight, band, c):
    group = 8
    targets = []
    for k in range(NEIGH):
        j = index[c, k : k + 1, :]
        j = jnp.where((j >= 0) & (j < EDGE), j, EDGE + (j & (EDGE - 1)))
        targets.append((jnp.broadcast_to(j, (group, EDGE)), jnp.broadcast_to(weight[c, k : k + 1, :], (group, EDGE))))
    row = lax.broadcasted_iota(jnp.int32, (group, EDGE), 0)
    for start in range(0, 2 * EDGE, 16):
        if EDGE + HALO_WIDTH <= start < 2 * EDGE - HALO_WIDTH:
            high = jnp.zeros((16, EDGE), BF16)
            low = high
        else:
            parts = []
            for at in (start, start + group):
                total = jnp.zeros((group, EDGE), F32)
                for j, d in targets:
                    total = total + jnp.where(row == j - at, d, 0.0)
                parts.append(total)
            exact = jnp.concatenate(parts, axis=0)
            high = exact.astype(BF16)
            low = (exact - high.astype(F32)).astype(BF16)
        band[c, start : start + 16, 0:EDGE] = high
        band[c, start : start + 16, EDGE : 2 * EDGE] = low


def fill_terms(index, weight, c, j, d):
    index[c, 0:NEIGH, :] = j
    index[c, NEIGH:8, :] = jnp.zeros((2, EDGE), jnp.int32)
    weight[c, 0:NEIGH, :] = d
    weight[c, NEIGH:8, :] = jnp.broadcast_to(1.0 - jnp.sum(d, axis=0, keepdims=True), (2, EDGE))


def fill_terms(index, weight, c, j, d):
    index[c, 0:NEIGH, :] = j
    index[c, NEIGH:8, :] = jnp.zeros((2, EDGE), jnp.int32)
    weight[c, 0:NEIGH, :] = d
    weight[c, NEIGH:8, :] = jnp.broadcast_to(1.0 - jnp.sum(d, axis=0, keepdims=True), (2, EDGE))


def mixing_power(vmix):
    eye = (lax.broadcasted_iota(jnp.int32, (LEVELS, LEVELS), 0) == lanes((LEVELS, LEVELS))).astype(F32)
    total = eye + 0.25 * vmix
    a = total
    for _ in range(SUBSTEPS - 1):
        total = jnp.dot(total, a, precision=HIGHEST, preferred_element_type=F32)
    return total


def one_step(e, f, f_next, weight, weight_halo, band, band_halo, e_next, outer, final):
    low = lanes((2 * LEVELS, EDGE)) < EDGE // 2
    for c in range(1, outer - 1) if final else range(outer):
        edge = 0 if c == 0 else 1 if c == outer - 1 else None
        matrix = band[c - 1] if edge is None else band_halo[edge]
        keep = weight[c - 1, NEIGH : NEIGH + 1, :] if edge is None else weight_halo[edge, NEIGH : NEIGH + 1, :]
        near = jnp.concatenate([f(c), jnp.where(low, f(min(c + 1, outer - 1)), f(max(c - 1, 0)))], axis=1)
        product = jnp.dot(near, matrix, preferred_element_type=F32)
        x = keep * e(c) + (product[0:LEVELS, 0:EDGE] + (product[0:LEVELS, EDGE:] + product[LEVELS:, 0:EDGE]))
        e_next[c] = x
        if not final:
            f_next[c, 0:LEVELS, :], f_next[c, LEVELS : 2 * LEVELS, :] = split(x)


def three_parts(x):
    high = x.astype(BF16).astype(F32)
    middle = (x - high).astype(BF16).astype(F32)
    return high, middle, x - high - middle


def absorbing(meta, absorb):
    active = (meta[0] != meta[2]).astype(F32)
    return jnp.concatenate(three_parts(absorb[...] * active), axis=1).astype(BF16)


def absorbed(x, absorb, flux):
    return x - jnp.dot(absorb, jnp.concatenate([flux, flux, flux], axis=0).astype(BF16), preferred_element_type=F32)


def forced_kernel(meta, state, flux, absorb, nbr, dif, e, f, weight, band, index):
    matrix = absorbing(meta, absorb)
    for c in range(e.shape[0]):
        at = slice(c * EDGE, (c + 1) * EDGE)
        x = absorbed(state[:, at], matrix, flux[:, at])
        e[c] = x
        f[c, 0:LEVELS, :], f[c, LEVELS : 2 * LEVELS, :] = split(x)
        j = jnp.concatenate([nbr[k, :, at] for k in range(NEIGH)], axis=0) - (HALO_WIDTH + c * EDGE)
        d = jnp.concatenate([dif[k, :, at] for k in range(NEIGH)], axis=0)
        fill_terms(index, weight, c, j, d)

    @pl.loop(0, e.shape[0], unroll=2)
    def _(c):
        build_band(index, weight, band, c)


def force_state(meta, state, flux, absorb_map, neighbours, diffusivity):
    blocks = state.shape[1] // EDGE
    return pl.pallas_call(
        forced_kernel,
        in_specs=[smem()] + [vmem()] * 5,
        out_specs=[vmem()] * 4,
        out_shape=[
            shape_of(blocks, LEVELS, EDGE),
            shape_of(blocks, 2 * LEVELS, EDGE, dtype=BF16),
            shape_of(blocks, 8, EDGE),
            shape_of(blocks, 2 * EDGE, 2 * EDGE, dtype=BF16),
        ],
        scratch_shapes=[pltpu.VMEM((blocks, 8, EDGE), jnp.int32)],
        compiler_params=params(),
        cost_estimate=cost(2**28, 2**21),
        name="force_state",
    )(meta, state, flux, absorb_map, neighbours, diffusivity)


def first_kernel(meta, e, f, sst, got_a, got_b, bulk, absorb, weight, band, vmix, power, e_next, f_next, weight_halo, band_halo, e_halo, f_halo, halo, index_halo):
    outer = weight.shape[0] + 2
    odd = meta[1] & 1

    @pl.when(odd == 0)
    def _():
        halo[0] = got_b[...]
        halo[1] = got_a[...]

    @pl.when(odd == 1)
    def _():
        halo[0] = got_a[...]
        halo[1] = got_b[...]

    power[...] = mixing_power(vmix[...])
    matrix = absorbing(meta, absorb)
    surface_rows = sst[...].astype(BF16)
    lane = lanes((FIELDS, EDGE))
    for edge in range(2):
        base = LEVELS
        x = halo[edge, 0:LEVELS, :].astype(F32)
        blocks_held = [halo[edge, base + h * EDGE : base + (h + 1) * EDGE, :] for h in range(2)]
        base += 2 * EDGE
        small = halo[edge, base : base + 16, :].astype(F32)
        rate = halo[edge, base + 16 : base + 32, :].astype(F32)
        scale = halo[edge, base + 32 : base + 48, :].astype(F32)
        fill_terms(index_halo, weight_halo, edge, small[0:NEIGH].astype(jnp.int32), (rate[0:8] + rate[8:16])[0:NEIGH])
        build_band(index_halo, weight_halo, band_halo, edge)
        target = small[8:16].astype(jnp.int32)
        warmth = jnp.zeros((FIELDS, EDGE), F32)
        for h in range(2):
            owner, local, alive = target[3 * h : 3 * h + 1], target[3 * h + 1 : 3 * h + 2], target[3 * h + 2 : 3 * h + 3]
            spot = jnp.broadcast_to((owner ^ meta[1]) * (outer - 2) + local, lane.shape)
            row = jnp.zeros((FIELDS, EDGE), F32)
            for q in range(0, sst.shape[0], EDGE):
                chosen = (lane + q == spot).astype(BF16)
                row = row + jnp.dot(chosen, surface_rows[q : q + EDGE], preferred_element_type=F32)
            row = jnp.where(lane < jnp.broadcast_to(alive, lane.shape), row, 0.0).astype(BF16)
            warmth = warmth + lax.dot_general(
                row, blocks_held[h], (((1,), (1,)), ((), ())), preferred_element_type=F32
            )
        linear = jnp.dot(bulk[...], x, precision=HIGHEST, preferred_element_type=F32)
        here = (linear - (scale[0:8] + scale[8:16]) * warmth).astype(BF16).astype(F32)
        x = absorbed(x, matrix, here)
        e_halo[edge] = x
        f_halo[edge, 0:LEVELS, :], f_halo[edge, LEVELS : 2 * LEVELS, :] = split(x)

    def block(own, edges):
        return lambda c: edges[0] if c == 0 else edges[1] if c == outer - 1 else own[c - 1]

    one_step(block(e, e_halo), block(f, f_halo), f_next, weight, weight_halo, band, band_halo, e_next, outer, False)


def first_step(meta, e, f, sst, got_a, got_b, bulk_map, absorb_map, weight, band, vertical_mix):
    outer = weight.shape[0] + 2
    return pl.pallas_call(
        first_kernel,
        in_specs=[smem()] + [vmem()] * 10,
        out_specs=[vmem()] * 5,
        out_shape=[
            shape_of(LEVELS, LEVELS),
            shape_of(outer, LEVELS, EDGE),
            shape_of(outer, 2 * LEVELS, EDGE, dtype=BF16),
            shape_of(2, 8, EDGE),
            shape_of(2, 2 * EDGE, 2 * EDGE, dtype=BF16),
        ],
        scratch_shapes=[
            pltpu.VMEM((2, LEVELS, EDGE), F32),
            pltpu.VMEM((2, 2 * LEVELS, EDGE), BF16),
            pltpu.VMEM((2, HALO_ROWS, EDGE), BF16),
            pltpu.VMEM((2, 8, EDGE), jnp.int32),
        ],
        compiler_params=params(),
        cost_estimate=cost(2**30, 2**22),
        name="first_step",
    )(meta, e, f, sst, got_a, got_b, bulk_map, absorb_map, weight, band, vertical_mix)


def middle_kernel(e, f, weight, weight_halo, band, band_halo, e_next, f_next):
    one_step(e.__getitem__, f.__getitem__, f_next, weight, weight_halo, band, band_halo, e_next, e.shape[0], False)


def last_kernel(e, f, weight, weight_halo, band, band_halo, power, mixed, out, e_next, done):
    outer = e.shape[0]
    one_step(e.__getitem__, f.__getitem__, None, weight, weight_halo, band, band_halo, e_next, outer, True)
    copies = []
    for c in range(outer - 2):
        mixed[:, c * EDGE : (c + 1) * EDGE] = jnp.dot(
            power[...], e_next[c + 1], precision=HIGHEST, preferred_element_type=F32
        )
        if c % 2:
            at = slice((c - 1) * EDGE, (c + 1) * EDGE)
            copies.append(pltpu.make_async_copy(mixed.at[:, at], out.at[0, :, at], done.at[c // 2]))
            copies[-1].start()
    for copy in copies:
        copy.wait()


def middle_step(e, f, weight, weight_halo, band, band_halo):
    return pl.pallas_call(
        middle_kernel,
        in_specs=[vmem()] * 6,
        out_specs=[vmem()] * 2,
        out_shape=[shape_of(*e.shape), shape_of(*f.shape, dtype=BF16)],
        compiler_params=params(),
        cost_estimate=cost(2**30, 2**22),
        name="middle_step",
    )(e, f, weight, weight_halo, band, band_halo)


def last_step(e, f, weight, weight_halo, band, band_halo, power):
    columns = (e.shape[0] - 2) * EDGE
    return pl.pallas_call(
        last_kernel,
        in_specs=[vmem()] * 7,
        out_specs=[vmem(), anywhere()],
        out_shape=[shape_of(LEVELS, columns), shape_of(1, LEVELS, columns)],
        scratch_shapes=[pltpu.VMEM(e.shape, F32), pltpu.SemaphoreType.DMA((columns // (2 * EDGE),))],
        compiler_params=params(),
        cost_estimate=cost(2**30, 2**22),
        name="last_step",
    )(e, f, weight, weight_halo, band, band_halo, power)


def reverse_bits(value, count):
    return sum(((value >> k) & 1) << (count - 1 - k) for k in range(count))


def flux_kernel(meta, dest, live, spots, sst, weights, turned, mapped, rates, places, keep, send, flux, terms):
    blocks = mapped.shape[1] // EDGE
    tiles = terms.shape[0] // SLOTS
    bits = tiles.bit_length() - 1
    strip = meta[3]
    shape = (FIELDS, EDGE)
    lane = lanes(shape)
    terms[...] = jnp.zeros_like(terms)
    for g in range(blocks):
        at = slice(g * EDGE, (g + 1) * EDGE)
        warmth = jnp.zeros(shape, F32)
        held = []
        for b in (2 * g, 2 * g + 1):
            alive = lane < live[strip, 0, b]
            row = sst[pl.ds(dest[strip, 0, b] ^ (meta[1] * blocks), 1), :]
            row = jnp.where(alive, jnp.broadcast_to(row, shape), 0.0).astype(BF16)
            warmth = warmth + jnp.dot(row, turned[b], preferred_element_type=F32)
            held.append((b, alive))
        here = (mapped[:, at] - rates[:, at] * warmth).astype(BF16)
        flux[:, at] = here.astype(F32)
        for b, alive in held:
            part = jnp.dot(here, weights[b], preferred_element_type=F32)
            terms[spots[b]] = jnp.where(alive, part, 0.0)
    for t in range(tiles):
        i = reverse_bits(t, bits)
        out, i = (keep, i) if i < tiles // 2 else (send, i - tiles // 2)
        body = terms[t * SLOTS : (t + 1) * SLOTS].reshape(SLOTS * FIELDS, EDGE)
        out[i, 0 : SLOTS * FIELDS, :] = body.astype(BF16)
        out[i, SLOTS * FIELDS : PAYLOAD, :] = places[t]


def make_flux(meta, tiles, dest, live, spots, sst, weights, turned, mapped, rates, places):
    columns = mapped.shape[1]
    piece = shape_of(tiles // 2, PAYLOAD, EDGE, dtype=BF16)
    return pl.pallas_call(
        flux_kernel,
        in_specs=[smem()] * 4 + [vmem()] * 6,
        out_specs=[vmem()] * 3,
        out_shape=[piece, piece, shape_of(FIELDS, columns)],
        scratch_shapes=[pltpu.VMEM((tiles * SLOTS, FIELDS, EDGE), F32)],
        compiler_params=params(),
        cost_estimate=cost(2**30, 2**22),
        name="make_flux",
    )(meta, dest, live, spots, sst, weights, turned, mapped, rates, places)


def collect_kernel(near, far, out):
    body = SLOTS * FIELDS
    row = (lax.broadcasted_iota(jnp.int32, (EDGE, EDGE), 0) + 1).astype(F32)
    total = jnp.zeros((EDGE, EDGE), F32)
    for got in (near, far):
        for q in range(0, got.shape[0], 4):
            codes = got[q, body:PAYLOAD, :].astype(F32)
            for p in range(q + 1, q + 4):
                codes = codes + got[p, body:PAYLOAD, :].astype(F32)
            chosen = (row == jnp.broadcast_to(codes[0:1, :], (EDGE, EDGE))).astype(BF16)
            data = jnp.concatenate([got[p, 0:body, :] for p in range(q, q + 4)], axis=0)
            total = total + jnp.dot(chosen, data, preferred_element_type=F32)
    out[...] = total


def collect(near, far):
    return pl.pallas_call(
        collect_kernel,
        in_specs=[vmem()] * 2,
        out_specs=vmem(),
        out_shape=shape_of(EDGE, EDGE),
        compiler_params=params(),
        cost_estimate=cost(2**27, 2**18),
        name="collect",
    )(near, far)


def final_kernel(meta, part0, part1, mixed, absorb, rates, before, out, ocean, result, flux, done):
    blocks = mixed.shape[1] // EDGE
    for b in range(blocks):
        rows = slice(b * FIELDS, (b + 1) * FIELDS)
        flux[:, b * EDGE : (b + 1) * EDGE] = part0[rows, :] + part1[rows, :]
    whole = pltpu.make_async_copy(flux, ocean, done.at[0])
    whole.start()

    @pl.when(meta[0] == meta[2])
    def _():
        a0, a1, _ = three_parts(absorb[...])
        absorbing = jnp.concatenate([a0, a0, a1, a1], axis=1).astype(BF16)
        chunk = 2 * EDGE
        copies = []
        for k in range(blocks // 2):
            at = slice(k * chunk, (k + 1) * chunk)
            x0, x1, _ = three_parts(rates[:, at] * flux[:, at])
            drive = jnp.concatenate([x0, x1, x0, x1], axis=0).astype(BF16)
            result[:, at] = mixed[:, at] + jnp.dot(absorbing, drive, preferred_element_type=F32)
            copy = pltpu.make_async_copy(result.at[:, at], out.at[0, :, at], done.at[k + 1])
            copy.start()
            copies.append(copy)
        for copy in copies:
            copy.wait()

    whole.wait()


def finish(meta, part0, part1, mixed, absorb_map, rates, before):
    columns = mixed.shape[1]
    return pl.pallas_call(
        final_kernel,
        in_specs=[smem()] + [vmem()] * 5 + [anywhere()],
        out_specs=[anywhere()] * 2,
        out_shape=[shape_of(1, LEVELS, columns), shape_of(FIELDS, columns)],
        scratch_shapes=[
            pltpu.VMEM((LEVELS, columns), F32),
            pltpu.VMEM((FIELDS, columns), F32),
            pltpu.SemaphoreType.DMA((1 + columns // (2 * EDGE),)),
        ],
        input_output_aliases={6: 0},
        compiler_params=params(),
        cost_estimate=cost(2**28, 2**21),
        name="finish",
    )(meta, part0, part1, mixed, absorb_map, rates, before)


def swap(x, axis, bit):
    return lax.ppermute(x, axis, [(i, i ^ bit) for i in range(lax.axis_size(axis))])


def shards(
    state,
    diffusivity,
    neighbours,
    vertical_mix,
    transfer_rates,
    bulk_map,
    absorb_map,
    block_dest,
    block_rows,
    block_weights,
):
    tiles, groups = lax.axis_size("tile"), lax.axis_size("mp")
    my_tile, my_group = lax.axis_index("tile"), lax.axis_index("mp")
    strip = jnp.minimum(my_group, block_dest.shape[1] - 1)
    meta = jnp.stack([my_group, my_tile, jnp.int32(groups - 1), strip]).astype(jnp.int32)
    neighbours = jnp.transpose(neighbours, (1, 0, 2))
    diffusivity = jnp.transpose(diffusivity, (1, 0, 2))
    dest = jnp.transpose(block_dest, (1, 0, 2))
    live = jnp.transpose(block_rows, (1, 0, 2))
    sst = surface(state)
    dest, live, spots, places, state, neighbours, diffusivity, bulk_map = load(
        meta, tiles, dest, live, state, neighbours, diffusivity, bulk_map
    )
    beside = lax.optimization_barrier
    bit = groups // 2
    while bit:
        other = swap(sst, "mp", bit)
        if bit > 1:
            other, state = beside((other, state))
        sst = jnp.where((my_group & bit) != 0, sst, other)
        bit //= 2
    weights, turned, rates, vertical_mix, absorb_map = load_weights(
        meta, block_weights, transfer_rates, vertical_mix, absorb_map.T
    )
    mapped = map_state(state, bulk_map)
    to_a, to_b, absorb_map = make_halo(meta, dest, live, state, weights, neighbours, diffusivity, rates, absorb_map)
    got_a = swap(to_a, "tile", 1)
    bit = 1
    while bit < tiles:
        other = swap(sst, "tile", bit)
        if bit == 1:
            other, weights = beside((other, weights))
        if bit == 2:
            other, to_b, mapped = beside((other, to_b, mapped))
            got_b = lax.ppermute(to_b, "tile", [(i, (i + (1 if i % 2 else -1)) % tiles) for i in range(tiles)])
        if bit == 4:
            other, got_a = beside((other, got_a))
        sst = jnp.concatenate([sst, other], axis=0)
        bit *= 2
    keep, send, flux = make_flux(meta, tiles, dest, live, spots, sst, weights, turned, mapped, rates, places)
    keep, send = keep[None], send[None]
    bit = 1
    while True:
        got = swap(send, "tile", bit)
        if bit == 1:
            e, f, weight, band = force_state(meta, state, flux, absorb_map, neighbours, diffusivity)
            got, e, got_a, got_b = beside((got, e, got_a, got_b))
            power, e, f, weight_halo, band_halo = first_step(
                meta, e, f, sst, got_a, got_b, bulk_map, absorb_map, weight, band, vertical_mix
            )
        if bit == 2:
            got, e = beside((got, e))
            for _ in range(SUBSTEPS - 2):
                e, f = middle_step(e, f, weight, weight_halo, band, band_halo)
        if bit == 4:
            got, e = beside((got, e))
            mixed, new_state = last_step(e, f, weight, weight_halo, band, band_halo, power)
        bit *= 2
        if bit == tiles:
            break
        half = keep.shape[1] // 2
        send = jnp.concatenate([keep[:, half:], got[:, half:]], axis=0)
        keep = jnp.concatenate([keep[:, :half], got[:, :half]], axis=0)
    total = collect(keep[:, 0], got[:, 0])
    total = total + swap(total, "mp", 1)
    bit = 2
    while True:
        other = swap(total, "mp", bit)
        if bit == 2:
            other, mixed = beside((other, mixed))
        bit *= 2
        if bit >= groups:
            break
        total = total + other
    return tuple(finish(meta, total, other, mixed, absorb_map, rates, new_state))


def solution(mesh):
    placed = (
        P("mp", None, "tile"),
        P("mp", None, "tile"),
        P("mp", None, "tile"),
        P("mp", None, None),
        P("mp", None, "tile"),
        P(),
        P(),
        P("tile", None, None),
        P("tile", None, None),
        P("tile", None, None, None, None),
    )
    return jax.shard_map(
        shards,
        mesh=mesh,
        in_specs=placed,
        out_specs=(P("mp", None, "tile"), P(None, "tile")),
        check_vma=False,
    )
```

```python
import jax
import jax.numpy as jnp
from jax import lax
from jax.experimental import pallas as pl
from jax.experimental.pallas import tpu as pltpu
from jax.sharding import PartitionSpec as P

HALO_WIDTH = 32
SUBSTEPS = 4
FIELDS = 8
EDGE = 128
LEVELS = 128
NEIGH = 6
SLOTS = 4
PAYLOAD = 48
HALO_ROWS = LEVELS + 2 * EDGE + 48
F32 = jnp.float32
BF16 = jnp.bfloat16
HIGHEST = lax.Precision.HIGHEST


def lanes(shape):
    return lax.broadcasted_iota(jnp.int32, shape, len(shape) - 1)


def split(x):
    high = x.astype(BF16)
    return high, (x - high.astype(F32)).astype(BF16)


def vmem():
    return pl.BlockSpec(memory_space=pltpu.VMEM)


def smem():
    return pl.BlockSpec(memory_space=pltpu.SMEM)


def params():
    return pltpu.CompilerParams(vmem_limit_bytes=10 * 2**20)


def shape_of(*shape, dtype=F32):
    return jax.ShapeDtypeStruct(shape, dtype)


def cost(flops, size):
    return pl.CostEstimate(flops=1024, bytes_accessed=1024, transcendentals=0)


def in_hbm(x):
    return pltpu.with_memory_space_constraint(x, pltpu.HBM)


def anywhere():
    return pl.BlockSpec(memory_space=pltpu.HBM)


def surface_kernel(state, sst, top, done):
    copy = pltpu.make_async_copy(state.at[0, 0:1, :], top, done)
    copy.start()
    copy.wait()
    for b in range(sst.shape[0]):
        row = top[0:1, b * EDGE : (b + 1) * EDGE]
        sst[b : b + 1, :] = row.astype(BF16).astype(F32)


def surface(state):
    columns = state.shape[2]
    return pl.pallas_call(
        surface_kernel,
        in_specs=[anywhere()],
        out_specs=vmem(),
        out_shape=shape_of(columns // EDGE, EDGE),
        scratch_shapes=[pltpu.VMEM((1, columns), F32), pltpu.SemaphoreType.DMA],
        compiler_params=params(),
        cost_estimate=cost(2**20, 2**16),
        name="surface",
    )(in_hbm(state))


def load_kernel(meta, dest_h, live_h, state, bulk, dest, live, spots, places, state_v, bulk_v, codes, count, done):
    tiles = places.shape[0]
    blocks = state_v.shape[1] // EDGE
    pairs = [(dest_h, dest), (live_h, live), (state.at[0], state_v), (bulk, bulk_v)]
    copies = [pltpu.make_async_copy(a, b, done.at[k]) for k, (a, b) in enumerate(pairs)]
    for copy in copies:
        copy.start()
    lane = lanes((8, EDGE))
    for t in range(tiles):
        count[t] = 0
    codes[...] = jnp.zeros_like(codes)
    active = meta[0] != meta[2]
    copies[0].wait()
    for b in range(spots.shape[0]):
        where = dest[meta[3], 0, b]
        owner, local = (where // blocks) ^ meta[1], where % blocks
        slot = count[owner]
        count[owner] = slot + 1
        spots[b] = owner * SLOTS + slot
        start = (owner % 4) * (SLOTS * FIELDS) + slot * FIELDS
        mine = (lane >= start) & (lane < start + FIELDS) & active
        codes[owner] = codes[owner] + jnp.where(mine, local * FIELDS + 1 + lane - start, 0)
    for t in range(tiles):
        place = codes[t].astype(F32)
        places[t] = jnp.concatenate([place, place], axis=0).astype(BF16)
    for copy in copies[1:]:
        copy.wait()


def load(meta, tiles, dest, live, state, bulk_map):
    columns = state.shape[2]
    arrays = (dest, live, state, bulk_map)
    return pl.pallas_call(
        load_kernel,
        in_specs=[smem()] + [anywhere()] * 4,
        out_specs=[smem()] * 3 + [vmem()] * 3,
        out_shape=[
            shape_of(*dest.shape, dtype=jnp.int32),
            shape_of(*live.shape, dtype=jnp.int32),
            shape_of(dest.shape[2], dtype=jnp.int32),
            shape_of(tiles, 16, EDGE, dtype=BF16),
            shape_of(LEVELS, columns),
            shape_of(FIELDS, LEVELS),
        ],
        scratch_shapes=[
            pltpu.VMEM((tiles, 8, EDGE), jnp.int32),
            pltpu.SMEM((tiles,), jnp.int32),
            pltpu.SemaphoreType.DMA((4,)),
        ],
        compiler_params=params(),
        cost_estimate=cost(2**20, 2**21),
        name="load",
    )(meta, *(in_hbm(x) for x in arrays))


def weights_kernel(meta, weights, rates, vmix, absorb, nbr, dif, weights_v, turned, rates_v, vmix_v, absorb_v, nbr_v, dif_v, done):
    count = weights_v.shape[0]
    part = count // 8
    pairs = [(weights.at[0, meta[3], pl.ds(k * part, part)], weights_v.at[pl.ds(k * part, part)]) for k in range(8)]
    pairs += [(rates.at[0], rates_v), (vmix.at[0], vmix_v), (absorb, absorb_v), (nbr, nbr_v), (dif, dif_v)]
    copies = [pltpu.make_async_copy(a, b, done.at[k]) for k, (a, b) in enumerate(pairs)]
    for copy in copies:
        copy.start()
    for k in range(8):
        copies[k].wait()
        for b in range(k * part, (k + 1) * part):
            turned[b] = jnp.transpose(weights_v[b])
    for copy in copies[8:]:
        copy.wait()


def load_weights(meta, weights, rates, vertical_mix, absorb_map, neighbours, diffusivity):
    columns, blocks = rates.shape[2], weights.shape[2]
    arrays = (weights, rates, vertical_mix, absorb_map, neighbours, diffusivity)
    square = shape_of(blocks, EDGE, EDGE, dtype=BF16)
    return pl.pallas_call(
        weights_kernel,
        in_specs=[smem()] + [anywhere()] * 6,
        out_specs=[vmem()] * 7,
        out_shape=[
            square,
            square,
            shape_of(FIELDS, columns),
            shape_of(LEVELS, LEVELS),
            shape_of(FIELDS, LEVELS),
            shape_of(NEIGH, 1, columns, dtype=jnp.int32),
            shape_of(NEIGH, 1, columns),
        ],
        scratch_shapes=[pltpu.SemaphoreType.DMA((13,))],
        compiler_params=params(),
        cost_estimate=cost(2**20, 2**21),
        name="load_weights",
    )(meta, *(in_hbm(x) for x in arrays))


def halo_kernel(meta, dest, live, state, weights, nbr, dif, rates, absorb_t, out_a, out_b, absorb):
    blocks = state.shape[1] // EDGE
    strip = meta[3]

    def fill(out, e):
        b = 0 if e == 0 else blocks - 1
        at = slice(b * EDGE, (b + 1) * EDGE)
        out[0:LEVELS, :] = state[:, at].astype(BF16)
        base = LEVELS
        out[base : base + EDGE, :] = weights[2 * b]
        out[base + EDGE : base + 2 * EDGE, :] = weights[2 * b + 1]
        base += 2 * EDGE
        row = lax.broadcasted_iota(jnp.int32, (8, EDGE), 0)
        place = jnp.zeros((8, EDGE), jnp.int32)
        rate = jnp.zeros((8, EDGE), F32)
        for k in range(NEIGH):
            place = jnp.where(row == k, nbr[k, :, at] - (HALO_WIDTH + b * EDGE), place)
            rate = jnp.where(row == k, dif[k, :, at], rate)
        target = jnp.zeros((8, EDGE), jnp.int32)
        for h in range(2):
            block = dest[strip, 0, 2 * b + h]
            for k, value in enumerate((block // blocks, block % blocks, live[strip, 0, 2 * b + h])):
                target = jnp.where(row == 3 * h + k, value, target)
        high, low = split(rate)
        out[base : base + 16, :] = jnp.concatenate([place, target], axis=0).astype(F32).astype(BF16)
        out[base + 16 : base + 32, :] = jnp.concatenate([high.astype(F32), low.astype(F32)], axis=0).astype(BF16)
        high, low = split(rates[:, at])
        out[base + 32 : base + 48, :] = jnp.concatenate([high.astype(F32), low.astype(F32)], axis=0).astype(BF16)

    odd = meta[1] & 1

    @pl.when(odd == 0)
    def _():
        fill(out_a, 1)
        fill(out_b, 0)

    @pl.when(odd == 1)
    def _():
        fill(out_a, 0)
        fill(out_b, 1)

    tall = jnp.concatenate([absorb_t[...], jnp.zeros((LEVELS - FIELDS, LEVELS), F32)], axis=0)
    absorb[...] = jnp.transpose(tall)[:, 0:FIELDS]


def make_halo(meta, dest, live, state, weights, neighbours, diffusivity, rates, absorb_t):
    halo = shape_of(HALO_ROWS, EDGE, dtype=BF16)
    return pl.pallas_call(
        halo_kernel,
        in_specs=[smem()] * 3 + [vmem()] * 6,
        out_specs=[vmem()] * 3,
        out_shape=[halo, halo, shape_of(LEVELS, FIELDS)],
        compiler_params=params(),
        cost_estimate=cost(2**20, 2**18),
        name="make_halo",
    )(meta, dest, live, state, weights, neighbours, diffusivity, rates, absorb_t)


def map_kernel(state, bulk, mapped):
    b0, b1 = split(bulk[...])
    both = jnp.concatenate([b0.astype(F32), b1.astype(F32)], axis=0).astype(BF16)
    for c in range(state.shape[1] // EDGE):
        at = slice(c * EDGE, (c + 1) * EDGE)
        x0, x1 = split(state[:, at])
        high = jnp.dot(both, x0, preferred_element_type=F32)
        low = jnp.dot(both, x1, preferred_element_type=F32)
        mapped[:, at] = high[0:FIELDS] + (high[FIELDS:] + low[0:FIELDS])


def map_state(state, bulk_map):
    return pl.pallas_call(
        map_kernel,
        in_specs=[vmem()] * 2,
        out_specs=vmem(),
        out_shape=shape_of(FIELDS, state.shape[1]),
        compiler_params=params(),
        cost_estimate=cost(2**28, 2**20),
        name="map_state",
    )(state, bulk_map)


def build_band(index, weight, band, c):
    group = 8
    targets = []
    for k in range(NEIGH):
        j = index[c, k : k + 1, :]
        j = jnp.where((j >= 0) & (j < EDGE), j, EDGE + (j & (EDGE - 1)))
        targets.append((jnp.broadcast_to(j, (group, EDGE)), jnp.broadcast_to(weight[c, k : k + 1, :], (group, EDGE))))
    row = lax.broadcasted_iota(jnp.int32, (group, EDGE), 0)
    for start in range(0, 2 * EDGE, 16):
        if EDGE + HALO_WIDTH <= start < 2 * EDGE - HALO_WIDTH:
            high = jnp.zeros((16, EDGE), BF16)
            low = high
        else:
            parts = []
            for at in (start, start + group):
                total = jnp.zeros((group, EDGE), F32)
                for j, d in targets:
                    total = total + jnp.where(row == j - at, d, 0.0)
                parts.append(total)
            exact = jnp.concatenate(parts, axis=0)
            high = exact.astype(BF16)
            low = (exact - high.astype(F32)).astype(BF16)
        band[c, start : start + 16, 0:EDGE] = high
        band[c, start : start + 16, EDGE : 2 * EDGE] = low


def fill_terms(index, weight, c, j, d):
    index[c, 0:NEIGH, :] = j
    index[c, NEIGH:8, :] = jnp.zeros((2, EDGE), jnp.int32)
    weight[c, 0:NEIGH, :] = d
    weight[c, NEIGH:8, :] = jnp.broadcast_to(1.0 - jnp.sum(d, axis=0, keepdims=True), (2, EDGE))


def fill_terms(index, weight, c, j, d):
    index[c, 0:NEIGH, :] = j
    index[c, NEIGH:8, :] = jnp.zeros((2, EDGE), jnp.int32)
    weight[c, 0:NEIGH, :] = d
    weight[c, NEIGH:8, :] = jnp.broadcast_to(1.0 - jnp.sum(d, axis=0, keepdims=True), (2, EDGE))


def mixing_power(vmix):
    eye = (lax.broadcasted_iota(jnp.int32, (LEVELS, LEVELS), 0) == lanes((LEVELS, LEVELS))).astype(F32)
    total = eye + 0.25 * vmix
    a = total
    for _ in range(SUBSTEPS - 1):
        total = jnp.dot(total, a, precision=HIGHEST, preferred_element_type=F32)
    return total


def one_step(e, f, f_next, weight, weight_halo, band, band_halo, e_next, outer, final):
    low = lanes((2 * LEVELS, EDGE)) < EDGE // 2
    for c in range(1, outer - 1) if final else range(outer):
        edge = 0 if c == 0 else 1 if c == outer - 1 else None
        matrix = band[c - 1] if edge is None else band_halo[edge]
        keep = weight[c - 1, NEIGH : NEIGH + 1, :] if edge is None else weight_halo[edge, NEIGH : NEIGH + 1, :]
        near = jnp.concatenate([f(c), jnp.where(low, f(min(c + 1, outer - 1)), f(max(c - 1, 0)))], axis=1)
        product = jnp.dot(near, matrix, preferred_element_type=F32)
        x = keep * e(c) + (product[0:LEVELS, 0:EDGE] + (product[0:LEVELS, EDGE:] + product[LEVELS:, 0:EDGE]))
        e_next[c] = x
        if not final:
            f_next[c, 0:LEVELS, :], f_next[c, LEVELS : 2 * LEVELS, :] = split(x)


def three_parts(x):
    high = x.astype(BF16).astype(F32)
    middle = (x - high).astype(BF16).astype(F32)
    return high, middle, x - high - middle


def absorbing(meta, absorb):
    active = (meta[0] != meta[2]).astype(F32)
    return jnp.concatenate(three_parts(absorb[...] * active), axis=1).astype(BF16)


def absorbed(x, absorb, flux):
    return x - jnp.dot(absorb, jnp.concatenate([flux, flux, flux], axis=0).astype(BF16), preferred_element_type=F32)


def forced_kernel(meta, state, flux, absorb, nbr, dif, e, f, weight, band, index):
    matrix = absorbing(meta, absorb)
    for c in range(e.shape[0]):
        at = slice(c * EDGE, (c + 1) * EDGE)
        x = absorbed(state[:, at], matrix, flux[:, at])
        e[c] = x
        f[c, 0:LEVELS, :], f[c, LEVELS : 2 * LEVELS, :] = split(x)
        j = jnp.concatenate([nbr[k, :, at] for k in range(NEIGH)], axis=0) - (HALO_WIDTH + c * EDGE)
        d = jnp.concatenate([dif[k, :, at] for k in range(NEIGH)], axis=0)
        fill_terms(index, weight, c, j, d)

    @pl.loop(0, e.shape[0], unroll=2)
    def _(c):
        build_band(index, weight, band, c)


def force_state(meta, state, flux, absorb_map, neighbours, diffusivity):
    blocks = state.shape[1] // EDGE
    return pl.pallas_call(
        forced_kernel,
        in_specs=[smem()] + [vmem()] * 5,
        out_specs=[vmem()] * 4,
        out_shape=[
            shape_of(blocks, LEVELS, EDGE),
            shape_of(blocks, 2 * LEVELS, EDGE, dtype=BF16),
            shape_of(blocks, 8, EDGE),
            shape_of(blocks, 2 * EDGE, 2 * EDGE, dtype=BF16),
        ],
        scratch_shapes=[pltpu.VMEM((blocks, 8, EDGE), jnp.int32)],
        compiler_params=params(),
        cost_estimate=cost(2**28, 2**21),
        name="force_state",
    )(meta, state, flux, absorb_map, neighbours, diffusivity)


def first_kernel(meta, e, f, sst, got_a, got_b, bulk, absorb, weight, band, vmix, power, e_next, f_next, weight_halo, band_halo, e_halo, f_halo, halo, index_halo):
    outer = weight.shape[0] + 2
    odd = meta[1] & 1

    @pl.when(odd == 0)
    def _():
        halo[0] = got_b[...]
        halo[1] = got_a[...]

    @pl.when(odd == 1)
    def _():
        halo[0] = got_a[...]
        halo[1] = got_b[...]

    power[...] = mixing_power(vmix[...])
    matrix = absorbing(meta, absorb)
    surface_rows = sst[...].astype(BF16)
    lane = lanes((FIELDS, EDGE))
    for edge in range(2):
        base = LEVELS
        x = halo[edge, 0:LEVELS, :].astype(F32)
        blocks_held = [halo[edge, base + h * EDGE : base + (h + 1) * EDGE, :] for h in range(2)]
        base += 2 * EDGE
        small = halo[edge, base : base + 16, :].astype(F32)
        rate = halo[edge, base + 16 : base + 32, :].astype(F32)
        scale = halo[edge, base + 32 : base + 48, :].astype(F32)
        fill_terms(index_halo, weight_halo, edge, small[0:NEIGH].astype(jnp.int32), (rate[0:8] + rate[8:16])[0:NEIGH])
        build_band(index_halo, weight_halo, band_halo, edge)
        target = small[8:16].astype(jnp.int32)
        warmth = jnp.zeros((FIELDS, EDGE), F32)
        for h in range(2):
            owner, local, alive = target[3 * h : 3 * h + 1], target[3 * h + 1 : 3 * h + 2], target[3 * h + 2 : 3 * h + 3]
            spot = jnp.broadcast_to((owner ^ meta[1]) * (outer - 2) + local, lane.shape)
            row = jnp.zeros((FIELDS, EDGE), F32)
            for q in range(0, sst.shape[0], EDGE):
                chosen = (lane + q == spot).astype(BF16)
                row = row + jnp.dot(chosen, surface_rows[q : q + EDGE], preferred_element_type=F32)
            row = jnp.where(lane < jnp.broadcast_to(alive, lane.shape), row, 0.0).astype(BF16)
            warmth = warmth + lax.dot_general(
                row, blocks_held[h], (((1,), (1,)), ((), ())), preferred_element_type=F32
            )
        linear = jnp.dot(bulk[...], x, precision=HIGHEST, preferred_element_type=F32)
        here = (linear - (scale[0:8] + scale[8:16]) * warmth).astype(BF16).astype(F32)
        x = absorbed(x, matrix, here)
        e_halo[edge] = x
        f_halo[edge, 0:LEVELS, :], f_halo[edge, LEVELS : 2 * LEVELS, :] = split(x)

    def block(own, edges):
        return lambda c: edges[0] if c == 0 else edges[1] if c == outer - 1 else own[c - 1]

    one_step(block(e, e_halo), block(f, f_halo), f_next, weight, weight_halo, band, band_halo, e_next, outer, False)


def first_step(meta, e, f, sst, got_a, got_b, bulk_map, absorb_map, weight, band, vertical_mix):
    outer = weight.shape[0] + 2
    return pl.pallas_call(
        first_kernel,
        in_specs=[smem()] + [vmem()] * 10,
        out_specs=[vmem()] * 5,
        out_shape=[
            shape_of(LEVELS, LEVELS),
            shape_of(outer, LEVELS, EDGE),
            shape_of(outer, 2 * LEVELS, EDGE, dtype=BF16),
            shape_of(2, 8, EDGE),
            shape_of(2, 2 * EDGE, 2 * EDGE, dtype=BF16),
        ],
        scratch_shapes=[
            pltpu.VMEM((2, LEVELS, EDGE), F32),
            pltpu.VMEM((2, 2 * LEVELS, EDGE), BF16),
            pltpu.VMEM((2, HALO_ROWS, EDGE), BF16),
            pltpu.VMEM((2, 8, EDGE), jnp.int32),
        ],
        compiler_params=params(),
        cost_estimate=cost(2**30, 2**22),
        name="first_step",
    )(meta, e, f, sst, got_a, got_b, bulk_map, absorb_map, weight, band, vertical_mix)


def middle_kernel(e, f, weight, weight_halo, band, band_halo, e_next, f_next):
    one_step(e.__getitem__, f.__getitem__, f_next, weight, weight_halo, band, band_halo, e_next, e.shape[0], False)


def last_kernel(e, f, weight, weight_halo, band, band_halo, power, mixed, out, e_next, done):
    outer = e.shape[0]
    one_step(e.__getitem__, f.__getitem__, None, weight, weight_halo, band, band_halo, e_next, outer, True)
    copies = []
    for c in range(outer - 2):
        mixed[:, c * EDGE : (c + 1) * EDGE] = jnp.dot(
            power[...], e_next[c + 1], precision=HIGHEST, preferred_element_type=F32
        )
        if c % 2:
            at = slice((c - 1) * EDGE, (c + 1) * EDGE)
            copies.append(pltpu.make_async_copy(mixed.at[:, at], out.at[0, :, at], done.at[c // 2]))
            copies[-1].start()
    for copy in copies:
        copy.wait()


def middle_step(e, f, weight, weight_halo, band, band_halo):
    return pl.pallas_call(
        middle_kernel,
        in_specs=[vmem()] * 6,
        out_specs=[vmem()] * 2,
        out_shape=[shape_of(*e.shape), shape_of(*f.shape, dtype=BF16)],
        compiler_params=params(),
        cost_estimate=cost(2**30, 2**22),
        name="middle_step",
    )(e, f, weight, weight_halo, band, band_halo)


def last_step(e, f, weight, weight_halo, band, band_halo, power):
    columns = (e.shape[0] - 2) * EDGE
    return pl.pallas_call(
        last_kernel,
        in_specs=[vmem()] * 7,
        out_specs=[vmem(), anywhere()],
        out_shape=[shape_of(LEVELS, columns), shape_of(1, LEVELS, columns)],
        scratch_shapes=[pltpu.VMEM(e.shape, F32), pltpu.SemaphoreType.DMA((columns // (2 * EDGE),))],
        compiler_params=params(),
        cost_estimate=cost(2**30, 2**22),
        name="last_step",
    )(e, f, weight, weight_halo, band, band_halo, power)


def reverse_bits(value, count):
    return sum(((value >> k) & 1) << (count - 1 - k) for k in range(count))


def flux_kernel(meta, dest, live, spots, sst, weights, turned, mapped, rates, places, keep, send, flux, terms):
    blocks = mapped.shape[1] // EDGE
    tiles = terms.shape[0] // SLOTS
    bits = tiles.bit_length() - 1
    strip = meta[3]
    shape = (FIELDS, EDGE)
    lane = lanes(shape)
    terms[...] = jnp.zeros_like(terms)
    for g in range(blocks):
        at = slice(g * EDGE, (g + 1) * EDGE)
        warmth = jnp.zeros(shape, F32)
        held = []
        for b in (2 * g, 2 * g + 1):
            alive = lane < live[strip, 0, b]
            row = sst[pl.ds(dest[strip, 0, b] ^ (meta[1] * blocks), 1), :]
            row = jnp.where(alive, jnp.broadcast_to(row, shape), 0.0).astype(BF16)
            warmth = warmth + jnp.dot(row, turned[b], preferred_element_type=F32)
            held.append((b, alive))
        here = (mapped[:, at] - rates[:, at] * warmth).astype(BF16)
        flux[:, at] = here.astype(F32)
        for b, alive in held:
            part = jnp.dot(here, weights[b], preferred_element_type=F32)
            terms[spots[b]] = jnp.where(alive, part, 0.0)
    for t in range(tiles):
        i = reverse_bits(t, bits)
        out, i = (keep, i) if i < tiles // 2 else (send, i - tiles // 2)
        body = terms[t * SLOTS : (t + 1) * SLOTS].reshape(SLOTS * FIELDS, EDGE)
        out[i, 0 : SLOTS * FIELDS, :] = body.astype(BF16)
        out[i, SLOTS * FIELDS : PAYLOAD, :] = places[t]


def make_flux(meta, tiles, dest, live, spots, sst, weights, turned, mapped, rates, places):
    columns = mapped.shape[1]
    piece = shape_of(tiles // 2, PAYLOAD, EDGE, dtype=BF16)
    return pl.pallas_call(
        flux_kernel,
        in_specs=[smem()] * 4 + [vmem()] * 6,
        out_specs=[vmem()] * 3,
        out_shape=[piece, piece, shape_of(FIELDS, columns)],
        scratch_shapes=[pltpu.VMEM((tiles * SLOTS, FIELDS, EDGE), F32)],
        compiler_params=params(),
        cost_estimate=cost(2**30, 2**22),
        name="make_flux",
    )(meta, dest, live, spots, sst, weights, turned, mapped, rates, places)


def collect_kernel(near, far, out):
    body = SLOTS * FIELDS
    row = (lax.broadcasted_iota(jnp.int32, (EDGE, EDGE), 0) + 1).astype(F32)
    total = jnp.zeros((EDGE, EDGE), F32)
    for got in (near, far):
        for q in range(0, got.shape[0], 4):
            codes = got[q, body:PAYLOAD, :].astype(F32)
            for p in range(q + 1, q + 4):
                codes = codes + got[p, body:PAYLOAD, :].astype(F32)
            chosen = (row == jnp.broadcast_to(codes[0:1, :], (EDGE, EDGE))).astype(BF16)
            data = jnp.concatenate([got[p, 0:body, :] for p in range(q, q + 4)], axis=0)
            total = total + jnp.dot(chosen, data, preferred_element_type=F32)
    out[...] = total


def collect(near, far):
    return pl.pallas_call(
        collect_kernel,
        in_specs=[vmem()] * 2,
        out_specs=vmem(),
        out_shape=shape_of(EDGE, EDGE),
        compiler_params=params(),
        cost_estimate=cost(2**27, 2**18),
        name="collect",
    )(near, far)


def final_kernel(meta, part0, part1, mixed, absorb, rates, before, out, ocean, result, flux, done):
    blocks = mixed.shape[1] // EDGE
    for b in range(blocks):
        rows = slice(b * FIELDS, (b + 1) * FIELDS)
        flux[:, b * EDGE : (b + 1) * EDGE] = part0[rows, :] + part1[rows, :]
    whole = pltpu.make_async_copy(flux, ocean, done.at[0])
    whole.start()

    @pl.when(meta[0] == meta[2])
    def _():
        a0, a1, _ = three_parts(absorb[...])
        absorbing = jnp.concatenate([a0, a0, a1, a1], axis=1).astype(BF16)
        chunk = 2 * EDGE
        copies = []
        for k in range(blocks // 2):
            at = slice(k * chunk, (k + 1) * chunk)
            x0, x1, _ = three_parts(rates[:, at] * flux[:, at])
            drive = jnp.concatenate([x0, x1, x0, x1], axis=0).astype(BF16)
            result[:, at] = mixed[:, at] + jnp.dot(absorbing, drive, preferred_element_type=F32)
            copy = pltpu.make_async_copy(result.at[:, at], out.at[0, :, at], done.at[k + 1])
            copy.start()
            copies.append(copy)
        for copy in copies:
            copy.wait()

    whole.wait()


def finish(meta, part0, part1, mixed, absorb_map, rates, before):
    columns = mixed.shape[1]
    return pl.pallas_call(
        final_kernel,
        in_specs=[smem()] + [vmem()] * 5 + [anywhere()],
        out_specs=[anywhere()] * 2,
        out_shape=[shape_of(1, LEVELS, columns), shape_of(FIELDS, columns)],
        scratch_shapes=[
            pltpu.VMEM((LEVELS, columns), F32),
            pltpu.VMEM((FIELDS, columns), F32),
            pltpu.SemaphoreType.DMA((1 + columns // (2 * EDGE),)),
        ],
        input_output_aliases={6: 0},
        compiler_params=params(),
        cost_estimate=cost(2**28, 2**21),
        name="finish",
    )(meta, part0, part1, mixed, absorb_map, rates, before)


def swap(x, axis, bit):
    return lax.ppermute(x, axis, [(i, i ^ bit) for i in range(lax.axis_size(axis))])


def shards(
    state,
    diffusivity,
    neighbours,
    vertical_mix,
    transfer_rates,
    bulk_map,
    absorb_map,
    block_dest,
    block_rows,
    block_weights,
):
    tiles, groups = lax.axis_size("tile"), lax.axis_size("mp")
    my_tile, my_group = lax.axis_index("tile"), lax.axis_index("mp")
    strip = jnp.minimum(my_group, block_dest.shape[1] - 1)
    meta = jnp.stack([my_group, my_tile, jnp.int32(groups - 1), strip]).astype(jnp.int32)
    neighbours = jnp.transpose(neighbours, (1, 0, 2))
    diffusivity = jnp.transpose(diffusivity, (1, 0, 2))
    dest = jnp.transpose(block_dest, (1, 0, 2))
    live = jnp.transpose(block_rows, (1, 0, 2))
    sst = surface(state)
    dest, live, spots, places, state, bulk_map = load(meta, tiles, dest, live, state, bulk_map)
    beside = lax.optimization_barrier
    bit = groups // 2
    while bit:
        other = swap(sst, "mp", bit)
        if bit > 1:
            other, state = beside((other, state))
        sst = jnp.where((my_group & bit) != 0, sst, other)
        bit //= 2
    weights, turned, rates, vertical_mix, absorb_map, neighbours, diffusivity = load_weights(
        meta, block_weights, transfer_rates, vertical_mix, absorb_map.T, neighbours, diffusivity
    )
    to_a, to_b, absorb_map = make_halo(meta, dest, live, state, weights, neighbours, diffusivity, rates, absorb_map)
    got_a = swap(to_a, "tile", 1)
    bit = 1
    while bit < tiles:
        other = swap(sst, "tile", bit)
        if bit == 1:
            other, weights = beside((other, weights))
        if bit == 2:
            other, to_b, bulk_map = beside((other, to_b, bulk_map))
            mapped = map_state(state, bulk_map)
            got_b = lax.ppermute(to_b, "tile", [(i, (i + (1 if i % 2 else -1)) % tiles) for i in range(tiles)])
        if bit == 4:
            other, got_a, mapped = beside((other, got_a, mapped))
        sst = jnp.concatenate([sst, other], axis=0)
        bit *= 2
    keep, send, flux = make_flux(meta, tiles, dest, live, spots, sst, weights, turned, mapped, rates, places)
    keep, send = keep[None], send[None]
    bit = 1
    while True:
        got = swap(send, "tile", bit)
        if bit == 1:
            e, f, weight, band = force_state(meta, state, flux, absorb_map, neighbours, diffusivity)
            got, e, got_a, got_b = beside((got, e, got_a, got_b))
            power, e, f, weight_halo, band_halo = first_step(
                meta, e, f, sst, got_a, got_b, bulk_map, absorb_map, weight, band, vertical_mix
            )
        if bit == 2:
            got, e = beside((got, e))
            for _ in range(SUBSTEPS - 2):
                e, f = middle_step(e, f, weight, weight_halo, band, band_halo)
        if bit == 4:
            got, e = beside((got, e))
            mixed, new_state = last_step(e, f, weight, weight_halo, band, band_halo, power)
        bit *= 2
        if bit == tiles:
            break
        half = keep.shape[1] // 2
        send = jnp.concatenate([keep[:, half:], got[:, half:]], axis=0)
        keep = jnp.concatenate([keep[:, :half], got[:, :half]], axis=0)
    total = collect(keep[:, 0], got[:, 0])
    total = total + swap(total, "mp", 1)
    bit = 2
    while True:
        other = swap(total, "mp", bit)
        if bit == 2:
            other, mixed = beside((other, mixed))
        bit *= 2
        if bit >= groups:
            break
        total = total + other
    return tuple(finish(meta, total, other, mixed, absorb_map, rates, new_state))


def solution(mesh):
    placed = (
        P("mp", None, "tile"),
        P("mp", None, "tile"),
        P("mp", None, "tile"),
        P("mp", None, None),
        P("mp", None, "tile"),
        P(),
        P(),
        P("tile", None, None),
        P("tile", None, None),
        P("tile", None, None, None, None),
    )
    return jax.shard_map(
        shards,
        mesh=mesh,
        in_specs=placed,
        out_specs=(P("mp", None, "tile"), P(None, "tile")),
        check_vma=False,
    )
```
